512 devices in a mesh: mesh: 64 (over y, z), obs: 8 (over x, core).
Axes of the slice: x: 4, y: 4, z: 16, core: 2. Of those that a mesh axis runs over, the one named last changes fastest.
Arguments:
- probes: bfloat16 [64, 512, 2048], P(None, 'mesh', 'obs'), may hold values from -6 to 6
- velocity: float32 [512, 2048], P('mesh', 'obs'), may hold values from 0.5 to 2
- viscosity: float32 [512, 2048], P('mesh', 'obs'), may hold values from 0.1 to 3
- friction: float32 [512, 2048], P('mesh', 'obs'), may hold values from 0.5 to 4
- obs_block: int32 [64, 512], P('mesh', 'obs'), may hold values from 0 to 127
- obs_weight: float32 [64, 512, 128], P('mesh', 'obs'), may hold values from -0.5 to 0.5
- obs_prec: float32 [64, 512], P('mesh', 'obs'), may hold values from 0.05 to 0.5
- rank: int32 [1], replicated, may hold values from 1 to 64
Outputs:
- basis: float32 [64, 512, 2048], P(None, 'mesh', 'obs')
- factor: float32 [64, 64], replicated
The draws below stay inside these ranges and needn't reach their ends.
All inputs are finite; a program needn't handle non-finite values.
Results may differ from the reference program's by a relative error of at most 0.0027.
Values may be sent and summed in bfloat16 or wider, within the bound.
A program may use at most 64 MiB of HBM per device.

```python
import math
import jax
import jax.numpy as jnp
from jax import lax

P_SIZE = 64
BLOCK = 128
SLABS = 64
NX = 512
NZ = 2048
OBS_SLAB = 512
NBLK = 128
CELLS = 1048576


def plant(values, key, low, largest):
    dims = values.shape
    spot = [jax.random.randint(jax.random.fold_in(key, axis), (), 0, dims[axis]) for axis in range(len(dims))]
    values = values.at[tuple(spot)].set(low)
    longest = dims.index(max(dims))
    spot[longest] = (spot[longest] + 1) % dims[longest]
    return values.at[tuple(spot)].set(largest)


def level_of(own_key, extent, shards, low, top_value):
    level, own = 1.0, jax.random.fold_in(own_key, 6)
    for axis_at, parts in shards:
        heights = jnp.exp(jax.random.uniform(jax.random.fold_in(own, axis_at), (parts,), jnp.float32, low / len(shards), top_value / len(shards)))
        level = level * jnp.repeat(heights, extent[axis_at] // parts).reshape([-1 if axis == axis_at else 1 for axis in range(len(extent))])
    return level


def normal_values(rng, dims, spread, most, cuts=(), kind=jnp.bfloat16):
    loudness = level_of(rng, dims, cuts, -0.22, 0.18) if cuts else 1.0
    values = jax.random.normal(rng, dims, jnp.float32) * spread * loudness
    return jnp.minimum(jnp.maximum(values, -most), most).astype(kind)


def setup_inputs(seed: int = 0) -> dict:
    key_of = jax.random.split(jax.random.key(seed), 9)
    probes = normal_values(key_of[0], (P_SIZE, NX, NZ), 1.0, 6.0, ((1, 64), (2, 8)))
    velocity = jnp.clip(jnp.exp(math.log(2.0) - 1.3862944 * jax.random.uniform(key_of[1], (NX, NZ), jnp.float32) ** level_of(key_of[1], (NX, NZ), ((0, 64), (1, 8)), -0.2, 0.2)), 0.5, 2.0)
    viscosity = jnp.clip(jnp.exp(math.log(3.0) - 3.4011974 * jax.random.uniform(key_of[2], (NX, NZ), jnp.float32) ** level_of(key_of[2], (NX, NZ), ((0, 64), (1, 8)), -0.2, 0.2)), 0.1, 3.0)
    friction = jnp.clip(jnp.exp(math.log(4.0) - 2.0794415 * jax.random.uniform(key_of[3], (NX, NZ), jnp.float32) ** level_of(key_of[3], (NX, NZ), ((0, 64), (1, 8)), -0.2, 0.2)), 0.5, 4.0)
    obs_block = plant(jax.random.randint(key_of[4], (SLABS, OBS_SLAB), 0, NBLK), jax.random.fold_in(key_of[4], 1), 0, NBLK - 1).astype(jnp.int32)
    obs_weight = normal_values(key_of[5], (SLABS, OBS_SLAB, BLOCK), BLOCK ** -0.5, 0.5, ((0, 64), (1, 8)), jnp.float32)
    obs_prec = jnp.clip(jnp.exp(math.log(0.5) - 2.3025851 * jax.random.uniform(key_of[6], (SLABS, OBS_SLAB), jnp.float32) ** level_of(key_of[6], (SLABS, OBS_SLAB), ((0, 64), (1, 8)), -0.2, 0.2)), 0.05, 0.5)
    rank = jax.random.randint(key_of[7], (1,), 1, P_SIZE + 1).astype(jnp.int32)
    return dict(probes=probes, velocity=velocity, viscosity=viscosity, friction=friction, obs_block=obs_block, obs_weight=obs_weight, obs_prec=obs_prec, rank=rank)


PRIOR = 1.0

def apply_padded(padded, visc_pad, friction):
    height = padded.shape[1] - 2
    width = padded.shape[2] - 2
    centre = padded[:, 1:-1, 1:-1]
    visc_mid = visc_pad[1:-1, 1:-1]
    result = friction * centre
    for shift_row, shift_col in ((2, 1), (0, 1), (1, 2), (1, 0)):
        neighbor = padded[:, shift_row:shift_row + height, shift_col:shift_col + width]
        face_coef = 0.5 * (visc_mid + visc_pad[shift_row:shift_row + height, shift_col:shift_col + width])
        result = result + face_coef * (centre - neighbor)
    return result

def operate(field, viscosity, friction):
    padded = jnp.pad(field, ((0, 0), (1, 1), (1, 1)))
    visc_pad = jnp.pad(viscosity, 1)
    return apply_padded(padded, visc_pad, friction)

def reference(probes, velocity, viscosity, friction, obs_block, obs_weight, obs_prec, rank):
    omega = probes.astype(jnp.float32)
    tangent = operate(velocity * omega, viscosity, friction).astype(jnp.bfloat16)
    blocks = tangent.astype(jnp.float32).reshape(P_SIZE, SLABS, NBLK, BLOCK)
    picked = jnp.take_along_axis(blocks, obs_block[None, :, :, None], axis=2)
    misfit = obs_prec[None] * jnp.sum(picked * obs_weight[None], axis=-1)
    contrib = misfit[..., None] * obs_weight[None]
    slab_ids = jnp.broadcast_to(jnp.arange(SLABS, dtype=jnp.int32)[:, None], (SLABS, OBS_SLAB))
    source = jnp.zeros((P_SIZE, SLABS, NBLK, BLOCK), jnp.float32).at[:, slab_ids, obs_block].add(contrib)
    source = source.reshape(P_SIZE, NX, NZ)
    gradient = velocity * operate(source, viscosity, friction)
    sketch = (gradient + PRIOR * omega).reshape(P_SIZE, CELLS)
    gram = jnp.dot(sketch.astype(jnp.float32), sketch.T.astype(jnp.float32), precision=lax.Precision.HIGHEST, preferred_element_type=jnp.float32) / CELLS
    factor = jnp.linalg.cholesky(gram)
    solved = lax.linalg.triangular_solve(factor, sketch, left_side=True, lower=True)
    retained = (jnp.arange(P_SIZE, dtype=jnp.int32) < rank[0])[:, None]
    basis = jnp.where(retained, solved, 0.0).reshape(P_SIZE, NX, NZ)
    return (basis, factor)
```

```python
import functools

import jax
import jax.numpy as jnp
from jax import lax
from jax.experimental import pallas as pl
from jax.experimental.pallas import tpu as pltpu
from jax.sharding import PartitionSpec as P

BLOCK = 128
PRIOR = 1.0
Z_RING = 16
MESH = pl.DeviceIdType.MESH
F32 = jnp.float32
BF16 = jnp.bfloat16
NORTH, SOUTH, WEST, EAST = 0, 1, 2, 3
OPPOSITE = (SOUTH, NORTH, EAST, WEST)
NT = (((1,), (1,)), ((), ()))
NN = (((1,), (0,)), ((), ()))


def dot(a, b, dims):
    return lax.dot_general(a, b, dims, preferred_element_type=F32)


def split(x):
    high = x.astype(BF16)
    return high, (x - high.astype(F32)).astype(BF16)


def kernel(
    n_mesh,
    n_obs,
    nz,
    probes_ref,
    vel_ref,
    visc_ref,
    fric_ref,
    block_ref,
    weight_ref,
    prec_ref,
    rank_ref,
    basis_ref,
    factor_ref,
    probe_pr,
    field,
    forced,
    coef,
    tiles,
    tiles_halo,
    prow,
    prow_halo,
    fcol,
    fcol_halo,
    srow_halo,
    scol,
    scol_halo,
    wall,
    wcat,
    tcat,
    xcat,
    part,
    rs_buf,
    y_buf,
    z_buf,
    ag_buf,
    tile_sem,
    prow_sem,
    fcol_sem,
    srow_sem,
    scol_sem,
    w_sem,
    rs_sem,
    y_sem,
    z_sem,
    ag_sem,
):
    ny = n_mesh // nz
    probe_count, rows, cols = probes_ref.shape
    halves = cols // BLOCK
    slab_columns = halves * n_obs
    per_dev = weight_ref.shape[1]
    obs_total = per_dev * n_obs
    piece = part.shape[1]

    m = lax.axis_index("mesh")
    o = lax.axis_index("obs")
    y = m // nz
    z = lax.rem(m, nz)
    neighbours = (
        {"mesh": lax.rem(m + n_mesh - 1, n_mesh)},
        {"mesh": lax.rem(m + 1, n_mesh)},
        {"obs": lax.rem(o + n_obs - 1, n_obs)},
        {"obs": lax.rem(o + 1, n_obs)},
    )
    obs_peers = [{"obs": lax.rem(o + d, n_obs)} for d in range(1, n_obs)]
    y_peers = [{"mesh": lax.rem(y + d, ny) * nz + z} for d in range(1, ny)]
    z_peers = [{"mesh": y * nz + lax.rem(z + d, nz)} for d in range(1, nz)]

    barrier = pltpu.get_barrier_semaphore()
    partners = neighbours[:2] + tuple(obs_peers) + tuple(y_peers) + tuple(z_peers)
    for peer in partners:
        pl.semaphore_signal(barrier, inc=1, device_id=peer, device_id_type=MESH)

    tiles[0] = visc_ref[...]
    tiles[1] = vel_ref[...]
    wall[o, 0:per_dev, :] = weight_ref[0]
    wall[o, per_dev : per_dev + 8, :] = jnp.zeros((8, BLOCK), F32)
    wall[o, per_dev : per_dev + 1, 0:per_dev] = block_ref[...].astype(F32)
    wall[o, per_dev + 1 : per_dev + 2, 0:per_dev] = prec_ref[...]
    tail = wall[o, per_dev : per_dev + 8, :]
    wall[o, per_dev : per_dev + 8, :] = tail + pltpu.roll(tail, per_dev, 1)

    lane = lax.broadcasted_iota(jnp.int32, (1, BLOCK), 1)
    for h in range(halves):
        probe_pr[h] = (
            probes_ref[:, :, h * BLOCK : (h + 1) * BLOCK]
            .astype(F32)
            .reshape(probe_count * rows, BLOCK)
        )

    def probe_rows(r):
        return [
            probe_pr[h, pl.ds(r, probe_count, stride=rows), :] for h in range(halves)
        ]

    def edges(get):
        low = jnp.zeros((probe_count, BLOCK), F32)
        high = jnp.zeros((probe_count, BLOCK), F32)
        for r in range(rows):
            first, last = get(r)
            low = jnp.where(lane == r, pltpu.roll(first, r, 1) if r else first, low)
            high = jnp.where(lane == r, pltpu.roll(last, r + 1, 1), high)
        return low, high

    for r in range(rows):
        parts = probe_rows(r)
        for h in range(halves):
            forced[r, :, h * BLOCK : (h + 1) * BLOCK] = (
                parts[h] * vel_ref[r : r + 1, h * BLOCK : (h + 1) * BLOCK]
            )
            if r == 0:
                prow[0, :, h * BLOCK : (h + 1) * BLOCK] = parts[h].astype(BF16)
            if r == rows - 1:
                prow[1, :, h * BLOCK : (h + 1) * BLOCK] = parts[h].astype(BF16)
    low, high = edges(lambda r: (forced[r, :, 0:BLOCK], forced[r, :, cols - BLOCK : cols]))
    fcol[0] = low
    fcol[1] = high

    pl.semaphore_wait(barrier, len(partners))

    def send(src, dst, sems, at, slot, peer):
        copy = pltpu.make_async_remote_copy(
            src_ref=src,
            dst_ref=dst,
            send_sem=sems.at[0, at],
            recv_sem=sems.at[1, slot],
            device_id=peer,
            device_id_type=MESH,
        )
        copy.start()
        return copy

    sent = []
    tile_copies = []
    for side in range(4):
        there = OPPOSITE[side]
        tile_copies.append(
            send(tiles, tiles_halo.at[there], tile_sem, side, there, neighbours[side])
        )
    prow_copies = [
        send(prow.at[i], prow_halo.at[1 - i], prow_sem, i, 1 - i, neighbours[i])
        for i in range(2)
    ]
    fcol_copies = [
        send(fcol.at[i], fcol_halo.at[1 - i], fcol_sem, i, 1 - i, neighbours[2 + i])
        for i in range(2)
    ]
    w_copies = [
        send(wall.at[o], wall.at[o], w_sem, d, d, obs_peers[d]) for d in range(n_obs - 1)
    ]
    sent += tile_copies + prow_copies + fcol_copies + w_copies

    for copy in tile_copies:
        copy.wait_recv()
    row_id = lax.broadcasted_iota(jnp.int32, (rows, cols), 0)
    col_id = lax.broadcasted_iota(jnp.int32, (rows, cols), 1)
    inner = (m > 0, m < n_mesh - 1, o > 0, o < n_obs - 1)
    visc = visc_ref[...]

    def face(side, shift, axis, edge):
        ghost = jnp.where(inner[side], pltpu.roll(tiles_halo[side, 0], shift, axis), 0.0)
        return 0.5 * (visc + jnp.where(edge, ghost, pltpu.roll(visc, shift, axis)))

    face_n = face(NORTH, 1, 0, row_id == 0)
    face_s = face(SOUTH, rows - 1, 0, row_id == rows - 1)
    face_w = face(WEST, 1, 1, col_id == 0)
    face_e = face(EAST, cols - 1, 1, col_id == cols - 1)
    coef[0] = fric_ref[...] + face_n + face_s + face_w + face_e
    coef[1] = jnp.where(inner[NORTH] | (row_id > 0), face_n, 0.0)
    coef[2] = jnp.where(inner[SOUTH] | (row_id < rows - 1), face_s, 0.0)
    coef[3] = jnp.where(col_id > 0, face_w, 0.0)
    coef[4] = jnp.where(col_id < cols - 1, face_e, 0.0)
    coef[5] = jnp.where(inner[WEST] & (col_id == 0), face_w, 0.0)
    coef[6] = jnp.where(inner[EAST] & (col_id == cols - 1), face_e, 0.0)

    def interior(src, r):
        left, right = src[r, :, 0:BLOCK], src[r, :, BLOCK:cols]
        left_up, right_up = pltpu.roll(left, 1, 1), pltpu.roll(right, 1, 1)
        left_dn, right_dn = pltpu.roll(left, BLOCK - 1, 1), pltpu.roll(right, BLOCK - 1, 1)
        west = (left_up, jnp.where(lane == 0, left_up, right_up))
        east = (jnp.where(lane == BLOCK - 1, right_dn, left_dn), right_dn)
        out = []
        for h, centre in enumerate((left, right)):
            at = slice(h * BLOCK, (h + 1) * BLOCK)
            value = coef[0, r : r + 1, at] * centre
            if r < rows - 1:
                value = value - coef[2, r : r + 1, at] * src[r + 1, :, at]
            if r > 0:
                value = value - coef[1, r : r + 1, at] * src[r - 1, :, at]
            value = value - coef[4, r : r + 1, at] * east[h]
            value = value - coef[3, r : r + 1, at] * west[h]
            out.append(value)
        return out

    def with_columns(out, r, halo):
        from_west = pltpu.roll(halo[0], BLOCK - r, 1) if r else halo[0]
        from_east = pltpu.roll(halo[1], BLOCK - 1 - r, 1)
        return [
            out[0] - coef[5, r : r + 1, 0:BLOCK] * from_west,
            out[1] - coef[6, r : r + 1, BLOCK:cols] * from_east,
        ]

    for r in range(rows):
        left, right = interior(forced, r)
        field[r, :, 0:BLOCK] = left
        field[r, :, BLOCK:cols] = right
    for copy in fcol_copies + prow_copies:
        copy.wait_recv()
    order = [0, rows - 1] + list(range(1, rows - 1))
    for place, r in enumerate(order):
        out = with_columns([field[r, :, 0:BLOCK], field[r, :, BLOCK:cols]], r, fcol_halo)
        for h in range(halves):
            at = slice(h * BLOCK, (h + 1) * BLOCK)
            if r == 0:
                scale = coef[1, 0:1, at] * tiles_halo[NORTH, 1, rows - 1 : rows, at]
                out[h] = out[h] - scale * prow_halo[0, :, at].astype(F32)
            if r == rows - 1:
                scale = coef[2, r : r + 1, at] * tiles_halo[SOUTH, 1, 0:1, at]
                out[h] = out[h] - scale * prow_halo[1, :, at].astype(F32)
            tangent = out[h].astype(BF16)
            tcat[h, place * probe_count : (place + 1) * probe_count, 0:BLOCK] = tangent
            tcat[h, place * probe_count : (place + 1) * probe_count, BLOCK : 2 * BLOCK] = tangent

    for copy in w_copies:
        copy.wait_recv()
    for i in range(n_obs):
        w_high, w_low = split(wall[i, 0:per_dev, :])
        wcat[i * per_dev : (i + 1) * per_dev, 0:BLOCK] = w_high
        wcat[i * per_dev : (i + 1) * per_dev, BLOCK : 2 * BLOCK] = w_low
    per_row = BLOCK // per_dev

    def obs_row(at):
        pieces = []
        for c in range(obs_total // BLOCK):
            value = wall[c * per_row, per_dev + at : per_dev + at + 1, :]
            for k in range(1, per_row):
                other = wall[c * per_row + k, per_dev + at : per_dev + at + 1, :]
                value = jnp.where(lane < k * per_dev, value, other)
            pieces.append(value)
        return jnp.concatenate(pieces, axis=1)

    obs_at = obs_row(0)
    obs_scale = obs_row(1)
    weights = wcat[...]
    srow_copies = []
    for group in (order[:2], order[2:]):
        start = order.index(group[0]) * probe_count
        size = len(group) * probe_count
        for h in range(halves):
            picked = dot(tcat[h, start : start + size, :], weights, NT)
            masked = []
            for k, r in enumerate(group):
                own = (r * slab_columns + o * halves + h).astype(F32)
                scale = jnp.where(obs_at == own, obs_scale, 0.0)
                masked.append(picked[k * probe_count : (k + 1) * probe_count] * scale)
            mis_high, mis_low = split(jnp.concatenate(masked, axis=0))
            both = dot(mis_high, weights, NN)
            source = both[:, 0:BLOCK] + (both[:, BLOCK:] + dot(mis_low, weights[:, 0:BLOCK], NN))
            for k, r in enumerate(group):
                field[r, :, h * BLOCK : (h + 1) * BLOCK] = source[
                    k * probe_count : (k + 1) * probe_count
                ]
        if group[0] == 0:
            srow_copies = [
                send(
                    field.at[(rows - 1) * i],
                    srow_halo.at[1 - i],
                    srow_sem,
                    i,
                    1 - i,
                    neighbours[i],
                )
                for i in range(2)
            ]
    low, high = edges(lambda r: (field[r, :, 0:BLOCK], field[r, :, cols - BLOCK : cols]))
    scol[0] = low
    scol[1] = high
    scol_copies = [
        send(scol.at[i], scol_halo.at[1 - i], scol_sem, i, 1 - i, neighbours[2 + i])
        for i in range(2)
    ]
    sent += srow_copies + scol_copies

    for r in range(rows):
        left, right = interior(field, r)
        forced[r, :, 0:BLOCK] = left
        forced[r, :, BLOCK:cols] = right
    for copy in scol_copies + srow_copies:
        copy.wait_recv()
    for r in range(rows):
        out = with_columns([forced[r, :, 0:BLOCK], forced[r, :, BLOCK:cols]], r, scol_halo)
        parts = probe_rows(r)
        for h in range(halves):
            at = slice(h * BLOCK, (h + 1) * BLOCK)
            if r == 0:
                out[h] = out[h] - coef[1, 0:1, at] * srow_halo[0, :, at]
            if r == rows - 1:
                out[h] = out[h] - coef[2, r : r + 1, at] * srow_halo[1, :, at]
            s_high, s_low = split(vel_ref[r : r + 1, at] * out[h] + PRIOR * parts[h])
            here = slice(r * cols + h * BLOCK, r * cols + (h + 1) * BLOCK)
            xcat[0:probe_count, here] = s_high
            xcat[probe_count : 2 * probe_count, here] = s_low

    sketch = xcat[...]
    quad = dot(sketch, sketch, NT)
    pair = quad[0:probe_count] + quad[probe_count:]
    gram = pair + pltpu.roll(pair, probe_count, 1)
    half = probe_count // 2
    packed = jnp.where(lane < probe_count, gram[0:half], gram[half:])
    for i in range(n_obs):
        part[i] = packed[i * piece : (i + 1) * piece]

    def exchange(src_at, buf, sems, own, peers, slots):
        copies = [
            send(src_at(slots[d]), buf.at[own], sems, d, d, peers[d])
            for d in range(len(peers))
        ]
        return copies

    def total(buf, count):
        value = buf[0]
        for i in range(1, count):
            value = value + buf[i]
        return value

    obs_slots = [lax.rem(o + d, n_obs) for d in range(1, n_obs)]
    rs_buf[o] = part[o]
    copies = exchange(lambda s: part.at[s], rs_buf, rs_sem, o, obs_peers, obs_slots)
    for copy in copies:
        copy.wait_recv()
    sent += copies
    y_buf[y] = total(rs_buf, n_obs)
    copies = exchange(lambda s: y_buf.at[y], y_buf, y_sem, y, y_peers, [0] * (ny - 1))
    for copy in copies:
        copy.wait_recv()
    sent += copies
    z_buf[z] = total(y_buf, ny)
    copies = exchange(lambda s: z_buf.at[z], z_buf, z_sem, z, z_peers, [0] * (nz - 1))
    for copy in copies:
        copy.wait_recv()
    sent += copies
    cells = rows * cols * n_mesh * n_obs
    ag_buf[o] = total(z_buf, nz) / cells
    copies = exchange(lambda s: ag_buf.at[o], ag_buf, ag_sem, o, obs_peers, obs_slots)
    for copy in copies:
        copy.wait_recv()
    sent += copies
    for i in range(n_obs):
        factor_ref[i * piece : (i + 1) * piece, :] = ag_buf[i]

    whole = factor_ref[0:half, :]
    sub = lax.broadcasted_iota(jnp.int32, (8, BLOCK), 0)
    lanes8 = lax.broadcasted_iota(jnp.int32, (8, BLOCK), 1)
    groups = probe_count // 8
    work = []
    for g in range(groups):
        if g < groups // 2:
            own = whole[8 * g : 8 * g + 8]
        else:
            at = 8 * g - half
            own = pltpu.roll(whole[at : at + 8], probe_count, 1)
        unit = jnp.where(lanes8 == sub + (8 * g + probe_count), 1.0, 0.0)
        work.append(jnp.where(lanes8 < probe_count, own, unit))
    columns = [jnp.zeros((8, BLOCK), F32) for _ in range(groups)]
    inverse = [jnp.zeros((8, BLOCK), F32) for _ in range(groups)]
    for k in range(probe_count):
        g, s = divmod(k, 8)
        row = work[g][s : s + 1, :]
        pivot = row[:, k : k + 1]
        root = lax.rsqrt(pivot)
        scaled = row * (1.0 / pivot)
        unit_row = row * root
        inverse[g] = jnp.where(sub == s, unit_row, inverse[g])
        for i in range(g, groups):
            column = work[i][:, k : k + 1]
            update = work[i] - column * scaled
            keep = column * root
            if i == g:
                update = jnp.where(sub > s, update, work[i])
                keep = jnp.where(sub >= s, keep, 0.0)
            work[i] = update
            columns[i] = jnp.where(lanes8 == k, keep, columns[i])
    rank = rank_ref[0]
    for g in range(groups):
        factor_ref[8 * g : 8 * g + 8, :] = columns[g]
    lower = jnp.concatenate(
        [jnp.where(sub + 8 * g < rank, inverse[g], 0.0) for g in range(groups)], axis=0
    )
    lower = jnp.where(lane >= probe_count, lower, 0.0)
    lower = lower + pltpu.roll(lower, probe_count, 1)
    l_high, l_low = split(lower)
    solved = dot(jnp.concatenate([l_high, l_low], axis=0), sketch, NN)
    result = solved[0:probe_count] + solved[probe_count:]
    for r in range(rows):
        for h in range(halves):
            probe_pr[h, pl.ds(r, probe_count, stride=rows), :] = result[
                :, r * cols + h * BLOCK : r * cols + (h + 1) * BLOCK
            ]
    for h in range(halves):
        basis_ref[:, :, h * BLOCK : (h + 1) * BLOCK] = probe_pr[h].reshape(
            probe_count, rows, BLOCK
        )

    for copy in sent:
        copy.wait_send()


def per_device(n_mesh, n_obs, nz, probes, velocity, viscosity, friction, obs_block, obs_weight, obs_prec, rank):
    probe_count, rows, cols = probes.shape
    per_dev = obs_weight.shape[1]
    obs_total = per_dev * n_obs
    ny = n_mesh // nz
    piece = probe_count // 2 // n_obs
    dma = pltpu.SemaphoreType.DMA
    vmem = pl.BlockSpec(memory_space=pltpu.VMEM)
    basis, factor = pl.pallas_call(
        functools.partial(kernel, n_mesh, n_obs, nz),
        out_shape=(
            jax.ShapeDtypeStruct((probe_count, rows, cols), F32),
            jax.ShapeDtypeStruct((probe_count, BLOCK), F32),
        ),
        in_specs=[vmem] * 7 + [pl.BlockSpec(memory_space=pltpu.SMEM)],
        out_specs=(vmem, vmem),
        scratch_shapes=[
            pltpu.VMEM((cols // BLOCK, probe_count * rows, BLOCK), F32),
            pltpu.VMEM((rows, probe_count, cols), F32),
            pltpu.VMEM((rows, probe_count, cols), F32),
            pltpu.VMEM((7, rows, cols), F32),
            pltpu.VMEM((2, rows, cols), F32),
            pltpu.VMEM((4, 2, rows, cols), F32),
            pltpu.VMEM((2, probe_count, cols), BF16),
            pltpu.VMEM((2, probe_count, cols), BF16),
            pltpu.VMEM((2, probe_count, BLOCK), F32),
            pltpu.VMEM((2, probe_count, BLOCK), F32),
            pltpu.VMEM((2, probe_count, cols), F32),
            pltpu.VMEM((2, probe_count, BLOCK), F32),
            pltpu.VMEM((2, probe_count, BLOCK), F32),
            pltpu.VMEM((n_obs, per_dev + 8, BLOCK), F32),
            pltpu.VMEM((obs_total, 2 * BLOCK), BF16),
            pltpu.VMEM((cols // BLOCK, rows * probe_count, 2 * BLOCK), BF16),
            pltpu.VMEM((2 * probe_count, rows * cols), BF16),
            pltpu.VMEM((n_obs, piece, BLOCK), F32),
            pltpu.VMEM((n_obs, piece, BLOCK), F32),
            pltpu.VMEM((ny, piece, BLOCK), F32),
            pltpu.VMEM((nz, piece, BLOCK), F32),
            pltpu.VMEM((n_obs, piece, BLOCK), F32),
            dma((2, 4)),
            dma((2, 2)),
            dma((2, 2)),
            dma((2, 2)),
            dma((2, 2)),
            dma((2, n_obs - 1)),
            dma((2, n_obs - 1)),
            dma((2, ny - 1)),
            dma((2, nz - 1)),
            dma((2, n_obs - 1)),
        ],
        compiler_params=pltpu.CompilerParams(collective_id=0, has_side_effects=True),
    )(probes, velocity, viscosity, friction, obs_block, obs_weight, obs_prec, rank)
    return basis, factor[:, :probe_count]


def solution(mesh):
    in_specs = (
        P(None, "mesh", "obs"),
        P("mesh", "obs"),
        P("mesh", "obs"),
        P("mesh", "obs"),
        P("mesh", "obs"),
        P("mesh", "obs", None),
        P("mesh", "obs"),
        P(),
    )
    n_mesh, n_obs = mesh.shape["mesh"], mesh.shape["obs"]
    nz = Z_RING if n_mesh % Z_RING == 0 else n_mesh // 2
    return jax.shard_map(
        functools.partial(per_device, n_mesh, n_obs, nz),
        mesh=mesh,
        in_specs=in_specs,
        out_specs=(P(None, "mesh", "obs"), P()),
        check_vma=False,
    )
```

```python
import functools

import jax
import jax.numpy as jnp
from jax import lax
from jax.experimental import pallas as pl
from jax.experimental.pallas import tpu as pltpu
from jax.sharding import PartitionSpec as P

BLOCK = 128
PRIOR = 1.0
Z_RING = 16
NEAR = 2
MESH = pl.DeviceIdType.MESH
F32 = jnp.float32
BF16 = jnp.bfloat16
NORTH, SOUTH, WEST, EAST = 0, 1, 2, 3
OPPOSITE = (SOUTH, NORTH, EAST, WEST)
NT = (((1,), (1,)), ((), ()))
NN = (((1,), (0,)), ((), ()))


def dot(a, b, dims):
    return lax.dot_general(a, b, dims, preferred_element_type=F32)


def split(x):
    high = x.astype(BF16)
    return high, (x - high.astype(F32)).astype(BF16)


def shifted(x, amount):
    amount %= BLOCK
    return pltpu.roll(x, amount, 1) if amount else x


def sketch_kernel(
    n_mesh,
    n_obs,
    nz,
    probes_hbm,
    vel_hbm,
    visc_hbm,
    fric_hbm,
    block_hbm,
    weight_hbm,
    prec_hbm,
    xcat,
    gram_ref,
    probes_ref,
    fric_ref,
    block_ref,
    weight_ref,
    prec_ref,
    probe_pr,
    field,
    forced,
    coef,
    tiles,
    tiles_halo,
    prow,
    prow_halo,
    fcol,
    fcol_halo,
    srow_halo,
    scol,
    scol_halo,
    wall,
    wcat,
    tcat,
    part,
    rs_buf,
    y_buf,
    z_buf,
    ag_buf,
    load_sem,
    send_sem,
    recv_sem,
    token,
):
    ny = n_mesh // nz
    probe_count, rows, cols = probes_ref.shape
    halves = cols // BLOCK
    slab_columns = halves * n_obs
    per_dev = weight_ref.shape[1]
    obs_total = per_dev * n_obs
    piece = part.shape[1]
    groups = probe_count // 8
    TILES, PROW, FCOL, SROW, SCOL, WALL, RS, YS, ZS, AG, FAR = range(11)

    m = lax.axis_index("mesh")
    o = lax.axis_index("obs")
    y = m // nz
    z = lax.rem(m, nz)
    neighbours = (
        {"mesh": lax.rem(m + n_mesh - 1, n_mesh)},
        {"mesh": lax.rem(m + 1, n_mesh)},
        {"obs": lax.rem(o + n_obs - 1, n_obs)},
        {"obs": lax.rem(o + 1, n_obs)},
    )
    obs_peers = [{"obs": lax.rem(o + d, n_obs)} for d in range(1, n_obs)]
    obs_slots = [lax.rem(o + d, n_obs) for d in range(1, n_obs)]
    y_peers = [{"mesh": lax.rem(y + d, ny) * nz + z} for d in range(1, ny)]

    def z_peer(d):
        return {"mesh": y * nz + lax.rem(z + d, nz)}

    z_peers = [z_peer(d) for d in range(1, nz)]
    near_z = [z_peer(d) for d in range(1, nz) if min(d, nz - d) <= NEAR]

    names = (probes_hbm, weight_hbm, block_hbm, prec_hbm, visc_hbm, vel_hbm, fric_hbm)
    places = (probes_ref, weight_ref, block_ref, prec_ref, tiles.at[0], tiles.at[1], fric_ref)
    loads = [
        pltpu.make_async_copy(src, dst, load_sem.at[i])
        for i, (src, dst) in enumerate(zip(names, places))
    ]
    for load in loads:
        load.start()

    barrier = pltpu.get_barrier_semaphore()
    partners = list(neighbours[:2]) + obs_peers + y_peers + near_z
    for peer in partners:
        pl.semaphore_signal(barrier, inc=1, device_id=peer, device_id_type=MESH)

    lane = lax.broadcasted_iota(jnp.int32, (1, BLOCK), 1)
    wall[o, per_dev : per_dev + 8, :] = jnp.zeros((8, BLOCK), F32)
    for load in loads[1:4]:
        load.wait()
    wall[o, 0:per_dev, :] = weight_ref[0]
    wall[o, per_dev : per_dev + 1, 0:per_dev] = block_ref[...].astype(F32)
    wall[o, per_dev + 1 : per_dev + 2, 0:per_dev] = prec_ref[...]
    tail = wall[o, per_dev : per_dev + 8, :]
    wall[o, per_dev : per_dev + 8, :] = tail + shifted(tail, per_dev)

    loads[0].wait()
    for h in range(halves):
        probe_pr[h] = (
            probes_ref[:, :, h * BLOCK : (h + 1) * BLOCK]
            .astype(F32)
            .reshape(probe_count * rows, BLOCK)
        )
    for load in loads[4:]:
        load.wait()

    def probe_rows(r):
        return [
            probe_pr[h, pl.ds(r, probe_count, stride=rows), :] for h in range(halves)
        ]

    def packed_edges(src, first):
        at = slice(0, BLOCK) if first else slice(cols - BLOCK, cols)
        out = jnp.zeros((8, BLOCK), F32)
        for g in range(groups):
            own = jnp.zeros((8, BLOCK), F32)
            for r in range(rows):
                value = src[r, 8 * g : 8 * g + 8, at]
                own = jnp.where(lane == r, shifted(value, r + (0 if first else 1)), own)
            out = out + shifted(own, rows * g)
        return out

    for r in range(rows):
        parts = probe_rows(r)
        for h in range(halves):
            at = slice(h * BLOCK, (h + 1) * BLOCK)
            forced[r, :, at] = parts[h] * tiles[1, r : r + 1, at]
            if r == 0:
                prow[0, :, at] = parts[h].astype(BF16)
            if r == rows - 1:
                prow[1, :, at] = parts[h].astype(BF16)
    fcol[0] = packed_edges(forced, True)
    fcol[1] = packed_edges(forced, False)

    pl.semaphore_wait(barrier, len(partners))

    def send(src, dst, stage, peer):
        pltpu.make_async_remote_copy(
            src_ref=src,
            dst_ref=dst,
            send_sem=send_sem.at[stage],
            recv_sem=recv_sem.at[stage],
            device_id=peer,
            device_id_type=MESH,
        ).start()

    def whole(buf, stage):
        return pltpu.make_async_remote_copy(
            src_ref=buf,
            dst_ref=buf,
            send_sem=send_sem.at[stage],
            recv_sem=recv_sem.at[stage],
            device_id=neighbours[NORTH],
            device_id_type=MESH,
        )

    unsent = []

    def arrived(buf, stage):
        copy = whole(buf, stage)
        unsent.append(copy)
        copy.wait_recv()

    for side in range(4):
        send(tiles, tiles_halo.at[OPPOSITE[side]], TILES, neighbours[side])
    for i in range(2):
        send(fcol.at[i], fcol_halo.at[1 - i], FCOL, neighbours[2 + i])
    for i in range(2):
        send(prow.at[i], prow_halo.at[1 - i], PROW, neighbours[i])
    sibling = {"obs": o + 1 - 2 * lax.rem(o, 2)}
    same_core = sorted(range(2, n_obs, 2), key=lambda d: min(d, n_obs - d))
    for d in same_core:
        send(wall.at[o], wall.at[o], FAR + d // 2 - 1, {"obs": lax.rem(o + d, n_obs)})
    send(wall.at[o], wall.at[o], WALL, sibling)

    tokens = []
    reach = NEAR
    while 2 * reach <= nz // 2:
        tokens.append(reach)
        reach *= 2

    def tell(level):
        for side, d in enumerate((tokens[level], nz - tokens[level])):
            pl.semaphore_signal(
                token.at[level, side], inc=1, device_id=z_peer(d), device_id_type=MESH
            )

    def hear(level):
        for side in range(2):
            pl.semaphore_wait(token.at[level, side], 1)

    if tokens:
        tell(0)

    arrived(tiles_halo, TILES)
    row_id = lax.broadcasted_iota(jnp.int32, (rows, cols), 0)
    col_id = lax.broadcasted_iota(jnp.int32, (rows, cols), 1)
    inner = (m > 0, m < n_mesh - 1, o > 0, o < n_obs - 1)
    visc = tiles[0]

    def face(side, shift, axis, edge):
        ghost = jnp.where(inner[side], pltpu.roll(tiles_halo[side, 0], shift, axis), 0.0)
        return 0.5 * (visc + jnp.where(edge, ghost, pltpu.roll(visc, shift, axis)))

    face_n = face(NORTH, 1, 0, row_id == 0)
    face_s = face(SOUTH, rows - 1, 0, row_id == rows - 1)
    face_w = face(WEST, 1, 1, col_id == 0)
    face_e = face(EAST, cols - 1, 1, col_id == cols - 1)
    coef[0] = fric_ref[...] + face_n + face_s + face_w + face_e
    coef[1] = jnp.where(inner[NORTH] | (row_id > 0), face_n, 0.0)
    coef[2] = jnp.where(inner[SOUTH] | (row_id < rows - 1), face_s, 0.0)
    coef[3] = jnp.where(col_id > 0, face_w, 0.0)
    coef[4] = jnp.where(col_id < cols - 1, face_e, 0.0)
    coef[5] = jnp.where(inner[WEST] & (col_id == 0), face_w, 0.0)
    coef[6] = jnp.where(inner[EAST] & (col_id == cols - 1), face_e, 0.0)

    def interior(src, r):
        left, right = src[r, :, 0:BLOCK], src[r, :, BLOCK:cols]
        left_up, right_up = shifted(left, 1), shifted(right, 1)
        left_dn, right_dn = shifted(left, -1), shifted(right, -1)
        west = (left_up, jnp.where(lane == 0, left_up, right_up))
        east = (jnp.where(lane == BLOCK - 1, right_dn, left_dn), right_dn)
        out = []
        for h, centre in enumerate((left, right)):
            at = slice(h * BLOCK, (h + 1) * BLOCK)
            value = coef[0, r : r + 1, at] * centre
            if r < rows - 1:
                value = value - coef[2, r : r + 1, at] * src[r + 1, :, at]
            if r > 0:
                value = value - coef[1, r : r + 1, at] * src[r - 1, :, at]
            value = value - coef[4, r : r + 1, at] * east[h]
            value = value - coef[3, r : r + 1, at] * west[h]
            out.append(value)
        return out

    def spread(halo):
        return [
            jnp.concatenate([shifted(halo[i], -rows * g) for g in range(groups)], axis=0)
            for i in range(2)
        ]

    def with_columns(out, r, halo):
        from_west = shifted(halo[0], -r)
        from_east = shifted(halo[1], -1 - r)
        return [
            out[0] - coef[5, r : r + 1, 0:BLOCK] * from_west,
            out[1] - coef[6, r : r + 1, BLOCK:cols] * from_east,
        ]

    for r in range(rows):
        left, right = interior(forced, r)
        field[r, :, 0:BLOCK] = left
        field[r, :, BLOCK:cols] = right
    arrived(fcol_halo, FCOL)
    arrived(prow_halo, PROW)
    columns = spread(fcol_halo)
    order = [0, rows - 1] + list(range(1, rows - 1))
    for place, r in enumerate(order):
        out = with_columns([field[r, :, 0:BLOCK], field[r, :, BLOCK:cols]], r, columns)
        for h in range(halves):
            at = slice(h * BLOCK, (h + 1) * BLOCK)
            if r == 0:
                scale = coef[1, 0:1, at] * tiles_halo[NORTH, 1, rows - 1 : rows, at]
                out[h] = out[h] - scale * prow_halo[0, :, at].astype(F32)
            if r == rows - 1:
                scale = coef[2, r : r + 1, at] * tiles_halo[SOUTH, 1, 0:1, at]
                out[h] = out[h] - scale * prow_halo[1, :, at].astype(F32)
            here = slice(place * probe_count, (place + 1) * probe_count)
            tcat[h, here, 0:BLOCK] = out[h].astype(BF16)
            tcat[h, here, BLOCK : 2 * BLOCK] = out[h].astype(BF16)
    if tokens:
        hear(0)
        for level in range(1, len(tokens)):
            tell(level)

    for d in same_core:
        source = lax.rem(o + n_obs - d, n_obs)
        arrived(wall.at[source], FAR + d // 2 - 1)
        send(wall.at[source], wall.at[source], WALL, sibling)
    arrived(wall.at[pl.ds(0, n_obs // 2)], WALL)
    for i in range(n_obs):
        w_high, w_low = split(wall[i, 0:per_dev, :])
        wcat[i * per_dev : (i + 1) * per_dev, 0:BLOCK] = w_high
        wcat[i * per_dev : (i + 1) * per_dev, BLOCK : 2 * BLOCK] = w_low
    per_row = BLOCK // per_dev
    tails = [wall[i, per_dev : per_dev + 8, :] for i in range(n_obs)]
    chunks = []
    for c in range(obs_total // BLOCK):
        value = tails[c * per_row]
        for k in range(1, per_row):
            value = jnp.where(lane < k * per_dev, value, tails[c * per_row + k])
        chunks.append(value)
    tail = jnp.concatenate(chunks, axis=1)
    obs_at, obs_scale = tail[0:1], tail[1:2]
    weights = wcat[...]
    for group in (order[:2], order[2:]):
        start = order.index(group[0]) * probe_count
        size = len(group) * probe_count
        for h in range(halves):
            picked = dot(tcat[h, start : start + size, :], weights, NT)
            masked = []
            for k, r in enumerate(group):
                own = (r * slab_columns + o * halves + h).astype(F32)
                scale = jnp.where(obs_at == own, obs_scale, 0.0)
                masked.append(picked[k * probe_count : (k + 1) * probe_count] * scale)
            mis_high, mis_low = split(jnp.concatenate(masked, axis=0))
            both = dot(mis_high, weights, NN)
            low = dot(mis_low, weights[:, 0:BLOCK], NN)
            source = both[:, 0:BLOCK] + (both[:, BLOCK:] + low)
            for k, r in enumerate(group):
                field[r, :, h * BLOCK : (h + 1) * BLOCK] = source[
                    k * probe_count : (k + 1) * probe_count
                ]
        if group[0] == 0:
            for i in range(2):
                send(field.at[(rows - 1) * i], srow_halo.at[1 - i], SROW, neighbours[i])
    scol[0] = packed_edges(field, True)
    scol[1] = packed_edges(field, False)
    for i in range(2):
        send(scol.at[i], scol_halo.at[1 - i], SCOL, neighbours[2 + i])

    for r in range(rows):
        left, right = interior(field, r)
        forced[r, :, 0:BLOCK] = left
        forced[r, :, BLOCK:cols] = right
    arrived(scol_halo, SCOL)
    arrived(srow_halo, SROW)
    columns = spread(scol_halo)
    for r in range(rows):
        out = with_columns([forced[r, :, 0:BLOCK], forced[r, :, BLOCK:cols]], r, columns)
        parts = probe_rows(r)
        for h in range(halves):
            at = slice(h * BLOCK, (h + 1) * BLOCK)
            if r == 0:
                out[h] = out[h] - coef[1, 0:1, at] * srow_halo[0, :, at]
            if r == rows - 1:
                out[h] = out[h] - coef[2, r : r + 1, at] * srow_halo[1, :, at]
            s_high, s_low = split(tiles[1, r : r + 1, at] * out[h] + PRIOR * parts[h])
            here = slice(r * cols + h * BLOCK, r * cols + (h + 1) * BLOCK)
            xcat[0:probe_count, here] = s_high
            xcat[probe_count : 2 * probe_count, here] = s_low

    sketch = xcat[...]
    quad = dot(sketch, sketch, NT)
    pair = quad[0:probe_count] + quad[probe_count:]
    gram = pair + shifted(pair, probe_count)
    half = probe_count // 2
    packed = jnp.where(lane < probe_count, gram[0:half], gram[half:])
    for i in range(n_obs):
        part[i] = packed[i * piece : (i + 1) * piece]

    def total(buf, count):
        values = [buf[i] for i in range(count)]
        while len(values) > 1:
            values = [
                sum(values[i : i + 2][1:], values[i]) for i in range(0, len(values), 2)
            ]
        return values[0]

    for peer, slot in zip(obs_peers, obs_slots):
        send(part.at[slot], rs_buf.at[o], RS, peer)
    rs_buf[o] = part[o]
    arrived(rs_buf.at[pl.ds(0, n_obs - 1)], RS)
    y_buf[y] = total(rs_buf, n_obs)
    for peer in y_peers:
        send(y_buf.at[y], y_buf.at[y], YS, peer)
    if tokens:
        for level in range(1, len(tokens)):
            hear(level)
    arrived(y_buf.at[pl.ds(0, ny - 1)], YS)
    z_buf[z] = total(y_buf, ny)
    for d in range(nz // 2, 0, -1):
        send(z_buf.at[z], z_buf.at[z], ZS, z_peer(d))
        if 2 * d < nz:
            send(z_buf.at[z], z_buf.at[z], ZS, z_peer(nz - d))
    arrived(z_buf.at[pl.ds(0, nz - 1)], ZS)
    cells = rows * cols * n_mesh * n_obs
    ag_buf[o] = total(z_buf, nz) / cells
    for peer in obs_peers:
        send(ag_buf.at[o], ag_buf.at[o], AG, peer)
    arrived(ag_buf.at[pl.ds(0, n_obs - 1)], AG)
    for i in range(n_obs):
        gram_ref[i * piece : (i + 1) * piece, :] = ag_buf[i]
    for copy in unsent:
        copy.wait_send()


def eliminate(work, probe_count):
    sub = lax.broadcasted_iota(jnp.int32, (8, BLOCK), 0)
    lanes = lax.broadcasted_iota(jnp.int32, (8, BLOCK), 1)
    groups = len(work)
    factor = [jnp.zeros((8, BLOCK), F32)] * groups
    inverse = [jnp.zeros((8, BLOCK), F32)] * groups

    def wide(x):
        return jnp.broadcast_to(x, (8, BLOCK))

    for k in range(0, probe_count, 4):
        g, s = divmod(k, 8)
        col = [[wide(work[i][:, k + j : k + j + 1]) for i in range(g, groups)] for j in range(4)]
        row = [wide(work[g][s + j : s + j + 1, :]) for j in range(4)]

        def pivot(i, j):
            return wide(col[j][0][s + i : s + i + 1, :])

        a, b, c = pivot(0, 0), pivot(1, 0), pivot(1, 1)
        p, q, t, u = pivot(2, 0), pivot(2, 1), pivot(3, 0), pivot(3, 1)
        det = a * c - b * b
        inv_a, inv_det = 1.0 / a, 1.0 / det
        inv_1 = a * inv_det
        m10 = b * inv_a
        p_0, p_1 = c * p - b * q, a * q - b * p
        t_0, t_1 = c * t - b * u, a * u - b * t
        e = pivot(2, 2) - (p * p_0 + q * p_1) * inv_det
        f = pivot(3, 2) - (t * p_0 + u * p_1) * inv_det
        h = pivot(3, 3) - (t * t_0 + u * t_1) * inv_det
        det_2 = e * h - f * f
        inv_e, inv_det_2 = 1.0 / e, 1.0 / det_2
        inv_3 = e * inv_det_2
        m20, m30 = p * inv_a, t * inv_a
        m21, m31 = (q - m10 * p) * inv_1, (u - m10 * t) * inv_1
        m32 = f * inv_e

        def reduce(v):
            v1 = v[1] - m10 * v[0]
            v2 = v[2] - m20 * v[0] - m21 * v1
            v3 = v[3] - m30 * v[0] - m31 * v1 - m32 * v2
            return v[0], v1, v2, v3

        inv = (inv_a, inv_1, inv_e, inv_3)
        roots = [lax.rsqrt(v) for v in (a, det * inv_a, e, det_2 * inv_e)]
        reduced = reduce(row)
        scaled = [v * w for v, w in zip(reduced, inv)]
        for j in range(4):
            inverse[g] = jnp.where(sub == s + j, reduced[j] * roots[j], inverse[g])
        for i in range(g, groups):
            column = reduce([col[j][i - g] for j in range(4)])
            update = (work[i] - column[0] * scaled[0] - column[1] * scaled[1]) - (
                column[2] * scaled[2] + column[3] * scaled[3]
            )
            for j in range(4):
                keep = column[j] * roots[j]
                if i == g:
                    keep = jnp.where(sub >= s + j, keep, 0.0)
                factor[i] = jnp.where(lanes == k + j, keep, factor[i])
            work[i] = jnp.where(sub > s + 3, update, work[i]) if i == g else update
    return factor, inverse


def basis_kernel(gram_ref, xcat, rank_ref, basis_ref, factor_ref, rows_out):
    probe_count, rows, cols = basis_ref.shape
    halves = cols // BLOCK
    half = probe_count // 2
    groups = probe_count // 8
    sub = lax.broadcasted_iota(jnp.int32, (8, BLOCK), 0)
    lanes = lax.broadcasted_iota(jnp.int32, (8, BLOCK), 1)
    work = []
    for g in range(groups):
        at = 8 * g % half
        own = gram_ref[at : at + 8, :]
        if 8 * g >= half:
            own = shifted(own, probe_count)
        unit = jnp.where(lanes == sub + (8 * g + probe_count), 1.0, 0.0)
        work.append(jnp.where(lanes < probe_count, own, unit))
    factor, inverse = eliminate(work, probe_count)
    rank = rank_ref[0]
    for g in range(groups):
        factor_ref[8 * g : 8 * g + 8, :] = factor[g][:, 0:probe_count]
    lower = jnp.concatenate(
        [
            jnp.where((sub + 8 * g < rank) & (lanes >= probe_count), inverse[g], 0.0)
            for g in range(groups)
        ],
        axis=0,
    )
    lower = lower + shifted(lower, probe_count)
    l_high, l_low = split(lower)
    both = jnp.concatenate([l_high, l_low], axis=0)
    for r in range(rows):
        for h in range(halves):
            here = slice(r * cols + h * BLOCK, r * cols + (h + 1) * BLOCK)
            solved = dot(both, xcat[:, here], NN)
            rows_out[h, pl.ds(r, probe_count, stride=rows), :] = (
                solved[0:probe_count] + solved[probe_count:]
            )
    for h in range(halves):
        basis_ref[:, :, h * BLOCK : (h + 1) * BLOCK] = rows_out[h].reshape(
            probe_count, rows, BLOCK
        )


def per_device(
    n_mesh, n_obs, nz, probes, velocity, viscosity, friction, obs_block, obs_weight, obs_prec, rank
):
    probe_count, rows, cols = probes.shape
    per_dev = obs_weight.shape[1]
    ny = n_mesh // nz
    piece = probe_count // 2 // n_obs
    dma = pltpu.SemaphoreType.DMA
    vmem = pl.BlockSpec(memory_space=pltpu.VMEM)
    xcat, gram = pl.pallas_call(
        functools.partial(sketch_kernel, n_mesh, n_obs, nz),
        out_shape=(
            jax.ShapeDtypeStruct((2 * probe_count, rows * cols), BF16),
            jax.ShapeDtypeStruct((probe_count // 2, BLOCK), F32),
        ),
        in_specs=[pl.BlockSpec(memory_space=pl.ANY)] * 7,
        out_specs=(vmem, vmem),
        scratch_shapes=[
            pltpu.VMEM((probe_count, rows, cols), BF16),
            pltpu.VMEM((rows, cols), F32),
            pltpu.VMEM((1, per_dev), jnp.int32),
            pltpu.VMEM((1, per_dev, BLOCK), F32),
            pltpu.VMEM((1, per_dev), F32),
            pltpu.VMEM((cols // BLOCK, probe_count * rows, BLOCK), F32),
            pltpu.VMEM((rows, probe_count, cols), F32),
            pltpu.VMEM((rows, probe_count, cols), F32),
            pltpu.VMEM((7, rows, cols), F32),
            pltpu.VMEM((2, rows, cols), F32),
            pltpu.VMEM((4, 2, rows, cols), F32),
            pltpu.VMEM((2, probe_count, cols), BF16),
            pltpu.VMEM((2, probe_count, cols), BF16),
            pltpu.VMEM((2, 8, BLOCK), F32),
            pltpu.VMEM((2, 8, BLOCK), F32),
            pltpu.VMEM((2, probe_count, cols), F32),
            pltpu.VMEM((2, 8, BLOCK), F32),
            pltpu.VMEM((2, 8, BLOCK), F32),
            pltpu.VMEM((n_obs, per_dev + 8, BLOCK), F32),
            pltpu.VMEM((n_obs * per_dev, 2 * BLOCK), BF16),
            pltpu.VMEM((cols // BLOCK, rows * probe_count, 2 * BLOCK), BF16),
            pltpu.VMEM((n_obs, piece, BLOCK), F32),
            pltpu.VMEM((n_obs, piece, BLOCK), F32),
            pltpu.VMEM((ny, piece, BLOCK), F32),
            pltpu.VMEM((nz, piece, BLOCK), F32),
            pltpu.VMEM((n_obs, piece, BLOCK), F32),
            dma((7,)),
            dma((10 + n_obs // 2 - 1,)),
            dma((10 + n_obs // 2 - 1,)),
            pltpu.SemaphoreType.REGULAR((2, 2)),
        ],
        compiler_params=pltpu.CompilerParams(collective_id=0, has_side_effects=True),
    )(probes, velocity, viscosity, friction, obs_block, obs_weight, obs_prec)
    basis, factor = pl.pallas_call(
        basis_kernel,
        out_shape=(
            jax.ShapeDtypeStruct((probe_count, rows, cols), F32),
            jax.ShapeDtypeStruct((probe_count, probe_count), F32),
        ),
        in_specs=[vmem, vmem, pl.BlockSpec(memory_space=pltpu.SMEM)],
        out_specs=(vmem, vmem),
        scratch_shapes=[pltpu.VMEM((cols // BLOCK, probe_count * rows, BLOCK), F32)],
    )(gram, xcat, rank)
    return basis, factor


def solution(mesh):
    in_specs = (
        P(None, "mesh", "obs"),
        P("mesh", "obs"),
        P("mesh", "obs"),
        P("mesh", "obs"),
        P("mesh", "obs"),
        P("mesh", "obs", None),
        P("mesh", "obs"),
        P(),
    )
    n_mesh, n_obs = mesh.shape["mesh"], mesh.shape["obs"]
    nz = Z_RING if n_mesh % Z_RING == 0 else n_mesh // 2
    return jax.shard_map(
        functools.partial(per_device, n_mesh, n_obs, nz),
        mesh=mesh,
        in_specs=in_specs,
        out_specs=(P(None, "mesh", "obs"), P()),
        check_vma=False,
    )
```

```python
import functools

import jax
import jax.numpy as jnp
from jax import lax
from jax.experimental import pallas as pl
from jax.experimental.pallas import tpu as pltpu
from jax.sharding import PartitionSpec as P

BLOCK = 128
PRIOR = 1.0
Z_RING = 16
NEAR = 2
WEIGHT_STEPS = 65534.0
PREC_STEPS = 32768.0
MESH = pl.DeviceIdType.MESH
F32 = jnp.float32
BF16 = jnp.bfloat16
NORTH, SOUTH, WEST, EAST = 0, 1, 2, 3
OPPOSITE = (SOUTH, NORTH, EAST, WEST)
NT = (((1,), (1,)), ((), ()))
NN = (((1,), (0,)), ((), ()))


def dot(a, b, dims):
    return lax.dot_general(a, b, dims, preferred_element_type=F32)


def split(x):
    high = x.astype(BF16)
    return high, (x - high.astype(F32)).astype(BF16)


def fixed(x):
    return jnp.floor(x + 0.5).astype(jnp.int32).astype(jnp.int16)


def shifted(x, amount):
    amount %= BLOCK
    return pltpu.roll(x, amount, 1) if amount else x


def sketch_kernel(
    n_mesh,
    n_obs,
    nz,
    probes_hbm,
    vel_hbm,
    visc_hbm,
    fric_hbm,
    block_hbm,
    weight_hbm,
    prec_hbm,
    xcat_hbm,
    gram_hbm,
    probes_ref,
    fric_ref,
    block_ref,
    weight_ref,
    prec_ref,
    probe_pr,
    field,
    forced,
    coef,
    tiles,
    tiles_halo,
    prow,
    prow_halo,
    fcol,
    fcol_halo,
    srow_halo,
    scol,
    scol_halo,
    meta,
    wall,
    wcat,
    tcat,
    xcat,
    part,
    chip_buf,
    plane_buf,
    z_buf,
    both_buf,
    load_sem,
    send_sem,
    recv_sem,
    z_token,
    y_token,
):
    ny = n_mesh // nz
    probe_count, rows, cols = probes_ref.shape
    halves = cols // BLOCK
    slab_columns = halves * n_obs
    per_dev = weight_ref.shape[1]
    obs_total = per_dev * n_obs
    piece = part.shape[1]
    nx = n_obs // 2
    groups = probe_count // 8
    TILES, PROW, FCOL, SROW, SCOL, WALL, CHIP, PLANE, ZS, BOTH = range(10)

    m = lax.axis_index("mesh")
    o = lax.axis_index("obs")
    y = m // nz
    z = lax.rem(m, nz)
    x = o // 2
    core = lax.rem(o, 2)
    sibling = {"obs": o + 1 - 2 * core}
    neighbours = (
        {"mesh": lax.rem(m + n_mesh - 1, n_mesh)},
        {"mesh": lax.rem(m + 1, n_mesh)},
        {"obs": lax.rem(o + n_obs - 1, n_obs)},
        {"obs": lax.rem(o + 1, n_obs)},
    )
    obs_peers = [
        {"obs": lax.rem(o + d, n_obs)}
        for d in sorted(range(1, n_obs), key=lambda d: -min(d, n_obs - d))
    ]
    plane_peers = [
        {"mesh": lax.rem(y + dy, ny) * nz + z, "obs": lax.rem(o + 2 * dx, n_obs)}
        for dx, dy in sorted(
            ((dx, dy) for dx in range(nx) for dy in range(ny) if dx or dy),
            key=lambda d: -min(d[0], nx - d[0]) - min(d[1], ny - d[1]),
        )
    ]
    y_peers = [{"mesh": lax.rem(y + d, ny) * nz + z} for d in range(1, ny)]

    def z_peer(d):
        return {"mesh": y * nz + lax.rem(z + d, nz)}

    z_peers = [z_peer(d) for d in sorted(range(1, nz), key=lambda d: -min(d, nz - d))]
    near_z = [z_peer(d) for d in range(1, nz) if min(d, nz - d) <= NEAR]

    names = (probes_hbm, weight_hbm, block_hbm, prec_hbm, visc_hbm, vel_hbm, fric_hbm)
    places = (probes_ref, weight_ref, block_ref, prec_ref, tiles.at[0], tiles.at[1], fric_ref)
    loads = [
        pltpu.make_async_copy(src, dst, load_sem.at[i])
        for i, (src, dst) in enumerate(zip(names, places))
    ]
    for load in loads:
        load.start()

    barrier = pltpu.get_barrier_semaphore()
    partners = list(neighbours[:2]) + obs_peers + y_peers + near_z
    for peer in partners:
        pl.semaphore_signal(barrier, inc=1, device_id=peer, device_id_type=MESH)

    lane = lax.broadcasted_iota(jnp.int32, (1, BLOCK), 1)
    meta[...] = jnp.zeros((16, BLOCK), F32)
    for load in loads[1:4]:
        load.wait()
    wall[o, 0:per_dev, :] = fixed(weight_ref[0] * WEIGHT_STEPS)
    scaled_prec = prec_ref[...] * PREC_STEPS
    coarse = jnp.floor(scaled_prec)
    meta[0:1, 0:per_dev] = block_ref[...].astype(F32)
    meta[1:2, 0:per_dev] = coarse
    meta[2:3, 0:per_dev] = (scaled_prec - coarse) * (PREC_STEPS - 1)
    tail = meta[...]
    wall[o, per_dev : per_dev + 16, :] = fixed(tail + shifted(tail, per_dev))

    loads[0].wait()
    for h in range(halves):
        probe_pr[h] = (
            probes_ref[:, :, h * BLOCK : (h + 1) * BLOCK]
            .astype(F32)
            .reshape(probe_count * rows, BLOCK)
        )
    for load in loads[4:]:
        load.wait()

    def probe_rows(r):
        return [
            probe_pr[h, pl.ds(r, probe_count, stride=rows), :] for h in range(halves)
        ]

    def packed_edges(src, first):
        at = slice(0, BLOCK) if first else slice(cols - BLOCK, cols)
        out = jnp.zeros((8, BLOCK), F32)
        for g in range(groups):
            own = jnp.zeros((8, BLOCK), F32)
            for r in range(rows):
                value = src[r, 8 * g : 8 * g + 8, at]
                own = jnp.where(lane == r, shifted(value, r + (0 if first else 1)), own)
            out = out + shifted(own, rows * g)
        return out

    for r in range(rows):
        parts = probe_rows(r)
        for h in range(halves):
            at = slice(h * BLOCK, (h + 1) * BLOCK)
            forced[r, :, at] = parts[h] * tiles[1, r : r + 1, at]
            if r == 0:
                prow[0, :, at] = parts[h].astype(BF16)
            if r == rows - 1:
                prow[1, :, at] = parts[h].astype(BF16)
    fcol[0] = packed_edges(forced, True)
    fcol[1] = packed_edges(forced, False)

    pl.semaphore_wait(barrier, len(partners))

    def send(src, dst, stage, peer):
        pltpu.make_async_remote_copy(
            src_ref=src,
            dst_ref=dst,
            send_sem=send_sem.at[stage],
            recv_sem=recv_sem.at[stage],
            device_id=peer,
            device_id_type=MESH,
        ).start()

    def whole(buf, stage):
        return pltpu.make_async_remote_copy(
            src_ref=buf,
            dst_ref=buf,
            send_sem=send_sem.at[stage],
            recv_sem=recv_sem.at[stage],
            device_id=neighbours[NORTH],
            device_id_type=MESH,
        )

    unsent = []

    def arrived(buf, stage):
        copy = whole(buf, stage)
        unsent.append(copy)
        copy.wait_recv()

    for side in range(4):
        send(tiles, tiles_halo.at[OPPOSITE[side]], TILES, neighbours[side])
    for i in range(2):
        send(fcol.at[i], fcol_halo.at[1 - i], FCOL, neighbours[2 + i])
    for i in range(2):
        send(prow.at[i], prow_halo.at[1 - i], PROW, neighbours[i])
    for peer in obs_peers:
        send(wall.at[o], wall.at[o], WALL, peer)

    tokens = []
    reach = NEAR
    while 2 * reach <= nz // 2:
        tokens.append(reach)
        reach *= 2

    def tell(level):
        for side, d in enumerate((tokens[level], nz - tokens[level])):
            pl.semaphore_signal(
                z_token.at[level, side], inc=1, device_id=z_peer(d), device_id_type=MESH
            )

    def hear(level):
        for side in range(2):
            pl.semaphore_wait(z_token.at[level, side], 1)

    for d in range(1, ny):
        pl.semaphore_signal(
            y_token.at[d - 1], inc=1, device_id=y_peers[d - 1], device_id_type=MESH
        )
    if tokens:
        tell(0)

    arrived(tiles_halo, TILES)
    row_id = lax.broadcasted_iota(jnp.int32, (rows, cols), 0)
    col_id = lax.broadcasted_iota(jnp.int32, (rows, cols), 1)
    inner = (m > 0, m < n_mesh - 1, o > 0, o < n_obs - 1)
    visc = tiles[0]

    def face(side, shift, axis, edge):
        ghost = jnp.where(inner[side], pltpu.roll(tiles_halo[side, 0], shift, axis), 0.0)
        return 0.5 * (visc + jnp.where(edge, ghost, pltpu.roll(visc, shift, axis)))

    face_n = face(NORTH, 1, 0, row_id == 0)
    face_s = face(SOUTH, rows - 1, 0, row_id == rows - 1)
    face_w = face(WEST, 1, 1, col_id == 0)
    face_e = face(EAST, cols - 1, 1, col_id == cols - 1)
    coef[0] = fric_ref[...] + face_n + face_s + face_w + face_e
    coef[1] = jnp.where(inner[NORTH] | (row_id > 0), face_n, 0.0)
    coef[2] = jnp.where(inner[SOUTH] | (row_id < rows - 1), face_s, 0.0)
    coef[3] = jnp.where(col_id > 0, face_w, 0.0)
    coef[4] = jnp.where(col_id < cols - 1, face_e, 0.0)
    coef[5] = jnp.where(inner[WEST] & (col_id == 0), face_w, 0.0)
    coef[6] = jnp.where(inner[EAST] & (col_id == cols - 1), face_e, 0.0)

    def interior(src, r):
        left, right = src[r, :, 0:BLOCK], src[r, :, BLOCK:cols]
        left_up, right_up = shifted(left, 1), shifted(right, 1)
        left_dn, right_dn = shifted(left, -1), shifted(right, -1)
        west = (left_up, jnp.where(lane == 0, left_up, right_up))
        east = (jnp.where(lane == BLOCK - 1, right_dn, left_dn), right_dn)
        out = []
        for h, centre in enumerate((left, right)):
            at = slice(h * BLOCK, (h + 1) * BLOCK)
            value = coef[0, r : r + 1, at] * centre
            if r < rows - 1:
                value = value - coef[2, r : r + 1, at] * src[r + 1, :, at]
            if r > 0:
                value = value - coef[1, r : r + 1, at] * src[r - 1, :, at]
            value = value - coef[4, r : r + 1, at] * east[h]
            value = value - coef[3, r : r + 1, at] * west[h]
            out.append(value)
        return out

    def spread(halo):
        return [
            jnp.concatenate([shifted(halo[i], -rows * g) for g in range(groups)], axis=0)
            for i in range(2)
        ]

    def with_columns(out, r, halo):
        from_west = shifted(halo[0], -r)
        from_east = shifted(halo[1], -1 - r)
        return [
            out[0] - coef[5, r : r + 1, 0:BLOCK] * from_west,
            out[1] - coef[6, r : r + 1, BLOCK:cols] * from_east,
        ]

    for r in range(rows):
        left, right = interior(forced, r)
        field[r, :, 0:BLOCK] = left
        field[r, :, BLOCK:cols] = right
    arrived(fcol_halo, FCOL)
    arrived(prow_halo, PROW)
    columns = spread(fcol_halo)
    order = [0, rows - 1] + list(range(1, rows - 1))
    for place, r in enumerate(order):
        out = with_columns([field[r, :, 0:BLOCK], field[r, :, BLOCK:cols]], r, columns)
        for h in range(halves):
            at = slice(h * BLOCK, (h + 1) * BLOCK)
            if r == 0:
                scale = coef[1, 0:1, at] * tiles_halo[NORTH, 1, rows - 1 : rows, at]
                out[h] = out[h] - scale * prow_halo[0, :, at].astype(F32)
            if r == rows - 1:
                scale = coef[2, r : r + 1, at] * tiles_halo[SOUTH, 1, 0:1, at]
                out[h] = out[h] - scale * prow_halo[1, :, at].astype(F32)
            here = slice(place * probe_count, (place + 1) * probe_count)
            tcat[h, here, 0:BLOCK] = out[h].astype(BF16)
            tcat[h, here, BLOCK : 2 * BLOCK] = out[h].astype(BF16)
    if tokens:
        hear(0)
        for level in range(1, len(tokens)):
            tell(level)

    arrived(wall.at[pl.ds(0, n_obs - 1)], WALL)
    for i in range(n_obs):
        w_high, w_low = split(wall[i, 0:per_dev, :].astype(jnp.int32).astype(F32))
        wcat[i * per_dev : (i + 1) * per_dev, 0:BLOCK] = w_high
        wcat[i * per_dev : (i + 1) * per_dev, BLOCK : 2 * BLOCK] = w_low
    per_row = BLOCK // per_dev
    tails = [wall[i, per_dev : per_dev + 16, :].astype(jnp.int32).astype(F32) for i in range(n_obs)]
    chunks = []
    for c in range(obs_total // BLOCK):
        value = tails[c * per_row]
        for k in range(1, per_row):
            value = jnp.where(lane < k * per_dev, value, tails[c * per_row + k])
        chunks.append(value)
    tail = jnp.concatenate(chunks, axis=1)
    obs_at = tail[0:1]
    prec = (tail[1:2] + tail[2:3] * (1.0 / (PREC_STEPS - 1))) * (1.0 / PREC_STEPS)
    obs_scale = prec * (1.0 / WEIGHT_STEPS**2)
    weights = wcat[...]
    for group in (order[:2], order[2:]):
        start = order.index(group[0]) * probe_count
        size = len(group) * probe_count
        for h in range(halves):
            picked = dot(tcat[h, start : start + size, :], weights, NT)
            masked = []
            for k, r in enumerate(group):
                own = (r * slab_columns + o * halves + h).astype(F32)
                scale = jnp.where(obs_at == own, obs_scale, 0.0)
                masked.append(picked[k * probe_count : (k + 1) * probe_count] * scale)
            mis_high, mis_low = split(jnp.concatenate(masked, axis=0))
            both = dot(mis_high, weights, NN)
            low = dot(mis_low, weights[:, 0:BLOCK], NN)
            source = both[:, 0:BLOCK] + (both[:, BLOCK:] + low)
            for k, r in enumerate(group):
                field[r, :, h * BLOCK : (h + 1) * BLOCK] = source[
                    k * probe_count : (k + 1) * probe_count
                ]
        if group[0] == 0:
            for i in range(2):
                send(field.at[(rows - 1) * i], srow_halo.at[1 - i], SROW, neighbours[i])
    scol[0] = packed_edges(field, True)
    scol[1] = packed_edges(field, False)
    for i in range(2):
        send(scol.at[i], scol_halo.at[1 - i], SCOL, neighbours[2 + i])

    for r in range(rows):
        left, right = interior(field, r)
        forced[r, :, 0:BLOCK] = left
        forced[r, :, BLOCK:cols] = right
    arrived(scol_halo, SCOL)
    columns = spread(scol_halo)
    quad = 0.0
    for group in (order[2:], order[:2]):
        if group[0] == 0:
            arrived(srow_halo, SROW)
        for r in group:
            out = with_columns([forced[r, :, 0:BLOCK], forced[r, :, BLOCK:cols]], r, columns)
            parts = probe_rows(r)
            for h in range(halves):
                at = slice(h * BLOCK, (h + 1) * BLOCK)
                if r == 0:
                    out[h] = out[h] - coef[1, 0:1, at] * srow_halo[0, :, at]
                if r == rows - 1:
                    out[h] = out[h] - coef[2, r : r + 1, at] * srow_halo[1, :, at]
                s_high, s_low = split(tiles[1, r : r + 1, at] * out[h] + PRIOR * parts[h])
                here = slice(r * cols + h * BLOCK, r * cols + (h + 1) * BLOCK)
                xcat[0:probe_count, here] = s_high
                xcat[probe_count : 2 * probe_count, here] = s_low
        if group[0] == 0:
            both = [xcat[:, r * cols : (r + 1) * cols] for r in group]
            for sketch in both:
                quad = quad + dot(sketch, sketch, NT)
        else:
            sketch = xcat[:, group[0] * cols : (group[-1] + 1) * cols]
            quad = dot(sketch, sketch, NT)

    keep_sketch = pltpu.make_async_copy(xcat, xcat_hbm, load_sem.at[0])
    keep_sketch.start()
    pair = quad[0:probe_count] + quad[probe_count:]
    gram = pair + shifted(pair, probe_count)
    half = probe_count // 2
    packed = jnp.where(lane < probe_count, gram[0:half], gram[half:])
    for i in range(2):
        part[i] = packed[i * piece : (i + 1) * piece]

    def total(buf, count):
        values = [buf[i] for i in range(count)]
        while len(values) > 1:
            values = [
                sum(values[i : i + 2][1:], values[i]) for i in range(0, len(values), 2)
            ]
        return values[0]

    send(part.at[1 - core], chip_buf, CHIP, sibling)
    for d in range(1, ny):
        pl.semaphore_wait(y_token.at[d - 1], 1)
    arrived(chip_buf, CHIP)
    here = y * nx + x
    plane_buf[here] = part[core] + chip_buf[...]
    for peer in plane_peers:
        send(plane_buf.at[here], plane_buf.at[here], PLANE, peer)
    if tokens:
        for level in range(1, len(tokens)):
            hear(level)
    arrived(plane_buf.at[pl.ds(0, nx * ny - 1)], PLANE)
    z_buf[z] = total(plane_buf, nx * ny)
    for peer in z_peers:
        send(z_buf.at[z], z_buf.at[z], ZS, peer)
    arrived(z_buf.at[pl.ds(0, nz - 1)], ZS)
    cells = rows * cols * n_mesh * n_obs
    both_buf[core] = total(z_buf, nz) / cells
    send(both_buf.at[core], both_buf.at[core], BOTH, sibling)
    arrived(both_buf.at[0], BOTH)
    keep_gram = pltpu.make_async_copy(both_buf, gram_hbm, load_sem.at[1])
    keep_gram.start()
    for copy in unsent:
        copy.wait_send()
    keep_sketch.wait()
    keep_gram.wait()


def eliminate(work, probe_count):
    sub = lax.broadcasted_iota(jnp.int32, (8, BLOCK), 0)
    lanes = lax.broadcasted_iota(jnp.int32, (8, BLOCK), 1)
    groups = len(work)
    factor = [jnp.zeros((8, BLOCK), F32)] * groups
    inverse = [jnp.zeros((8, BLOCK), F32)] * groups

    def wide(x):
        return jnp.broadcast_to(x, (8, BLOCK))

    for k in range(0, probe_count, 4):
        g, s = divmod(k, 8)
        col = [[wide(work[i][:, k + j : k + j + 1]) for i in range(g, groups)] for j in range(4)]
        row = [wide(work[g][s + j : s + j + 1, :]) for j in range(4)]

        def pivot(i, j):
            return wide(col[j][0][s + i : s + i + 1, :])

        a, b, c = pivot(0, 0), pivot(1, 0), pivot(1, 1)
        p, q, t, u = pivot(2, 0), pivot(2, 1), pivot(3, 0), pivot(3, 1)
        det = a * c - b * b
        inv_a, inv_det = 1.0 / a, 1.0 / det
        inv_1 = a * inv_det
        m10 = b * inv_a
        p_0, p_1 = c * p - b * q, a * q - b * p
        t_0, t_1 = c * t - b * u, a * u - b * t
        e = pivot(2, 2) - (p * p_0 + q * p_1) * inv_det
        f = pivot(3, 2) - (t * p_0 + u * p_1) * inv_det
        h = pivot(3, 3) - (t * t_0 + u * t_1) * inv_det
        det_2 = e * h - f * f
        inv_e, inv_det_2 = 1.0 / e, 1.0 / det_2
        inv_3 = e * inv_det_2
        m20, m30 = p * inv_a, t * inv_a
        m21, m31 = (q - m10 * p) * inv_1, (u - m10 * t) * inv_1
        m32 = f * inv_e

        def reduce(v):
            v1 = v[1] - m10 * v[0]
            v2 = v[2] - m20 * v[0] - m21 * v1
            v3 = v[3] - m30 * v[0] - m31 * v1 - m32 * v2
            return v[0], v1, v2, v3

        inv = (inv_a, inv_1, inv_e, inv_3)
        roots = [lax.rsqrt(v) for v in (a, det * inv_a, e, det_2 * inv_e)]
        reduced = reduce(row)
        scaled = [v * w for v, w in zip(reduced, inv)]
        for j in range(4):
            inverse[g] = jnp.where(sub == s + j, reduced[j] * roots[j], inverse[g])
        for i in range(g, groups):
            column = reduce([col[j][i - g] for j in range(4)])
            update = (work[i] - column[0] * scaled[0] - column[1] * scaled[1]) - (
                column[2] * scaled[2] + column[3] * scaled[3]
            )
            for j in range(4):
                keep = column[j] * roots[j]
                if i == g:
                    keep = jnp.where(sub >= s + j, keep, 0.0)
                factor[i] = jnp.where(lanes == k + j, keep, factor[i])
            work[i] = jnp.where(sub > s + 3, update, work[i]) if i == g else update
    return factor, inverse


def basis_kernel(gram_hbm, xcat_hbm, rank_ref, basis_hbm, factor_ref, gram_ref, xcat, out, sem):
    halves, cells, _ = out.shape
    probe_count = factor_ref.shape[0]
    rows = cells // probe_count
    cols = halves * BLOCK
    piece = gram_ref.shape[1]
    groups = probe_count // 8
    load_gram = pltpu.make_async_copy(gram_hbm, gram_ref, sem.at[0])
    load_gram.start()
    load_sketch = pltpu.make_async_copy(xcat_hbm, xcat, sem.at[1])
    load_sketch.start()
    load_gram.wait()
    sub = lax.broadcasted_iota(jnp.int32, (8, BLOCK), 0)
    lanes = lax.broadcasted_iota(jnp.int32, (8, BLOCK), 1)
    work = []
    for g in range(groups):
        at = 8 * g % piece
        own = gram_ref[8 * g // piece % 2, at : at + 8, :]
        if 8 * g >= 2 * piece:
            own = shifted(own, probe_count)
        unit = jnp.where(lanes == sub + (8 * g + probe_count), 1.0, 0.0)
        work.append(jnp.where(lanes < probe_count, own, unit))
    factor, inverse = eliminate(work, probe_count)
    rank = rank_ref[0]
    for g in range(groups):
        factor_ref[8 * g : 8 * g + 8, :] = factor[g][:, 0:probe_count]
    lower = jnp.concatenate(
        [
            jnp.where((sub + 8 * g < rank) & (lanes >= probe_count), inverse[g], 0.0)
            for g in range(groups)
        ],
        axis=0,
    )
    lower = lower + shifted(lower, probe_count)
    l_high, l_low = split(lower)
    both = jnp.concatenate([l_high, l_low], axis=0)
    load_sketch.wait()
    stores = []
    for h in range(halves):
        for r in range(rows):
            here = slice(r * cols + h * BLOCK, r * cols + (h + 1) * BLOCK)
            solved = dot(both, xcat[:, here], NN)
            out[h, pl.ds(r, probe_count, stride=rows), :] = (
                solved[0:probe_count] + solved[probe_count:]
            )
        store = pltpu.make_async_copy(
            out.at[h], basis_hbm.at[:, pl.ds(h * BLOCK, BLOCK)], sem.at[2 + h]
        )
        store.start()
        stores.append(store)
    for store in stores:
        store.wait()


def per_device(
    n_mesh, n_obs, nz, probes, velocity, viscosity, friction, obs_block, obs_weight, obs_prec, rank
):
    probe_count, rows, cols = probes.shape
    per_dev = obs_weight.shape[1]
    ny = n_mesh // nz
    piece = probe_count // 4
    dma = pltpu.SemaphoreType.DMA
    vmem = pl.BlockSpec(memory_space=pltpu.VMEM)
    hbm = pl.BlockSpec(memory_space=pltpu.HBM)
    xcat, gram = pl.pallas_call(
        functools.partial(sketch_kernel, n_mesh, n_obs, nz),
        out_shape=(
            jax.ShapeDtypeStruct((2 * probe_count, rows * cols), BF16),
            jax.ShapeDtypeStruct((2, piece, BLOCK), F32),
        ),
        in_specs=[hbm] * 7,
        out_specs=(hbm, hbm),
        scratch_shapes=[
            pltpu.VMEM((probe_count, rows, cols), BF16),
            pltpu.VMEM((rows, cols), F32),
            pltpu.VMEM((1, per_dev), jnp.int32),
            pltpu.VMEM((1, per_dev, BLOCK), F32),
            pltpu.VMEM((1, per_dev), F32),
            pltpu.VMEM((cols // BLOCK, probe_count * rows, BLOCK), F32),
            pltpu.VMEM((rows, probe_count, cols), F32),
            pltpu.VMEM((rows, probe_count, cols), F32),
            pltpu.VMEM((7, rows, cols), F32),
            pltpu.VMEM((2, rows, cols), F32),
            pltpu.VMEM((4, 2, rows, cols), F32),
            pltpu.VMEM((2, probe_count, cols), BF16),
            pltpu.VMEM((2, probe_count, cols), BF16),
            pltpu.VMEM((2, 8, BLOCK), F32),
            pltpu.VMEM((2, 8, BLOCK), F32),
            pltpu.VMEM((2, probe_count, cols), F32),
            pltpu.VMEM((2, 8, BLOCK), F32),
            pltpu.VMEM((2, 8, BLOCK), F32),
            pltpu.VMEM((16, BLOCK), F32),
            pltpu.VMEM((n_obs, per_dev + 16, BLOCK), jnp.int16),
            pltpu.VMEM((n_obs * per_dev, 2 * BLOCK), BF16),
            pltpu.VMEM((cols // BLOCK, rows * probe_count, 2 * BLOCK), BF16),
            pltpu.VMEM((2 * probe_count, rows * cols), BF16),
            pltpu.VMEM((2, piece, BLOCK), F32),
            pltpu.VMEM((piece, BLOCK), F32),
            pltpu.VMEM((n_obs // 2 * ny, piece, BLOCK), F32),
            pltpu.VMEM((nz, piece, BLOCK), F32),
            pltpu.VMEM((2, piece, BLOCK), F32),
            dma((7,)),
            dma((10,)),
            dma((10,)),
            pltpu.SemaphoreType.REGULAR((2, 2)),
            pltpu.SemaphoreType.REGULAR((max(ny - 1, 1),)),
        ],
        compiler_params=pltpu.CompilerParams(collective_id=0, has_side_effects=True),
    )(probes, velocity, viscosity, friction, obs_block, obs_weight, obs_prec)
    basis, factor = pl.pallas_call(
        basis_kernel,
        out_shape=(
            jax.ShapeDtypeStruct((probe_count * rows, cols), F32),
            jax.ShapeDtypeStruct((probe_count, probe_count), F32),
        ),
        in_specs=[hbm, hbm, pl.BlockSpec(memory_space=pltpu.SMEM)],
        out_specs=(hbm, vmem),
        scratch_shapes=[
            pltpu.VMEM((2, piece, BLOCK), F32),
            pltpu.VMEM((2 * probe_count, rows * cols), BF16),
            pltpu.VMEM((cols // BLOCK, probe_count * rows, BLOCK), F32),
            dma((2 + cols // BLOCK,)),
        ],
    )(gram, xcat, rank)
    return basis.reshape(probe_count, rows, cols), factor


def solution(mesh):
    in_specs = (
        P(None, "mesh", "obs"),
        P("mesh", "obs"),
        P("mesh", "obs"),
        P("mesh", "obs"),
        P("mesh", "obs"),
        P("mesh", "obs", None),
        P("mesh", "obs"),
        P(),
    )
    n_mesh, n_obs = mesh.shape["mesh"], mesh.shape["obs"]
    nz = Z_RING if n_mesh % Z_RING == 0 else n_mesh // 2
    return jax.shard_map(
        functools.partial(per_device, n_mesh, n_obs, nz),
        mesh=mesh,
        in_specs=in_specs,
        out_specs=(P(None, "mesh", "obs"), P()),
        check_vma=False,
    )
```

```python
import functools

import jax
import jax.numpy as jnp
from jax import lax
from jax.experimental import pallas as pl
from jax.experimental.pallas import tpu as pltpu
from jax.sharding import PartitionSpec as P

BLOCK = 128
PRIOR = 1.0
Z_RING = 16
NEAR = 2
PIVOTS = 8
WEIGHT_STEPS = 65534.0
PREC_STEPS = 32768.0
MESH = pl.DeviceIdType.MESH
F32 = jnp.float32
BF16 = jnp.bfloat16
NORTH, SOUTH, WEST, EAST = 0, 1, 2, 3
OPPOSITE = (SOUTH, NORTH, EAST, WEST)
NT = (((1,), (1,)), ((), ()))
NN = (((1,), (0,)), ((), ()))


def dot(a, b, dims):
    return lax.dot_general(a, b, dims, preferred_element_type=F32)


def split(x):
    high = x.astype(BF16)
    return high, (x - high.astype(F32)).astype(BF16)


def fixed(x):
    return jnp.floor(x + 0.5).astype(jnp.int32).astype(jnp.int16)


def shifted(x, amount):
    amount %= BLOCK
    return pltpu.roll(x, amount, 1) if amount else x


def sketch_kernel(
    n_mesh,
    n_obs,
    nz,
    probes_hbm,
    vel_hbm,
    visc_hbm,
    fric_hbm,
    block_hbm,
    weight_hbm,
    prec_hbm,
    xcat_hbm,
    gram_hbm,
    probes_ref,
    fric_ref,
    block_ref,
    weight_ref,
    prec_ref,
    probe_pr,
    field,
    forced,
    coef,
    tiles,
    tiles_halo,
    prow,
    prow_halo,
    fcol,
    fcol_halo,
    srow_halo,
    scol,
    scol_halo,
    meta,
    wall,
    wcat,
    tcat,
    xcat,
    part,
    chip_buf,
    plane_buf,
    z_buf,
    both_buf,
    load_sem,
    send_sem,
    recv_sem,
    z_token,
    y_token,
):
    ny = n_mesh // nz
    probe_count, rows, cols = probes_ref.shape
    halves = cols // BLOCK
    slab_columns = halves * n_obs
    per_dev = weight_ref.shape[1]
    obs_total = per_dev * n_obs
    piece = part.shape[1]
    nx = n_obs // 2
    groups = probe_count // 8
    WALL, CHIP, PLANE, ZS, BOTH, TILES, FORCED, SOURCE = 0, 1, 2, 3, 4, 5, 9, 13

    m = lax.axis_index("mesh")
    o = lax.axis_index("obs")
    y = m // nz
    z = lax.rem(m, nz)
    x = o // 2
    core = lax.rem(o, 2)
    sibling = {"obs": o + 1 - 2 * core}
    neighbours = (
        {"mesh": lax.rem(m + n_mesh - 1, n_mesh)},
        {"mesh": lax.rem(m + 1, n_mesh)},
        {"obs": lax.rem(o + n_obs - 1, n_obs)},
        {"obs": lax.rem(o + 1, n_obs)},
    )
    obs_peers = [
        {"obs": lax.rem(o + d, n_obs)}
        for d in sorted(range(1, n_obs), key=lambda d: -min(d, n_obs - d))
    ]
    plane_peers = [
        {"mesh": lax.rem(y + dy, ny) * nz + z, "obs": lax.rem(o + 2 * dx, n_obs)}
        for dx, dy in sorted(
            ((dx, dy) for dx in range(nx) for dy in range(ny) if dx or dy),
            key=lambda d: -min(d[0], nx - d[0]) - min(d[1], ny - d[1]),
        )
    ]
    y_peers = [{"mesh": lax.rem(y + d, ny) * nz + z} for d in range(1, ny)]

    def z_peer(d):
        return {"mesh": y * nz + lax.rem(z + d, nz)}

    z_peers = [z_peer(d) for d in sorted(range(1, nz), key=lambda d: -min(d, nz - d))]
    near_z = [z_peer(d) for d in range(1, nz) if min(d, nz - d) <= NEAR]

    names = (probes_hbm, weight_hbm, block_hbm, prec_hbm, visc_hbm, vel_hbm, fric_hbm)
    places = (probes_ref, weight_ref, block_ref, prec_ref, tiles.at[0], tiles.at[1], fric_ref)
    loads = [
        pltpu.make_async_copy(src, dst, load_sem.at[i])
        for i, (src, dst) in enumerate(zip(names, places))
    ]
    for load in loads:
        load.start()

    barrier = pltpu.get_barrier_semaphore()
    inner = (m > 0, m < n_mesh - 1, o > 0, o < n_obs - 1)
    over_wrap = (inner[NORTH] & (z == 0), inner[SOUTH] & (z == nz - 1))
    partners = obs_peers + y_peers + near_z
    for peer in partners:
        pl.semaphore_signal(barrier, inc=1, device_id=peer, device_id_type=MESH)
    for side in (NORTH, SOUTH):

        @pl.when(over_wrap[side])
        def _():
            pl.semaphore_signal(
                barrier, inc=1, device_id=neighbours[side], device_id_type=MESH
            )

    rows_in, columns_in = (prow_halo, srow_halo), (fcol_halo, scol_halo)
    for side in range(4):

        @pl.when(jnp.logical_not(inner[side]))
        def _():
            tiles_halo[side] = jnp.zeros((2, rows, cols), F32)
            for buf in columns_in if side >= WEST else rows_in:
                buf[side % 2] = jnp.zeros(buf.shape[1:], buf.dtype)

    lane = lax.broadcasted_iota(jnp.int32, (1, BLOCK), 1)
    meta[...] = jnp.zeros((16, BLOCK), F32)
    for load in loads[1:4]:
        load.wait()
    wall[o, 0:per_dev, :] = fixed(weight_ref[0] * WEIGHT_STEPS)
    scaled_prec = prec_ref[...] * PREC_STEPS
    coarse = jnp.floor(scaled_prec)
    meta[0:1, 0:per_dev] = block_ref[...].astype(F32)
    meta[1:2, 0:per_dev] = coarse
    meta[2:3, 0:per_dev] = (scaled_prec - coarse) * (PREC_STEPS - 1)
    tail = meta[...]
    wall[o, per_dev : per_dev + 16, :] = fixed(tail + shifted(tail, per_dev))

    loads[0].wait()
    for h in range(halves):
        probe_pr[h] = (
            probes_ref[:, :, h * BLOCK : (h + 1) * BLOCK]
            .astype(F32)
            .reshape(probe_count * rows, BLOCK)
        )
    for load in loads[4:]:
        load.wait()

    def probe_rows(r):
        return [
            probe_pr[h, pl.ds(r, probe_count, stride=rows), :] for h in range(halves)
        ]

    def packed_edges(src, first):
        at = slice(0, BLOCK) if first else slice(cols - BLOCK, cols)
        out = jnp.zeros((8, BLOCK), F32)
        for g in range(groups):
            own = jnp.zeros((8, BLOCK), F32)
            for r in range(rows):
                value = src[r, 8 * g : 8 * g + 8, at]
                own = jnp.where(lane == r, shifted(value, r + (0 if first else 1)), own)
            out = out + shifted(own, rows * g)
        return out

    for r in range(rows):
        parts = probe_rows(r)
        for h in range(halves):
            at = slice(h * BLOCK, (h + 1) * BLOCK)
            forced[r, :, at] = parts[h] * tiles[1, r : r + 1, at]
            if r == 0:
                prow[0, :, at] = parts[h].astype(BF16)
            if r == rows - 1:
                prow[1, :, at] = parts[h].astype(BF16)
    fcol[0] = packed_edges(forced, True)
    fcol[1] = packed_edges(forced, False)

    pl.semaphore_wait(
        barrier,
        len(partners) + over_wrap[0].astype(jnp.int32) + over_wrap[1].astype(jnp.int32),
    )

    def send(src, dst, stage, peer):
        pltpu.make_async_remote_copy(
            src_ref=src,
            dst_ref=dst,
            send_sem=send_sem.at[stage],
            recv_sem=recv_sem.at[stage],
            device_id=peer,
            device_id_type=MESH,
        ).start()

    def whole(buf, stage):
        return pltpu.make_async_remote_copy(
            src_ref=buf,
            dst_ref=buf,
            send_sem=send_sem.at[stage],
            recv_sem=recv_sem.at[stage],
            device_id=neighbours[NORTH],
            device_id_type=MESH,
        )

    unsent = []

    def arrived(buf, stage):
        copy = whole(buf, stage)
        unsent.append(copy)
        copy.wait_recv()

    edge_copies = []

    def to_neighbour(src, dst, stage, side):
        there = OPPOSITE[side]

        @pl.when(inner[side])
        def _():
            pltpu.make_async_remote_copy(
                src_ref=src,
                dst_ref=dst,
                send_sem=send_sem.at[stage + side],
                recv_sem=recv_sem.at[stage + there],
                device_id=neighbours[side],
                device_id_type=MESH,
            ).start()

        edge_copies.append((src, stage + side, side))

    def from_neighbour(buf, stage, side):
        @pl.when(inner[side])
        def _():
            whole(buf, stage + side).wait_recv()

    for side in range(4):
        to_neighbour(tiles, tiles_halo.at[OPPOSITE[side]], TILES, side)
    for i in range(2):
        to_neighbour(fcol.at[i], fcol_halo.at[1 - i], FORCED, WEST + i)
    for i in range(2):
        to_neighbour(prow.at[i], prow_halo.at[1 - i], FORCED, NORTH + i)
    for peer in obs_peers:
        send(wall.at[o], wall.at[o], WALL, peer)

    tokens = []
    reach = NEAR
    while 2 * reach <= nz // 2:
        tokens.append(reach)
        reach *= 2

    def tell(level):
        for side, d in enumerate((tokens[level], nz - tokens[level])):
            pl.semaphore_signal(
                z_token.at[level, side], inc=1, device_id=z_peer(d), device_id_type=MESH
            )

    def hear(level):
        for side in range(2):
            pl.semaphore_wait(z_token.at[level, side], 1)

    for d in range(1, ny):
        pl.semaphore_signal(
            y_token.at[d - 1], inc=1, device_id=y_peers[d - 1], device_id_type=MESH
        )
    if tokens:
        tell(0)

    for side in range(4):
        from_neighbour(tiles_halo.at[side], TILES, side)
    row_id = lax.broadcasted_iota(jnp.int32, (rows, cols), 0)
    col_id = lax.broadcasted_iota(jnp.int32, (rows, cols), 1)
    visc = tiles[0]

    def face(side, shift, axis, edge):
        ghost = jnp.where(inner[side], pltpu.roll(tiles_halo[side, 0], shift, axis), 0.0)
        return 0.5 * (visc + jnp.where(edge, ghost, pltpu.roll(visc, shift, axis)))

    face_n = face(NORTH, 1, 0, row_id == 0)
    face_s = face(SOUTH, rows - 1, 0, row_id == rows - 1)
    face_w = face(WEST, 1, 1, col_id == 0)
    face_e = face(EAST, cols - 1, 1, col_id == cols - 1)
    coef[0] = fric_ref[...] + face_n + face_s + face_w + face_e
    coef[1] = jnp.where(inner[NORTH] | (row_id > 0), face_n, 0.0)
    coef[2] = jnp.where(inner[SOUTH] | (row_id < rows - 1), face_s, 0.0)
    coef[3] = jnp.where(col_id > 0, face_w, 0.0)
    coef[4] = jnp.where(col_id < cols - 1, face_e, 0.0)
    coef[5] = jnp.where(inner[WEST] & (col_id == 0), face_w, 0.0)
    coef[6] = jnp.where(inner[EAST] & (col_id == cols - 1), face_e, 0.0)

    def interior(src, r):
        left, right = src[r, :, 0:BLOCK], src[r, :, BLOCK:cols]
        left_up, right_up = shifted(left, 1), shifted(right, 1)
        left_dn, right_dn = shifted(left, -1), shifted(right, -1)
        west = (left_up, jnp.where(lane == 0, left_up, right_up))
        east = (jnp.where(lane == BLOCK - 1, right_dn, left_dn), right_dn)
        out = []
        for h, centre in enumerate((left, right)):
            at = slice(h * BLOCK, (h + 1) * BLOCK)
            value = coef[0, r : r + 1, at] * centre
            if r < rows - 1:
                value = value - coef[2, r : r + 1, at] * src[r + 1, :, at]
            if r > 0:
                value = value - coef[1, r : r + 1, at] * src[r - 1, :, at]
            value = value - coef[4, r : r + 1, at] * east[h]
            value = value - coef[3, r : r + 1, at] * west[h]
            out.append(value)
        return out

    def spread(halo):
        return [
            jnp.concatenate([shifted(halo[i], -rows * g) for g in range(groups)], axis=0)
            for i in range(2)
        ]

    def with_columns(out, r, halo):
        from_west = shifted(halo[0], -r)
        from_east = shifted(halo[1], -1 - r)
        return [
            out[0] - coef[5, r : r + 1, 0:BLOCK] * from_west,
            out[1] - coef[6, r : r + 1, BLOCK:cols] * from_east,
        ]

    for r in range(rows):
        left, right = interior(forced, r)
        field[r, :, 0:BLOCK] = left
        field[r, :, BLOCK:cols] = right
    for i in range(2):
        from_neighbour(fcol_halo.at[i], FORCED, WEST + i)
    columns = spread(fcol_halo)
    order = [0, rows - 1] + list(range(1, rows - 1))

    def tangent(r):
        out = with_columns([field[r, :, 0:BLOCK], field[r, :, BLOCK:cols]], r, columns)
        place = order.index(r)
        here = slice(place * probe_count, (place + 1) * probe_count)
        for h in range(halves):
            at = slice(h * BLOCK, (h + 1) * BLOCK)
            if r == 0:
                scale = coef[1, 0:1, at] * tiles_halo[NORTH, 1, rows - 1 : rows, at]
                out[h] = out[h] - scale * prow_halo[0, :, at].astype(F32)
            if r == rows - 1:
                scale = coef[2, r : r + 1, at] * tiles_halo[SOUTH, 1, 0:1, at]
                out[h] = out[h] - scale * prow_halo[1, :, at].astype(F32)
            tcat[h, here, 0:BLOCK] = out[h].astype(BF16)
            tcat[h, here, BLOCK : 2 * BLOCK] = out[h].astype(BF16)

    for r in order[2:]:
        tangent(r)
    if tokens:
        hear(0)
        for level in range(1, len(tokens)):
            tell(level)

    arrived(wall.at[pl.ds(0, n_obs - 1)], WALL)
    for i in range(n_obs):
        w_high, w_low = split(wall[i, 0:per_dev, :].astype(jnp.int32).astype(F32))
        wcat[i * per_dev : (i + 1) * per_dev, 0:BLOCK] = w_high
        wcat[i * per_dev : (i + 1) * per_dev, BLOCK : 2 * BLOCK] = w_low
    per_row = BLOCK // per_dev
    tails = [wall[i, per_dev : per_dev + 16, :].astype(jnp.int32).astype(F32) for i in range(n_obs)]
    chunks = []
    for c in range(obs_total // BLOCK):
        value = tails[c * per_row]
        for k in range(1, per_row):
            value = jnp.where(lane < k * per_dev, value, tails[c * per_row + k])
        chunks.append(value)
    tail = jnp.concatenate(chunks, axis=1)
    obs_at = tail[0:1]
    prec = (tail[1:2] + tail[2:3] * (1.0 / (PREC_STEPS - 1))) * (1.0 / PREC_STEPS)
    obs_scale = prec * (1.0 / WEIGHT_STEPS**2)
    weights = wcat[...]
    for i in range(2):
        from_neighbour(prow_halo.at[i], FORCED, NORTH + i)
    for r in order[:2]:
        tangent(r)
    for group in (order[:2], order[2:]):
        start = order.index(group[0]) * probe_count
        size = len(group) * probe_count
        for h in range(halves):
            picked = dot(tcat[h, start : start + size, :], weights, NT)
            masked = []
            for k, r in enumerate(group):
                own = (r * slab_columns + o * halves + h).astype(F32)
                scale = jnp.where(obs_at == own, obs_scale, 0.0)
                masked.append(picked[k * probe_count : (k + 1) * probe_count] * scale)
            mis_high, mis_low = split(jnp.concatenate(masked, axis=0))
            both = dot(mis_high, weights, NN)
            low = dot(mis_low, weights[:, 0:BLOCK], NN)
            source = both[:, 0:BLOCK] + (both[:, BLOCK:] + low)
            for k, r in enumerate(group):
                field[r, :, h * BLOCK : (h + 1) * BLOCK] = source[
                    k * probe_count : (k + 1) * probe_count
                ]
        if group[0] == 0:
            for i in range(2):
                to_neighbour(field.at[(rows - 1) * i], srow_halo.at[1 - i], SOURCE, NORTH + i)
    scol[0] = packed_edges(field, True)
    scol[1] = packed_edges(field, False)
    for i in range(2):
        to_neighbour(scol.at[i], scol_halo.at[1 - i], SOURCE, WEST + i)

    for r in range(rows):
        left, right = interior(field, r)
        forced[r, :, 0:BLOCK] = left
        forced[r, :, BLOCK:cols] = right
    for i in range(2):
        from_neighbour(scol_halo.at[i], SOURCE, WEST + i)
    columns = spread(scol_halo)
    quad = 0.0
    for group in (order[2:], order[:2]):
        if group[0] == 0:
            for i in range(2):
                from_neighbour(srow_halo.at[i], SOURCE, NORTH + i)
        for r in group:
            out = with_columns([forced[r, :, 0:BLOCK], forced[r, :, BLOCK:cols]], r, columns)
            parts = probe_rows(r)
            for h in range(halves):
                at = slice(h * BLOCK, (h + 1) * BLOCK)
                if r == 0:
                    out[h] = out[h] - coef[1, 0:1, at] * srow_halo[0, :, at]
                if r == rows - 1:
                    out[h] = out[h] - coef[2, r : r + 1, at] * srow_halo[1, :, at]
                s_high, s_low = split(tiles[1, r : r + 1, at] * out[h] + PRIOR * parts[h])
                here = slice(r * cols + h * BLOCK, r * cols + (h + 1) * BLOCK)
                xcat[0:probe_count, here] = s_high
                xcat[probe_count : 2 * probe_count, here] = s_low
        if group[0] == 0:
            both = [xcat[:, r * cols : (r + 1) * cols] for r in group]
            for sketch in both:
                quad = quad + dot(sketch, sketch, NT)
        else:
            sketch = xcat[:, group[0] * cols : (group[-1] + 1) * cols]
            quad = dot(sketch, sketch, NT)

    keep_sketch = pltpu.make_async_copy(xcat, xcat_hbm, load_sem.at[0])
    keep_sketch.start()
    pair = quad[0:probe_count] + quad[probe_count:]
    gram = pair + shifted(pair, probe_count)
    half = probe_count // 2
    packed = jnp.where(lane < probe_count, gram[0:half], gram[half:])
    for i in range(2):
        part[i] = packed[i * piece : (i + 1) * piece]

    def total(buf, count):
        values = [buf[i] for i in range(count)]
        while len(values) > 1:
            values = [
                sum(values[i : i + 2][1:], values[i]) for i in range(0, len(values), 2)
            ]
        return values[0]

    send(part.at[1 - core], chip_buf, CHIP, sibling)
    for d in range(1, ny):
        pl.semaphore_wait(y_token.at[d - 1], 1)
    arrived(chip_buf, CHIP)
    here = y * nx + x
    plane_buf[here] = part[core] + chip_buf[...]
    for peer in plane_peers:
        send(plane_buf.at[here], plane_buf.at[here], PLANE, peer)
    if tokens:
        for level in range(1, len(tokens)):
            hear(level)
    arrived(plane_buf.at[pl.ds(0, nx * ny - 1)], PLANE)
    z_buf[z] = total(plane_buf, nx * ny)
    for peer in z_peers:
        send(z_buf.at[z], z_buf.at[z], ZS, peer)
    arrived(z_buf.at[pl.ds(0, nz - 1)], ZS)
    cells = rows * cols * n_mesh * n_obs
    both_buf[core] = total(z_buf, nz) / cells
    send(both_buf.at[core], both_buf.at[core], BOTH, sibling)
    arrived(both_buf.at[0], BOTH)
    keep_gram = pltpu.make_async_copy(both_buf, gram_hbm, load_sem.at[1])
    keep_gram.start()
    for copy in unsent:
        copy.wait_send()
    for src, at, side in edge_copies:

        @pl.when(inner[side])
        def _():
            whole(src, at).wait_send()

    keep_sketch.wait()
    keep_gram.wait()


def eliminate(work, probe_count):
    sub = lax.broadcasted_iota(jnp.int32, (8, BLOCK), 0)
    lanes = lax.broadcasted_iota(jnp.int32, (8, BLOCK), 1)
    groups = len(work)
    factor = [jnp.zeros((8, BLOCK), F32)] * groups
    inverse = [jnp.zeros((8, BLOCK), F32)] * groups

    def wide(x):
        return jnp.broadcast_to(x, (8, BLOCK))

    for k in range(0, probe_count, PIVOTS):
        g, s = divmod(k, 8)
        span = range(PIVOTS)
        col = [[wide(work[i][:, k + j : k + j + 1]) for i in range(g, groups)] for j in span]
        row = [wide(work[g][s + j : s + j + 1, :]) for j in span]
        local = [[wide(col[j][0][s + i : s + i + 1, :]) for j in range(i + 1)] for i in span]
        lower = [[None] * PIVOTS for _ in span]
        inv, roots = [], []
        for p in range(0, PIVOTS, 2):
            a, b, c = local[p][p], local[p + 1][p], local[p + 1][p + 1]
            det = a * c - b * b
            inv_a, inv_det = 1.0 / a, 1.0 / det
            inv_1 = a * inv_det
            slope = b * inv_a
            inv += [inv_a, inv_1]
            roots += [lax.rsqrt(a), lax.rsqrt(det * inv_a)]
            lower[p + 1][p] = slope
            for i in range(p + 2, PIVOTS):
                u, v = local[i][p], local[i][p + 1]
                lower[i][p] = u * inv_a
                lower[i][p + 1] = (v - slope * u) * inv_1
                for j in range(p + 2, i + 1):
                    t, w = local[j][p], local[j][p + 1]
                    local[i][j] = (
                        local[i][j] - (u * (c * t - b * w) + v * (a * w - b * t)) * inv_det
                    )

        def reduce(v):
            done = []
            for j in span:
                value = v[j]
                for i in range(j):
                    value = value - lower[j][i] * done[i]
                done.append(value)
            return done

        reduced = reduce(row)
        scaled = [v * w for v, w in zip(reduced, inv)]
        for j in span:
            inverse[g] = jnp.where(sub == s + j, reduced[j] * roots[j], inverse[g])
        for i in range(g, groups):
            column = reduce([col[j][i - g] for j in span])
            if not (i == g and s + PIVOTS == 8):
                update = work[i]
                for j in range(0, PIVOTS, 2):
                    update = update - (column[j] * scaled[j] + column[j + 1] * scaled[j + 1])
                work[i] = jnp.where(sub >= s + PIVOTS, update, work[i]) if i == g else update
            for j in span:
                keep = column[j] * roots[j]
                if i == g:
                    keep = jnp.where(sub >= s + j, keep, 0.0)
                factor[i] = jnp.where(lanes == k + j, keep, factor[i])
    return factor, inverse


def basis_kernel(
    gram_hbm, xcat_hbm, rank_hbm, basis_hbm, factor_ref, gram_ref, xcat, rank_ref, out, sem
):
    halves, cells, _ = out.shape
    probe_count = factor_ref.shape[0]
    rows = cells // probe_count
    cols = halves * BLOCK
    piece = gram_ref.shape[1]
    groups = probe_count // 8
    load_gram = pltpu.make_async_copy(gram_hbm, gram_ref, sem.at[0])
    load_gram.start()
    load_sketch = pltpu.make_async_copy(xcat_hbm, xcat, sem.at[1])
    load_sketch.start()
    load_rank = pltpu.make_async_copy(rank_hbm, rank_ref, sem.at[2])
    load_rank.start()
    load_gram.wait()
    sub = lax.broadcasted_iota(jnp.int32, (8, BLOCK), 0)
    lanes = lax.broadcasted_iota(jnp.int32, (8, BLOCK), 1)
    work = []
    for g in range(groups):
        at = 8 * g % piece
        own = gram_ref[8 * g // piece % 2, at : at + 8, :]
        if 8 * g >= 2 * piece:
            own = shifted(own, probe_count)
        unit = jnp.where(lanes == sub + (8 * g + probe_count), 1.0, 0.0)
        work.append(jnp.where(lanes < probe_count, own, unit))
    factor, inverse = eliminate(work, probe_count)
    load_rank.wait()
    rank = rank_ref[0]
    for g in range(groups):
        factor_ref[8 * g : 8 * g + 8, :] = factor[g][:, 0:probe_count]
    lower = jnp.concatenate(
        [
            jnp.where((sub + 8 * g < rank) & (lanes >= probe_count), inverse[g], 0.0)
            for g in range(groups)
        ],
        axis=0,
    )
    lower = lower + shifted(lower, probe_count)
    l_high, l_low = split(lower)
    both = jnp.concatenate([l_high, l_low], axis=0)
    load_sketch.wait()
    stores = []
    for h in range(halves):
        for r in range(rows):
            here = slice(r * cols + h * BLOCK, r * cols + (h + 1) * BLOCK)
            solved = dot(both, xcat[:, here], NN)
            out[h, pl.ds(r, probe_count, stride=rows), :] = (
                solved[0:probe_count] + solved[probe_count:]
            )
        store = pltpu.make_async_copy(
            out.at[h], basis_hbm.at[:, pl.ds(h * BLOCK, BLOCK)], sem.at[3 + h]
        )
        store.start()
        stores.append(store)
    for store in stores:
        store.wait()


def per_device(
    n_mesh, n_obs, nz, probes, velocity, viscosity, friction, obs_block, obs_weight, obs_prec, rank
):
    probe_count, rows, cols = probes.shape
    per_dev = obs_weight.shape[1]
    ny = n_mesh // nz
    piece = probe_count // 4
    dma = pltpu.SemaphoreType.DMA
    vmem = pl.BlockSpec(memory_space=pltpu.VMEM)
    hbm = pl.BlockSpec(memory_space=pltpu.HBM)
    xcat, gram = pl.pallas_call(
        functools.partial(sketch_kernel, n_mesh, n_obs, nz),
        out_shape=(
            jax.ShapeDtypeStruct((2 * probe_count, rows * cols), BF16),
            jax.ShapeDtypeStruct((2, piece, BLOCK), F32),
        ),
        in_specs=[hbm] * 7,
        out_specs=(hbm, hbm),
        scratch_shapes=[
            pltpu.VMEM((probe_count, rows, cols), BF16),
            pltpu.VMEM((rows, cols), F32),
            pltpu.VMEM((1, per_dev), jnp.int32),
            pltpu.VMEM((1, per_dev, BLOCK), F32),
            pltpu.VMEM((1, per_dev), F32),
            pltpu.VMEM((cols // BLOCK, probe_count * rows, BLOCK), F32),
            pltpu.VMEM((rows, probe_count, cols), F32),
            pltpu.VMEM((rows, probe_count, cols), F32),
            pltpu.VMEM((7, rows, cols), F32),
            pltpu.VMEM((2, rows, cols), F32),
            pltpu.VMEM((4, 2, rows, cols), F32),
            pltpu.VMEM((2, probe_count, cols), BF16),
            pltpu.VMEM((2, probe_count, cols), BF16),
            pltpu.VMEM((2, 8, BLOCK), F32),
            pltpu.VMEM((2, 8, BLOCK), F32),
            pltpu.VMEM((2, probe_count, cols), F32),
            pltpu.VMEM((2, 8, BLOCK), F32),
            pltpu.VMEM((2, 8, BLOCK), F32),
            pltpu.VMEM((16, BLOCK), F32),
            pltpu.VMEM((n_obs, per_dev + 16, BLOCK), jnp.int16),
            pltpu.VMEM((n_obs * per_dev, 2 * BLOCK), BF16),
            pltpu.VMEM((cols // BLOCK, rows * probe_count, 2 * BLOCK), BF16),
            pltpu.VMEM((2 * probe_count, rows * cols), BF16),
            pltpu.VMEM((2, piece, BLOCK), F32),
            pltpu.VMEM((piece, BLOCK), F32),
            pltpu.VMEM((n_obs // 2 * ny, piece, BLOCK), F32),
            pltpu.VMEM((nz, piece, BLOCK), F32),
            pltpu.VMEM((2, piece, BLOCK), F32),
            dma((7,)),
            dma((17,)),
            dma((17,)),
            pltpu.SemaphoreType.REGULAR((2, 2)),
            pltpu.SemaphoreType.REGULAR((max(ny - 1, 1),)),
        ],
        compiler_params=pltpu.CompilerParams(collective_id=0, has_side_effects=True),
    )(probes, velocity, viscosity, friction, obs_block, obs_weight, obs_prec)
    basis, factor = pl.pallas_call(
        basis_kernel,
        out_shape=(
            jax.ShapeDtypeStruct((probe_count * rows, cols), F32),
            jax.ShapeDtypeStruct((probe_count, probe_count), F32),
        ),
        in_specs=[hbm, hbm, hbm],
        out_specs=(hbm, vmem),
        scratch_shapes=[
            pltpu.VMEM((2, piece, BLOCK), F32),
            pltpu.VMEM((2 * probe_count, rows * cols), BF16),
            pltpu.SMEM((1,), jnp.int32),
            pltpu.VMEM((cols // BLOCK, probe_count * rows, BLOCK), F32),
            dma((3 + cols // BLOCK,)),
        ],
    )(gram, xcat, rank)
    return basis.reshape(probe_count, rows, cols), factor


def solution(mesh):
    in_specs = (
        P(None, "mesh", "obs"),
        P("mesh", "obs"),
        P("mesh", "obs"),
        P("mesh", "obs"),
        P("mesh", "obs"),
        P("mesh", "obs", None),
        P("mesh", "obs"),
        P(),
    )
    n_mesh, n_obs = mesh.shape["mesh"], mesh.shape["obs"]
    nz = Z_RING if n_mesh % Z_RING == 0 else n_mesh // 2
    return jax.shard_map(
        functools.partial(per_device, n_mesh, n_obs, nz),
        mesh=mesh,
        in_specs=in_specs,
        out_specs=(P(None, "mesh", "obs"), P()),
        check_vma=False,
    )
```

```python
import functools

import jax
import jax.numpy as jnp
from jax import lax
from jax.experimental import pallas as pl
from jax.experimental.pallas import tpu as pltpu
from jax.sharding import PartitionSpec as P

BLOCK = 128
PRIOR = 1.0
Z_RING = 16
NEAR = 1
PIVOTS = 8
WEIGHT_STEPS = 65534.0
PREC_STEPS = 32768.0
MESH = pl.DeviceIdType.MESH
F32 = jnp.float32
BF16 = jnp.bfloat16
NORTH, SOUTH, WEST, EAST = 0, 1, 2, 3
OPPOSITE = (SOUTH, NORTH, EAST, WEST)
NT = (((1,), (1,)), ((), ()))
NN = (((1,), (0,)), ((), ()))


def dot(a, b, dims):
    return lax.dot_general(a, b, dims, preferred_element_type=F32)


def split(x):
    high = x.astype(BF16)
    return high, (x - high.astype(F32)).astype(BF16)


def fixed(x):
    return jnp.floor(x + 0.5).astype(jnp.int32).astype(jnp.int16)


def shifted(x, amount):
    amount %= BLOCK
    return pltpu.roll(x, amount, 1) if amount else x


def sketch_kernel(
    n_mesh,
    n_obs,
    nz,
    probes_hbm,
    vel_hbm,
    visc_hbm,
    fric_hbm,
    block_hbm,
    weight_hbm,
    prec_hbm,
    xcat_hbm,
    gram_hbm,
    probes_ref,
    fric_ref,
    block_ref,
    weight_ref,
    prec_ref,
    probe_pr,
    field,
    forced,
    coef,
    tiles,
    edge_rows,
    rows_halo,
    cols_halo,
    prow,
    prow_halo,
    fcol,
    fcol_halo,
    srow_halo,
    scol,
    scol_halo,
    meta,
    wall,
    wcat,
    tcat,
    xcat,
    part,
    chip_buf,
    plane_buf,
    z_buf,
    both_buf,
    load_sem,
    send_sem,
    recv_sem,
    z_token,
    y_token,
):
    ny = n_mesh // nz
    probe_count, rows, cols = probes_ref.shape
    halves = cols // BLOCK
    slab_columns = halves * n_obs
    per_dev = weight_ref.shape[1]
    obs_total = per_dev * n_obs
    piece = part.shape[1]
    nx = n_obs // 2
    groups = probe_count // 8
    WALL, RELAY, CHIP, PLANE, ZS, BOTH, TILES, FORCED, SOURCE = 0, 1, 2, 3, 4, 5, 6, 10, 14

    m = lax.axis_index("mesh")
    o = lax.axis_index("obs")
    y = m // nz
    z = lax.rem(m, nz)
    x = o // 2
    core = lax.rem(o, 2)
    sibling = {"obs": o + 1 - 2 * core}
    neighbours = (
        {"mesh": lax.rem(m + n_mesh - 1, n_mesh)},
        {"mesh": lax.rem(m + 1, n_mesh)},
        {"obs": lax.rem(o + n_obs - 1, n_obs)},
        {"obs": lax.rem(o + 1, n_obs)},
    )

    def chip_of(d):
        same = lax.rem(o + 2 * (d % nx), n_obs)
        return {"obs": same}, {"obs": same + 1 - 2 * core}

    chips = [chip_of(d) for d in ((1, nx - 1) if nx > 2 else (1,))]
    plane_peers = [
        {"mesh": lax.rem(y + dy, ny) * nz + z, "obs": lax.rem(o + 2 * dx, n_obs)}
        for dx, dy in sorted(
            ((dx, dy) for dx in range(nx) for dy in range(ny) if dx or dy),
            key=lambda d: -min(d[0], nx - d[0]) - min(d[1], ny - d[1]),
        )
    ]

    def y_peer(d):
        return {"mesh": lax.rem(y + d, ny) * nz + z}

    def z_peer(d):
        return {"mesh": y * nz + lax.rem(z + d, nz)}

    z_peers = [z_peer(d) for d in sorted(range(1, nz), key=lambda d: -min(d, nz - d))]
    near_z = [z_peer(d) for d in range(1, nz) if min(d, nz - d) <= NEAR]

    names = (probes_hbm, weight_hbm, block_hbm, prec_hbm, visc_hbm, vel_hbm, fric_hbm)
    places = (probes_ref, weight_ref, block_ref, prec_ref, tiles.at[0], tiles.at[1], fric_ref)
    loads = [
        pltpu.make_async_copy(src, dst, load_sem.at[i])
        for i, (src, dst) in enumerate(zip(names, places))
    ]
    barrier = pltpu.get_barrier_semaphore()
    inner = (m > 0, m < n_mesh - 1, o > 0, o < n_obs - 1)
    over_wrap = (inner[NORTH] & (z == 0), inner[SOUTH] & (z == nz - 1))
    partners = [peer for pair in chips for peer in pair] + near_z
    partners += [y_peer(d) for d in sorted({1, ny - 1})] + [sibling]
    for peer in partners:
        pl.semaphore_signal(barrier, inc=1, device_id=peer, device_id_type=MESH)
    for side in (NORTH, SOUTH):

        @pl.when(over_wrap[side])
        def _():
            pl.semaphore_signal(
                barrier, inc=1, device_id=neighbours[side], device_id_type=MESH
            )

    for load in loads:
        load.start()

    rows_in = (rows_halo, prow_halo, srow_halo)
    columns_in = (cols_halo, fcol_halo, scol_halo)
    for side in range(4):

        @pl.when(jnp.logical_not(inner[side]))
        def _():
            for buf in columns_in if side >= WEST else rows_in:
                buf[side % 2] = jnp.zeros(buf.shape[1:], buf.dtype)

    lane = lax.broadcasted_iota(jnp.int32, (1, BLOCK), 1)
    meta[...] = jnp.zeros((16, BLOCK), F32)
    for load in loads[1:4]:
        load.wait()
    wall[o, 0:per_dev, :] = fixed(weight_ref[0] * WEIGHT_STEPS)
    scaled_prec = prec_ref[...] * PREC_STEPS
    coarse = jnp.floor(scaled_prec)
    meta[0:1, 0:per_dev] = block_ref[...].astype(F32)
    meta[1:2, 0:per_dev] = coarse
    meta[2:3, 0:per_dev] = (scaled_prec - coarse) * (PREC_STEPS - 1)
    tail = meta[...]
    wall[o, per_dev : per_dev + 16, :] = fixed(tail + shifted(tail, per_dev))

    loads[0].wait()
    for h in range(halves):
        probe_pr[h] = (
            probes_ref[:, :, h * BLOCK : (h + 1) * BLOCK]
            .astype(F32)
            .reshape(probe_count * rows, BLOCK)
        )
    for load in loads[4:]:
        load.wait()

    def probe_rows(r):
        return [
            probe_pr[h, pl.ds(r, probe_count, stride=rows), :] for h in range(halves)
        ]

    def packed_edges(src, first):
        at = slice(0, BLOCK) if first else slice(cols - BLOCK, cols)
        out = jnp.zeros((8, BLOCK), F32)
        for g in range(groups):
            own = jnp.zeros((8, BLOCK), F32)
            for r in range(rows):
                value = src[r, 8 * g : 8 * g + 8, at]
                own = jnp.where(lane == r, shifted(value, r + (0 if first else 1)), own)
            out = out + shifted(own, rows * g)
        return out

    for r in range(rows):
        parts = probe_rows(r)
        for h in range(halves):
            at = slice(h * BLOCK, (h + 1) * BLOCK)
            forced[r, :, at] = parts[h] * tiles[1, r : r + 1, at]
            if r == 0:
                prow[0, :, at] = parts[h].astype(BF16)
            if r == rows - 1:
                prow[1, :, at] = parts[h].astype(BF16)
    eight = lax.broadcasted_iota(jnp.int32, (8, cols), 0)
    for i, r in enumerate((0, rows - 1)):
        edge_rows[i] = jnp.where(eight == 0, tiles[0, r : r + 1, :], tiles[1, r : r + 1, :])
    fcol[0] = packed_edges(forced, True)
    fcol[1] = packed_edges(forced, False)

    pl.semaphore_wait(
        barrier,
        len(partners) + over_wrap[0].astype(jnp.int32) + over_wrap[1].astype(jnp.int32),
    )

    def send(src, dst, stage, peer):
        pltpu.make_async_remote_copy(
            src_ref=src,
            dst_ref=dst,
            send_sem=send_sem.at[stage],
            recv_sem=recv_sem.at[stage],
            device_id=peer,
            device_id_type=MESH,
        ).start()

    def whole(buf, stage):
        return pltpu.make_async_remote_copy(
            src_ref=buf,
            dst_ref=buf,
            send_sem=send_sem.at[stage],
            recv_sem=recv_sem.at[stage],
            device_id=neighbours[NORTH],
            device_id_type=MESH,
        )

    unsent = []

    def arrived(buf, stage):
        copy = whole(buf, stage)
        unsent.append(copy)
        copy.wait_recv()

    edge_copies = []

    def to_neighbour(src, dst, stage, side):
        there = OPPOSITE[side]

        @pl.when(inner[side])
        def _():
            pltpu.make_async_remote_copy(
                src_ref=src,
                dst_ref=dst,
                send_sem=send_sem.at[stage + side],
                recv_sem=recv_sem.at[stage + there],
                device_id=neighbours[side],
                device_id_type=MESH,
            ).start()

        edge_copies.append((src, stage + side, side))

    def from_neighbour(buf, stage, side):
        @pl.when(inner[side])
        def _():
            whole(buf, stage + side).wait_recv()

    relays = nx == 4
    if relays:
        ahead, behind = lax.rem(o + 2 - 4 * core + n_obs, n_obs), lax.rem(o - 2 + 4 * core + n_obs, n_obs)
        for pair, relay_core in zip(chips, (0, 1)):
            stage = jnp.where(core == relay_core, RELAY, WALL)
            send(wall.at[o], wall.at[o], stage, pair[0])
    for pair in chips:
        for peer in pair[1:] if relays else pair:
            send(wall.at[o], wall.at[o], WALL, peer)
    send(wall.at[o], wall.at[o], WALL, sibling)
    for i in range(2):
        edge = pl.ds(0, BLOCK) if i == 0 else pl.ds(cols - BLOCK, BLOCK)
        to_neighbour(tiles.at[0, :, edge], cols_halo.at[1 - i], TILES, WEST + i)
        to_neighbour(edge_rows.at[i], rows_halo.at[1 - i], TILES, NORTH + i)
    for i in range(2):
        to_neighbour(fcol.at[i], fcol_halo.at[1 - i], FORCED, WEST + i)
    for i in range(2):
        to_neighbour(prow.at[i], prow_halo.at[1 - i], FORCED, NORTH + i)

    tokens = []
    reach = NEAR
    while 2 * reach <= nz // 2:
        tokens.append(reach)
        reach *= 2

    def tell(level):
        for side, d in enumerate((tokens[level], nz - tokens[level])):
            pl.semaphore_signal(
                z_token.at[level, side], inc=1, device_id=z_peer(d), device_id_type=MESH
            )

    def hear(level):
        for side in range(2):
            pl.semaphore_wait(z_token.at[level, side], 1)

    def advance(level):
        if level < len(tokens):
            hear(level)
            if level + 1 < len(tokens):
                tell(level + 1)

    def tell_y(level):
        for side, d in enumerate((1, ny - 1)):
            pl.semaphore_signal(
                y_token.at[level, side], inc=1, device_id=y_peer(d), device_id_type=MESH
            )

    def hear_y(level):
        for side in range(2):
            pl.semaphore_wait(y_token.at[level, side], 1)

    if tokens:
        tell(0)
    if relays:
        arrived(wall.at[behind], RELAY)
        for peer in ({"obs": ahead}, {"obs": ahead + 1 - 2 * core}):
            send(wall.at[behind], wall.at[behind], WALL, peer)

    for i in range(2):
        from_neighbour(rows_halo.at[i], TILES, NORTH + i)
        from_neighbour(cols_halo.at[i], TILES, WEST + i)
    row_id = lax.broadcasted_iota(jnp.int32, (rows, cols), 0)
    col_id = lax.broadcasted_iota(jnp.int32, (rows, cols), 1)
    visc = tiles[0]

    def face(side, ghost, shift, axis, edge):
        ghost = jnp.where(inner[side], ghost, 0.0)
        return 0.5 * (visc + jnp.where(edge, ghost, pltpu.roll(visc, shift, axis)))

    from_west, from_east = shifted(cols_halo[0], 1), shifted(cols_halo[1], -1)
    face_n = face(NORTH, rows_halo[0, 0:1, :], 1, 0, row_id == 0)
    face_s = face(SOUTH, rows_halo[1, 0:1, :], rows - 1, 0, row_id == rows - 1)
    face_w = face(WEST, jnp.concatenate([from_west] * halves, axis=1), 1, 1, col_id == 0)
    face_e = face(
        EAST, jnp.concatenate([from_east] * halves, axis=1), cols - 1, 1, col_id == cols - 1
    )
    coef[0] = fric_ref[...] + face_n + face_s + face_w + face_e
    coef[1] = jnp.where(inner[NORTH] | (row_id > 0), face_n, 0.0)
    coef[2] = jnp.where(inner[SOUTH] | (row_id < rows - 1), face_s, 0.0)
    coef[3] = jnp.where(col_id > 0, face_w, 0.0)
    coef[4] = jnp.where(col_id < cols - 1, face_e, 0.0)
    coef[5] = jnp.where(inner[WEST] & (col_id == 0), face_w, 0.0)
    coef[6] = jnp.where(inner[EAST] & (col_id == cols - 1), face_e, 0.0)

    def interior(src, r):
        left, right = src[r, :, 0:BLOCK], src[r, :, BLOCK:cols]
        left_up, right_up = shifted(left, 1), shifted(right, 1)
        left_dn, right_dn = shifted(left, -1), shifted(right, -1)
        west = (left_up, jnp.where(lane == 0, left_up, right_up))
        east = (jnp.where(lane == BLOCK - 1, right_dn, left_dn), right_dn)
        out = []
        for h, centre in enumerate((left, right)):
            at = slice(h * BLOCK, (h + 1) * BLOCK)
            value = coef[0, r : r + 1, at] * centre
            if r < rows - 1:
                value = value - coef[2, r : r + 1, at] * src[r + 1, :, at]
            if r > 0:
                value = value - coef[1, r : r + 1, at] * src[r - 1, :, at]
            value = value - coef[4, r : r + 1, at] * east[h]
            value = value - coef[3, r : r + 1, at] * west[h]
            out.append(value)
        return out

    def spread(halo):
        return [
            jnp.concatenate([shifted(halo[i], -rows * g) for g in range(groups)], axis=0)
            for i in range(2)
        ]

    def with_columns(out, r, halo):
        from_west = shifted(halo[0], -r)
        from_east = shifted(halo[1], -1 - r)
        return [
            out[0] - coef[5, r : r + 1, 0:BLOCK] * from_west,
            out[1] - coef[6, r : r + 1, BLOCK:cols] * from_east,
        ]

    for r in range(rows):
        left, right = interior(forced, r)
        field[r, :, 0:BLOCK] = left
        field[r, :, BLOCK:cols] = right
    for i in range(2):
        from_neighbour(fcol_halo.at[i], FORCED, WEST + i)
    columns = spread(fcol_halo)
    order = [0, rows - 1] + list(range(1, rows - 1))

    def tangent(r):
        out = with_columns([field[r, :, 0:BLOCK], field[r, :, BLOCK:cols]], r, columns)
        place = order.index(r)
        here = slice(place * probe_count, (place + 1) * probe_count)
        for h in range(halves):
            at = slice(h * BLOCK, (h + 1) * BLOCK)
            if r == 0:
                scale = coef[1, 0:1, at] * rows_halo[0, 1:2, at]
                out[h] = out[h] - scale * prow_halo[0, :, at].astype(F32)
            if r == rows - 1:
                scale = coef[2, r : r + 1, at] * rows_halo[1, 1:2, at]
                out[h] = out[h] - scale * prow_halo[1, :, at].astype(F32)
            tcat[h, here, 0:BLOCK] = out[h].astype(BF16)
            tcat[h, here, BLOCK : 2 * BLOCK] = out[h].astype(BF16)

    for r in order[2:]:
        tangent(r)
    advance(0)

    arrived(wall.at[pl.ds(0, n_obs - 1 - relays)], WALL)
    tell_y(0)
    for i in range(n_obs):
        w_high, w_low = split(wall[i, 0:per_dev, :].astype(jnp.int32).astype(F32))
        wcat[i * per_dev : (i + 1) * per_dev, 0:BLOCK] = w_high
        wcat[i * per_dev : (i + 1) * per_dev, BLOCK : 2 * BLOCK] = w_low
    per_row = BLOCK // per_dev
    tails = [wall[i, per_dev : per_dev + 16, :].astype(jnp.int32).astype(F32) for i in range(n_obs)]
    chunks = []
    for c in range(obs_total // BLOCK):
        value = tails[c * per_row]
        for k in range(1, per_row):
            value = jnp.where(lane < k * per_dev, value, tails[c * per_row + k])
        chunks.append(value)
    tail = jnp.concatenate(chunks, axis=1)
    obs_at = tail[0:1]
    prec = (tail[1:2] + tail[2:3] * (1.0 / (PREC_STEPS - 1))) * (1.0 / PREC_STEPS)
    obs_scale = prec * (1.0 / WEIGHT_STEPS**2)
    weights = wcat[...]
    for i in range(2):
        from_neighbour(prow_halo.at[i], FORCED, NORTH + i)
    for r in order[:2]:
        tangent(r)
    for group in (order[:2], order[2:]):
        start = order.index(group[0]) * probe_count
        size = len(group) * probe_count
        for h in range(halves):
            picked = dot(tcat[h, start : start + size, :], weights, NT)
            masked = []
            for k, r in enumerate(group):
                own = (r * slab_columns + o * halves + h).astype(F32)
                scale = jnp.where(obs_at == own, obs_scale, 0.0)
                masked.append(picked[k * probe_count : (k + 1) * probe_count] * scale)
            mis_high, mis_low = split(jnp.concatenate(masked, axis=0))
            both = dot(mis_high, weights, NN)
            low = dot(mis_low, weights[:, 0:BLOCK], NN)
            source = both[:, 0:BLOCK] + (both[:, BLOCK:] + low)
            for k, r in enumerate(group):
                field[r, :, h * BLOCK : (h + 1) * BLOCK] = source[
                    k * probe_count : (k + 1) * probe_count
                ]
        if group[0] == 0:
            for i in range(2):
                to_neighbour(field.at[(rows - 1) * i], srow_halo.at[1 - i], SOURCE, NORTH + i)
    scol[0] = packed_edges(field, True)
    scol[1] = packed_edges(field, False)
    for i in range(2):
        to_neighbour(scol.at[i], scol_halo.at[1 - i], SOURCE, WEST + i)

    advance(1)
    hear_y(0)
    tell_y(1)

    for r in range(rows):
        left, right = interior(field, r)
        forced[r, :, 0:BLOCK] = left
        forced[r, :, BLOCK:cols] = right
    for i in range(2):
        from_neighbour(scol_halo.at[i], SOURCE, WEST + i)
    columns = spread(scol_halo)
    quad = 0.0
    for group in (order[2:], order[:2]):
        if group[0] == 0:
            for i in range(2):
                from_neighbour(srow_halo.at[i], SOURCE, NORTH + i)
        for r in group:
            out = with_columns([forced[r, :, 0:BLOCK], forced[r, :, BLOCK:cols]], r, columns)
            parts = probe_rows(r)
            for h in range(halves):
                at = slice(h * BLOCK, (h + 1) * BLOCK)
                if r == 0:
                    out[h] = out[h] - coef[1, 0:1, at] * srow_halo[0, :, at]
                if r == rows - 1:
                    out[h] = out[h] - coef[2, r : r + 1, at] * srow_halo[1, :, at]
                s_high, s_low = split(tiles[1, r : r + 1, at] * out[h] + PRIOR * parts[h])
                here = slice(r * cols + h * BLOCK, r * cols + (h + 1) * BLOCK)
                xcat[0:probe_count, here] = s_high
                xcat[probe_count : 2 * probe_count, here] = s_low
        if group[0] == 0:
            both = [xcat[:, r * cols : (r + 1) * cols] for r in group]
            for sketch in both:
                quad = quad + dot(sketch, sketch, NT)
        else:
            sketch = xcat[:, group[0] * cols : (group[-1] + 1) * cols]
            quad = dot(sketch, sketch, NT)

    keep_sketch = pltpu.make_async_copy(xcat, xcat_hbm, load_sem.at[0])
    keep_sketch.start()
    pair = quad[0:probe_count] + quad[probe_count:]
    gram = pair + shifted(pair, probe_count)
    half = probe_count // 2
    packed = jnp.where(lane < probe_count, gram[0:half], gram[half:])
    for i in range(2):
        part[i] = packed[i * piece : (i + 1) * piece]

    def total(buf, count):
        values = [buf[i] for i in range(count)]
        while len(values) > 1:
            values = [
                sum(values[i : i + 2][1:], values[i]) for i in range(0, len(values), 2)
            ]
        return values[0]

    send(part.at[1 - core], chip_buf, CHIP, sibling)
    hear_y(1)
    arrived(chip_buf, CHIP)
    here = y * nx + x
    plane_buf[here] = part[core] + chip_buf[...]
    for peer in plane_peers:
        send(plane_buf.at[here], plane_buf.at[here], PLANE, peer)
    advance(2)
    arrived(plane_buf.at[pl.ds(0, nx * ny - 1)], PLANE)
    z_buf[z] = total(plane_buf, nx * ny)
    for peer in z_peers:
        send(z_buf.at[z], z_buf.at[z], ZS, peer)
    arrived(z_buf.at[pl.ds(0, nz - 1)], ZS)
    cells = rows * cols * n_mesh * n_obs
    both_buf[core] = total(z_buf, nz) / cells
    send(both_buf.at[core], both_buf.at[core], BOTH, sibling)
    arrived(both_buf.at[0], BOTH)
    keep_gram = pltpu.make_async_copy(both_buf, gram_hbm, load_sem.at[1])
    keep_gram.start()
    for copy in unsent:
        copy.wait_send()
    for src, at, side in edge_copies:

        @pl.when(inner[side])
        def _():
            whole(src, at).wait_send()

    keep_sketch.wait()
    keep_gram.wait()


def eliminate(work, probe_count):
    sub = lax.broadcasted_iota(jnp.int32, (8, BLOCK), 0)
    lanes = lax.broadcasted_iota(jnp.int32, (8, BLOCK), 1)
    groups = len(work)
    factor = [jnp.zeros((8, BLOCK), F32)] * groups
    inverse = [jnp.zeros((8, BLOCK), F32)] * groups

    def wide(x):
        return jnp.broadcast_to(x, (8, BLOCK))

    for k in range(0, probe_count, PIVOTS):
        g, s = divmod(k, 8)
        span = range(PIVOTS)
        col = [[wide(work[i][:, k + j : k + j + 1]) for i in range(g, groups)] for j in span]
        row = [wide(work[g][s + j : s + j + 1, :]) for j in span]
        local = [[wide(col[j][0][s + i : s + i + 1, :]) for j in range(i + 1)] for i in span]
        lower = [[None] * PIVOTS for _ in span]
        inv, roots = [], []
        for p in range(0, PIVOTS, 2):
            a, b, c = local[p][p], local[p + 1][p], local[p + 1][p + 1]
            det = a * c - b * b
            inv_a, inv_det = 1.0 / a, 1.0 / det
            inv_1 = a * inv_det
            slope = b * inv_a
            inv += [inv_a, inv_1]
            roots += [lax.rsqrt(a), lax.rsqrt(det * inv_a)]
            lower[p + 1][p] = slope
            for i in range(p + 2, PIVOTS):
                u, v = local[i][p], local[i][p + 1]
                lower[i][p] = u * inv_a
                lower[i][p + 1] = (v - slope * u) * inv_1
                for j in range(p + 2, i + 1):
                    t, w = local[j][p], local[j][p + 1]
                    local[i][j] = (
                        local[i][j] - (u * (c * t - b * w) + v * (a * w - b * t)) * inv_det
                    )

        def reduce(v):
            done = []
            for j in span:
                value = v[j]
                for i in range(j):
                    value = value - lower[j][i] * done[i]
                done.append(value)
            return done

        reduced = reduce(row)
        scaled = [v * w for v, w in zip(reduced, inv)]
        for j in span:
            inverse[g] = jnp.where(sub == s + j, reduced[j] * roots[j], inverse[g])
        for i in range(g, groups):
            column = reduce([col[j][i - g] for j in span])
            if not (i == g and s + PIVOTS == 8):
                update = work[i]
                for j in range(0, PIVOTS, 2):
                    update = update - (column[j] * scaled[j] + column[j + 1] * scaled[j + 1])
                work[i] = jnp.where(sub >= s + PIVOTS, update, work[i]) if i == g else update
            for j in span:
                keep = column[j] * roots[j]
                if i == g:
                    keep = jnp.where(sub >= s + j, keep, 0.0)
                factor[i] = jnp.where(lanes == k + j, keep, factor[i])
    return factor, inverse


def basis_kernel(
    gram_hbm, xcat_hbm, rank_hbm, basis_hbm, factor_ref, gram_ref, xcat, rank_ref, out, sem
):
    halves, cells, _ = out.shape
    probe_count = factor_ref.shape[0]
    rows = cells // probe_count
    cols = halves * BLOCK
    piece = gram_ref.shape[1]
    groups = probe_count // 8
    load_gram = pltpu.make_async_copy(gram_hbm, gram_ref, sem.at[0])
    load_gram.start()
    load_sketch = pltpu.make_async_copy(xcat_hbm, xcat, sem.at[1])
    load_sketch.start()
    load_rank = pltpu.make_async_copy(rank_hbm, rank_ref, sem.at[2])
    load_rank.start()
    load_gram.wait()
    sub = lax.broadcasted_iota(jnp.int32, (8, BLOCK), 0)
    lanes = lax.broadcasted_iota(jnp.int32, (8, BLOCK), 1)
    work = []
    for g in range(groups):
        at = 8 * g % piece
        own = gram_ref[8 * g // piece % 2, at : at + 8, :]
        if 8 * g >= 2 * piece:
            own = shifted(own, probe_count)
        unit = jnp.where(lanes == sub + (8 * g + probe_count), 1.0, 0.0)
        work.append(jnp.where(lanes < probe_count, own, unit))
    factor, inverse = eliminate(work, probe_count)
    load_rank.wait()
    rank = rank_ref[0]
    for g in range(groups):
        factor_ref[8 * g : 8 * g + 8, :] = factor[g][:, 0:probe_count]
    lower = jnp.concatenate(
        [
            jnp.where((sub + 8 * g < rank) & (lanes >= probe_count), inverse[g], 0.0)
            for g in range(groups)
        ],
        axis=0,
    )
    lower = lower + shifted(lower, probe_count)
    l_high, l_low = split(lower)
    both = jnp.concatenate([l_high, l_low], axis=0)
    load_sketch.wait()
    stores = []
    for h in range(halves):
        for r in range(rows):
            here = slice(r * cols + h * BLOCK, r * cols + (h + 1) * BLOCK)
            solved = dot(both, xcat[:, here], NN)
            out[h, pl.ds(r, probe_count, stride=rows), :] = (
                solved[0:probe_count] + solved[probe_count:]
            )
        store = pltpu.make_async_copy(
            out.at[h], basis_hbm.at[:, pl.ds(h * BLOCK, BLOCK)], sem.at[3 + h]
        )
        store.start()
        stores.append(store)
    for store in stores:
        store.wait()


def per_device(
    n_mesh, n_obs, nz, probes, velocity, viscosity, friction, obs_block, obs_weight, obs_prec, rank
):
    probe_count, rows, cols = probes.shape
    per_dev = obs_weight.shape[1]
    ny = n_mesh // nz
    piece = probe_count // 4
    dma = pltpu.SemaphoreType.DMA
    vmem = pl.BlockSpec(memory_space=pltpu.VMEM)
    hbm = pl.BlockSpec(memory_space=pltpu.HBM)
    xcat, gram = pl.pallas_call(
        functools.partial(sketch_kernel, n_mesh, n_obs, nz),
        out_shape=(
            jax.ShapeDtypeStruct((2 * probe_count, rows * cols), BF16),
            jax.ShapeDtypeStruct((2, piece, BLOCK), F32),
        ),
        in_specs=[hbm] * 7,
        out_specs=(hbm, hbm),
        scratch_shapes=[
            pltpu.VMEM((probe_count, rows, cols), BF16),
            pltpu.VMEM((rows, cols), F32),
            pltpu.VMEM((1, per_dev), jnp.int32),
            pltpu.VMEM((1, per_dev, BLOCK), F32),
            pltpu.VMEM((1, per_dev), F32),
            pltpu.VMEM((cols // BLOCK, probe_count * rows, BLOCK), F32),
            pltpu.VMEM((rows, probe_count, cols), F32),
            pltpu.VMEM((rows, probe_count, cols), F32),
            pltpu.VMEM((7, rows, cols), F32),
            pltpu.VMEM((2, rows, cols), F32),
            pltpu.VMEM((2, 8, cols), F32),
            pltpu.VMEM((2, 8, cols), F32),
            pltpu.VMEM((2, rows, BLOCK), F32),
            pltpu.VMEM((2, probe_count, cols), BF16),
            pltpu.VMEM((2, probe_count, cols), BF16),
            pltpu.VMEM((2, 8, BLOCK), F32),
            pltpu.VMEM((2, 8, BLOCK), F32),
            pltpu.VMEM((2, probe_count, cols), F32),
            pltpu.VMEM((2, 8, BLOCK), F32),
            pltpu.VMEM((2, 8, BLOCK), F32),
            pltpu.VMEM((16, BLOCK), F32),
            pltpu.VMEM((n_obs, per_dev + 16, BLOCK), jnp.int16),
            pltpu.VMEM((n_obs * per_dev, 2 * BLOCK), BF16),
            pltpu.VMEM((cols // BLOCK, rows * probe_count, 2 * BLOCK), BF16),
            pltpu.VMEM((2 * probe_count, rows * cols), BF16),
            pltpu.VMEM((2, piece, BLOCK), F32),
            pltpu.VMEM((piece, BLOCK), F32),
            pltpu.VMEM((n_obs // 2 * ny, piece, BLOCK), F32),
            pltpu.VMEM((nz, piece, BLOCK), F32),
            pltpu.VMEM((2, piece, BLOCK), F32),
            dma((7,)),
            dma((18,)),
            dma((18,)),
            pltpu.SemaphoreType.REGULAR((3, 2)),
            pltpu.SemaphoreType.REGULAR((2, 2)),
        ],
        compiler_params=pltpu.CompilerParams(collective_id=0, has_side_effects=True),
    )(probes, velocity, viscosity, friction, obs_block, obs_weight, obs_prec)
    basis, factor = pl.pallas_call(
        basis_kernel,
        out_shape=(
            jax.ShapeDtypeStruct((probe_count * rows, cols), F32),
            jax.ShapeDtypeStruct((probe_count, probe_count), F32),
        ),
        in_specs=[hbm, hbm, hbm],
        out_specs=(hbm, vmem),
        scratch_shapes=[
            pltpu.VMEM((2, piece, BLOCK), F32),
            pltpu.VMEM((2 * probe_count, rows * cols), BF16),
            pltpu.SMEM((1,), jnp.int32),
            pltpu.VMEM((cols // BLOCK, probe_count * rows, BLOCK), F32),
            dma((3 + cols // BLOCK,)),
        ],
    )(gram, xcat, rank)
    return basis.reshape(probe_count, rows, cols), factor


def solution(mesh):
    in_specs = (
        P(None, "mesh", "obs"),
        P("mesh", "obs"),
        P("mesh", "obs"),
        P("mesh", "obs"),
        P("mesh", "obs"),
        P("mesh", "obs", None),
        P("mesh", "obs"),
        P(),
    )
    n_mesh, n_obs = mesh.shape["mesh"], mesh.shape["obs"]
    nz = Z_RING if n_mesh % Z_RING == 0 else n_mesh // 2
    return jax.shard_map(
        functools.partial(per_device, n_mesh, n_obs, nz),
        mesh=mesh,
        in_specs=in_specs,
        out_specs=(P(None, "mesh", "obs"), P()),
        check_vma=False,
    )
```

```python
import functools

import jax
import jax.numpy as jnp
from jax import lax
from jax.experimental import pallas as pl
from jax.experimental.pallas import tpu as pltpu
from jax.sharding import PartitionSpec as P

BLOCK = 128
PRIOR = 1.0
Z_RING = 16
NEAR = 1
PIVOTS = 8
WEIGHT_STEPS = 65534.0
PREC_STEPS = 32768.0
MESH = pl.DeviceIdType.MESH
F32 = jnp.float32
BF16 = jnp.bfloat16
NORTH, SOUTH, WEST, EAST = 0, 1, 2, 3
OPPOSITE = (SOUTH, NORTH, EAST, WEST)
NT = (((1,), (1,)), ((), ()))
NN = (((1,), (0,)), ((), ()))


def dot(a, b, dims):
    return lax.dot_general(a, b, dims, preferred_element_type=F32)


def split(x):
    high = x.astype(BF16)
    return high, (x - high.astype(F32)).astype(BF16)


def fixed(x):
    return jnp.floor(x + 0.5).astype(jnp.int32).astype(jnp.int16)


def shifted(x, amount):
    amount %= BLOCK
    return pltpu.roll(x, amount, 1) if amount else x


def sketch_kernel(
    n_mesh,
    n_obs,
    nz,
    probes_hbm,
    vel_hbm,
    visc_hbm,
    fric_hbm,
    block_hbm,
    weight_hbm,
    prec_hbm,
    xcat_hbm,
    gram_hbm,
    probes_ref,
    fric_ref,
    block_ref,
    weight_ref,
    prec_ref,
    probe_pr,
    field,
    forced,
    coef,
    tiles,
    edge_rows,
    rows_halo,
    cols_halo,
    prow,
    prow_halo,
    fcol,
    fcol_halo,
    srow,
    srow_halo,
    scol,
    scol_halo,
    meta,
    wall,
    wcat,
    tcat,
    xcat,
    part,
    chip_buf,
    plane_buf,
    z_buf,
    both_buf,
    load_sem,
    send_sem,
    recv_sem,
    z_token,
    y_token,
):
    ny = n_mesh // nz
    probe_count, rows, cols = probes_ref.shape
    halves = cols // BLOCK
    slab_columns = halves * n_obs
    per_dev = weight_ref.shape[1]
    obs_total = per_dev * n_obs
    piece = part.shape[1]
    nx = n_obs // 2
    groups = probe_count // 8
    WALL, CHIP, PLANE, ZS, BOTH, TILES, FORCED, SOURCE = 0, 1, 2, 3, 4, 5, 9, 13

    m = lax.axis_index("mesh")
    o = lax.axis_index("obs")
    y = m // nz
    z = lax.rem(m, nz)
    x = o // 2
    core = lax.rem(o, 2)
    sibling = {"obs": o + 1 - 2 * core}
    neighbours = (
        {"mesh": lax.rem(m + n_mesh - 1, n_mesh)},
        {"mesh": lax.rem(m + 1, n_mesh)},
        {"obs": lax.rem(o + n_obs - 1, n_obs)},
        {"obs": lax.rem(o + 1, n_obs)},
    )
    obs_peers = [
        {"obs": lax.rem(o + d, n_obs)}
        for d in sorted(range(1, n_obs), key=lambda d: -min(d, n_obs - d))
    ]
    plane_peers = [
        {"mesh": lax.rem(y + dy, ny) * nz + z, "obs": lax.rem(o + 2 * dx, n_obs)}
        for dx, dy in sorted(
            ((dx, dy) for dx in range(nx) for dy in range(ny) if dx or dy),
            key=lambda d: -min(d[0], nx - d[0]) - min(d[1], ny - d[1]),
        )
    ]

    def y_peer(d):
        return {"mesh": lax.rem(y + d, ny) * nz + z}

    def z_peer(d):
        return {"mesh": y * nz + lax.rem(z + d, nz)}

    z_peers = [z_peer(d) for d in sorted(range(1, nz), key=lambda d: -min(d, nz - d))]
    near_z = [z_peer(d) for d in range(1, nz) if min(d, nz - d) <= NEAR]

    names = (probes_hbm, weight_hbm, block_hbm, prec_hbm, visc_hbm, vel_hbm, fric_hbm)
    places = (probes_ref, weight_ref, block_ref, prec_ref, tiles.at[0], tiles.at[1], fric_ref)
    loads = [
        pltpu.make_async_copy(src, dst, load_sem.at[i])
        for i, (src, dst) in enumerate(zip(names, places))
    ]
    barrier = pltpu.get_barrier_semaphore()
    inner = (m > 0, m < n_mesh - 1, o > 0, o < n_obs - 1)
    over_wrap = (inner[NORTH] & (z == 0), inner[SOUTH] & (z == nz - 1))
    partners = obs_peers + [y_peer(d) for d in sorted({1, ny - 1})] + near_z
    for peer in partners:
        pl.semaphore_signal(barrier, inc=1, device_id=peer, device_id_type=MESH)
    for side in (NORTH, SOUTH):

        @pl.when(over_wrap[side])
        def _():
            pl.semaphore_signal(
                barrier, inc=1, device_id=neighbours[side], device_id_type=MESH
            )

    for load in loads:
        load.start()

    rows_in = (rows_halo, prow_halo, srow_halo)
    columns_in = (cols_halo, fcol_halo, scol_halo)
    for side in range(4):

        @pl.when(jnp.logical_not(inner[side]))
        def _():
            for buf in columns_in if side >= WEST else rows_in:
                buf[side % 2] = jnp.zeros(buf.shape[1:], buf.dtype)

    lane = lax.broadcasted_iota(jnp.int32, (1, BLOCK), 1)
    meta[...] = jnp.zeros((16, BLOCK), F32)
    for load in loads[1:4]:
        load.wait()
    wall[o, 0:per_dev, :] = fixed(weight_ref[0] * WEIGHT_STEPS)
    scaled_prec = prec_ref[...] * PREC_STEPS
    coarse = jnp.floor(scaled_prec)
    meta[0:1, 0:per_dev] = block_ref[...].astype(F32)
    meta[1:2, 0:per_dev] = coarse
    meta[2:3, 0:per_dev] = (scaled_prec - coarse) * (PREC_STEPS - 1)
    tail = meta[...]
    wall[o, per_dev : per_dev + 16, :] = fixed(tail + shifted(tail, per_dev))

    loads[0].wait()
    for h in range(halves):
        probe_pr[h] = (
            probes_ref[:, :, h * BLOCK : (h + 1) * BLOCK]
            .astype(F32)
            .reshape(probe_count * rows, BLOCK)
        )
    for load in loads[4:]:
        load.wait()

    def probe_rows(r):
        return [
            probe_pr[h, pl.ds(r, probe_count, stride=rows), :] for h in range(halves)
        ]

    def packed_edges(src, first):
        at = slice(0, BLOCK) if first else slice(cols - BLOCK, cols)
        out = jnp.zeros((8, BLOCK), F32)
        for g in range(groups):
            own = jnp.zeros((8, BLOCK), F32)
            for r in range(rows):
                value = src[r, 8 * g : 8 * g + 8, at]
                own = jnp.where(lane == r, shifted(value, r + (0 if first else 1)), own)
            out = out + shifted(own, rows * g)
        return out

    for r in range(rows):
        parts = probe_rows(r)
        for h in range(halves):
            at = slice(h * BLOCK, (h + 1) * BLOCK)
            forced[r, :, at] = parts[h] * tiles[1, r : r + 1, at]
            if r == 0:
                prow[0, :, at] = parts[h].astype(BF16)
            if r == rows - 1:
                prow[1, :, at] = parts[h].astype(BF16)
    eight = lax.broadcasted_iota(jnp.int32, (8, cols), 0)
    for i, r in enumerate((0, rows - 1)):
        edge_rows[i] = jnp.where(eight == 0, tiles[0, r : r + 1, :], tiles[1, r : r + 1, :])
    fcol[0] = packed_edges(forced, True)
    fcol[1] = packed_edges(forced, False)

    pl.semaphore_wait(
        barrier,
        len(partners) + over_wrap[0].astype(jnp.int32) + over_wrap[1].astype(jnp.int32),
    )

    def send(src, dst, stage, peer):
        pltpu.make_async_remote_copy(
            src_ref=src,
            dst_ref=dst,
            send_sem=send_sem.at[stage],
            recv_sem=recv_sem.at[stage],
            device_id=peer,
            device_id_type=MESH,
        ).start()

    def whole(buf, stage):
        return pltpu.make_async_remote_copy(
            src_ref=buf,
            dst_ref=buf,
            send_sem=send_sem.at[stage],
            recv_sem=recv_sem.at[stage],
            device_id=neighbours[NORTH],
            device_id_type=MESH,
        )

    unsent = []

    def arrived(buf, stage):
        copy = whole(buf, stage)
        unsent.append(copy)
        copy.wait_recv()

    edge_copies = []

    def to_neighbour(src, dst, stage, side):
        there = OPPOSITE[side]

        @pl.when(inner[side])
        def _():
            pltpu.make_async_remote_copy(
                src_ref=src,
                dst_ref=dst,
                send_sem=send_sem.at[stage + side],
                recv_sem=recv_sem.at[stage + there],
                device_id=neighbours[side],
                device_id_type=MESH,
            ).start()

        edge_copies.append((src, stage + side, side))

    def from_neighbour(buf, stage, side):
        @pl.when(inner[side])
        def _():
            whole(buf, stage + side).wait_recv()

    for i in range(2):
        edge = pl.ds(0, BLOCK) if i == 0 else pl.ds(cols - BLOCK, BLOCK)
        to_neighbour(tiles.at[0, :, edge], cols_halo.at[1 - i], TILES, WEST + i)
        to_neighbour(edge_rows.at[i], rows_halo.at[1 - i], TILES, NORTH + i)
    for i in range(2):
        to_neighbour(prow.at[i], prow_halo.at[1 - i], FORCED, NORTH + i)
        to_neighbour(fcol.at[i], fcol_halo.at[1 - i], FORCED, WEST + i)
    for peer in obs_peers:
        send(wall.at[o], wall.at[o], WALL, peer)

    tokens = []
    reach = NEAR
    while 2 * reach <= nz // 2:
        tokens.append(reach)
        reach *= 2

    def tell(level):
        for side, d in enumerate((tokens[level], nz - tokens[level])):
            pl.semaphore_signal(
                z_token.at[level, side], inc=1, device_id=z_peer(d), device_id_type=MESH
            )

    def hear(level):
        for side in range(2):
            pl.semaphore_wait(z_token.at[level, side], 1)

    def advance(level):
        if level < len(tokens):
            hear(level)
            if level + 1 < len(tokens):
                tell(level + 1)

    def tell_y(level):
        for side, d in enumerate((1, ny - 1)):
            pl.semaphore_signal(
                y_token.at[level, side], inc=1, device_id=y_peer(d), device_id_type=MESH
            )

    def hear_y(level):
        for side in range(2):
            pl.semaphore_wait(y_token.at[level, side], 1)

    if tokens:
        tell(0)
    tell_y(0)

    for i in range(2):
        from_neighbour(rows_halo.at[i], TILES, NORTH + i)
        from_neighbour(cols_halo.at[i], TILES, WEST + i)
    row_id = lax.broadcasted_iota(jnp.int32, (rows, cols), 0)
    col_id = lax.broadcasted_iota(jnp.int32, (rows, cols), 1)
    visc = tiles[0]

    def face(side, ghost, shift, axis, edge):
        ghost = jnp.where(inner[side], ghost, 0.0)
        return 0.5 * (visc + jnp.where(edge, ghost, pltpu.roll(visc, shift, axis)))

    from_west, from_east = shifted(cols_halo[0], 1), shifted(cols_halo[1], -1)
    face_n = face(NORTH, rows_halo[0, 0:1, :], 1, 0, row_id == 0)
    face_s = face(SOUTH, rows_halo[1, 0:1, :], rows - 1, 0, row_id == rows - 1)
    face_w = face(WEST, jnp.concatenate([from_west] * halves, axis=1), 1, 1, col_id == 0)
    face_e = face(
        EAST, jnp.concatenate([from_east] * halves, axis=1), cols - 1, 1, col_id == cols - 1
    )
    coef[0] = fric_ref[...] + face_n + face_s + face_w + face_e
    coef[1] = jnp.where(inner[NORTH] | (row_id > 0), face_n, 0.0)
    coef[2] = jnp.where(inner[SOUTH] | (row_id < rows - 1), face_s, 0.0)
    coef[3] = jnp.where(col_id > 0, face_w, 0.0)
    coef[4] = jnp.where(col_id < cols - 1, face_e, 0.0)
    coef[5] = jnp.where(inner[WEST] & (col_id == 0), face_w, 0.0)
    coef[6] = jnp.where(inner[EAST] & (col_id == cols - 1), face_e, 0.0)

    def interior(src, r):
        left, right = src[r, :, 0:BLOCK], src[r, :, BLOCK:cols]
        left_up, right_up = shifted(left, 1), shifted(right, 1)
        left_dn, right_dn = shifted(left, -1), shifted(right, -1)
        west = (left_up, jnp.where(lane == 0, left_up, right_up))
        east = (jnp.where(lane == BLOCK - 1, right_dn, left_dn), right_dn)
        out = []
        for h, centre in enumerate((left, right)):
            at = slice(h * BLOCK, (h + 1) * BLOCK)
            value = coef[0, r : r + 1, at] * centre
            if r < rows - 1:
                value = value - coef[2, r : r + 1, at] * src[r + 1, :, at]
            if r > 0:
                value = value - coef[1, r : r + 1, at] * src[r - 1, :, at]
            value = value - coef[4, r : r + 1, at] * east[h]
            value = value - coef[3, r : r + 1, at] * west[h]
            out.append(value)
        return out

    def spread(halo):
        return [
            jnp.concatenate([shifted(halo[i], -rows * g) for g in range(groups)], axis=0)
            for i in range(2)
        ]

    def with_columns(out, r, halo):
        from_west = shifted(halo[0], -r)
        from_east = shifted(halo[1], -1 - r)
        return [
            out[0] - coef[5, r : r + 1, 0:BLOCK] * from_west,
            out[1] - coef[6, r : r + 1, BLOCK:cols] * from_east,
        ]

    for r in range(rows):
        left, right = interior(forced, r)
        field[r, :, 0:BLOCK] = left
        field[r, :, BLOCK:cols] = right
    for i in range(2):
        from_neighbour(fcol_halo.at[i], FORCED, WEST + i)
    columns = spread(fcol_halo)
    order = [0, rows - 1] + list(range(1, rows - 1))

    def tangent(r):
        out = with_columns([field[r, :, 0:BLOCK], field[r, :, BLOCK:cols]], r, columns)
        place = order.index(r)
        here = slice(place * probe_count, (place + 1) * probe_count)
        for h in range(halves):
            at = slice(h * BLOCK, (h + 1) * BLOCK)
            if r == 0:
                scale = coef[1, 0:1, at] * rows_halo[0, 1:2, at]
                out[h] = out[h] - scale * prow_halo[0, :, at].astype(F32)
            if r == rows - 1:
                scale = coef[2, r : r + 1, at] * rows_halo[1, 1:2, at]
                out[h] = out[h] - scale * prow_halo[1, :, at].astype(F32)
            tcat[h, here, 0:BLOCK] = out[h].astype(BF16)
            tcat[h, here, BLOCK : 2 * BLOCK] = out[h].astype(BF16)

    for r in order[2:]:
        tangent(r)
    advance(0)

    arrived(wall.at[pl.ds(0, n_obs - 1)], WALL)
    for i in range(n_obs):
        w_high, w_low = split(wall[i, 0:per_dev, :].astype(jnp.int32).astype(F32))
        wcat[i * per_dev : (i + 1) * per_dev, 0:BLOCK] = w_high
        wcat[i * per_dev : (i + 1) * per_dev, BLOCK : 2 * BLOCK] = w_low
    per_row = BLOCK // per_dev
    tails = [wall[i, per_dev : per_dev + 16, :].astype(jnp.int32).astype(F32) for i in range(n_obs)]
    chunks = []
    for c in range(obs_total // BLOCK):
        value = tails[c * per_row]
        for k in range(1, per_row):
            value = jnp.where(lane < k * per_dev, value, tails[c * per_row + k])
        chunks.append(value)
    tail = jnp.concatenate(chunks, axis=1)
    obs_at = tail[0:1]
    prec = (tail[1:2] + tail[2:3] * (1.0 / (PREC_STEPS - 1))) * (1.0 / PREC_STEPS)
    obs_scale = prec * (1.0 / WEIGHT_STEPS**2)
    weights = wcat[...]
    for i in range(2):
        from_neighbour(prow_halo.at[i], FORCED, NORTH + i)
    for r in order[:2]:
        tangent(r)
    for group in (order[:2], order[2:]):
        start = order.index(group[0]) * probe_count
        size = len(group) * probe_count
        for h in range(halves):
            picked = dot(tcat[h, start : start + size, :], weights, NT)
            masked = []
            for k, r in enumerate(group):
                own = (r * slab_columns + o * halves + h).astype(F32)
                scale = jnp.where(obs_at == own, obs_scale, 0.0)
                masked.append(picked[k * probe_count : (k + 1) * probe_count] * scale)
            mis_high, mis_low = split(jnp.concatenate(masked, axis=0))
            both = dot(mis_high, weights, NN)
            low = dot(mis_low, weights[:, 0:BLOCK], NN)
            source = both[:, 0:BLOCK] + (both[:, BLOCK:] + low)
            for k, r in enumerate(group):
                field[r, :, h * BLOCK : (h + 1) * BLOCK] = source[
                    k * probe_count : (k + 1) * probe_count
                ]
        if group[0] == 0:
            for i in range(2):
                srow[i] = field[(rows - 1) * i].astype(BF16)
                to_neighbour(srow.at[i], srow_halo.at[1 - i], SOURCE, NORTH + i)
    scol[0] = packed_edges(field, True)
    scol[1] = packed_edges(field, False)
    for i in range(2):
        to_neighbour(scol.at[i], scol_halo.at[1 - i], SOURCE, WEST + i)

    advance(1)
    hear_y(0)
    tell_y(1)

    for r in range(rows):
        left, right = interior(field, r)
        forced[r, :, 0:BLOCK] = left
        forced[r, :, BLOCK:cols] = right
    for i in range(2):
        from_neighbour(scol_halo.at[i], SOURCE, WEST + i)
    columns = spread(scol_halo)
    quad = 0.0
    for group in (order[2:], order[:2]):
        if group[0] == 0:
            for i in range(2):
                from_neighbour(srow_halo.at[i], SOURCE, NORTH + i)
        for r in group:
            out = with_columns([forced[r, :, 0:BLOCK], forced[r, :, BLOCK:cols]], r, columns)
            parts = probe_rows(r)
            for h in range(halves):
                at = slice(h * BLOCK, (h + 1) * BLOCK)
                if r == 0:
                    out[h] = out[h] - coef[1, 0:1, at] * srow_halo[0, :, at].astype(F32)
                if r == rows - 1:
                    out[h] = out[h] - coef[2, r : r + 1, at] * srow_halo[1, :, at].astype(F32)
                s_high, s_low = split(tiles[1, r : r + 1, at] * out[h] + PRIOR * parts[h])
                here = slice(r * cols + h * BLOCK, r * cols + (h + 1) * BLOCK)
                xcat[0:probe_count, here] = s_high
                xcat[probe_count : 2 * probe_count, here] = s_low
        if group[0] == 0:
            both = [xcat[:, r * cols : (r + 1) * cols] for r in group]
            for sketch in both:
                quad = quad + dot(sketch, sketch, NT)
        else:
            sketch = xcat[:, group[0] * cols : (group[-1] + 1) * cols]
            quad = dot(sketch, sketch, NT)

    keep_sketch = pltpu.make_async_copy(xcat, xcat_hbm, load_sem.at[0])
    keep_sketch.start()
    pair = quad[0:probe_count] + quad[probe_count:]
    gram = pair + shifted(pair, probe_count)
    half = probe_count // 2
    packed = jnp.where(lane < probe_count, gram[0:half], gram[half:])
    for i in range(2):
        part[i] = packed[i * piece : (i + 1) * piece]

    def total(buf, count):
        values = [buf[i] for i in range(count)]
        while len(values) > 1:
            values = [
                sum(values[i : i + 2][1:], values[i]) for i in range(0, len(values), 2)
            ]
        return values[0]

    send(part.at[1 - core], chip_buf, CHIP, sibling)
    hear_y(1)
    arrived(chip_buf, CHIP)
    here = y * nx + x
    plane_buf[here] = part[core] + chip_buf[...]
    for peer in plane_peers:
        send(plane_buf.at[here], plane_buf.at[here], PLANE, peer)
    advance(2)
    arrived(plane_buf.at[pl.ds(0, nx * ny - 1)], PLANE)
    z_buf[z] = total(plane_buf, nx * ny)
    for peer in z_peers:
        send(z_buf.at[z], z_buf.at[z], ZS, peer)
    arrived(z_buf.at[pl.ds(0, nz - 1)], ZS)
    cells = rows * cols * n_mesh * n_obs
    both_buf[core] = total(z_buf, nz) / cells
    send(both_buf.at[core], both_buf.at[core], BOTH, sibling)
    arrived(both_buf.at[0], BOTH)
    keep_gram = pltpu.make_async_copy(both_buf, gram_hbm, load_sem.at[1])
    keep_gram.start()
    for copy in unsent:
        copy.wait_send()
    for src, at, side in edge_copies:

        @pl.when(inner[side])
        def _():
            whole(src, at).wait_send()

    keep_sketch.wait()
    keep_gram.wait()


def eliminate(work, probe_count):
    sub = lax.broadcasted_iota(jnp.int32, (8, BLOCK), 0)
    lanes = lax.broadcasted_iota(jnp.int32, (8, BLOCK), 1)
    groups = len(work)
    factor = [jnp.zeros((8, BLOCK), F32)] * groups
    inverse = [jnp.zeros((8, BLOCK), F32)] * groups

    def wide(x):
        return jnp.broadcast_to(x, (8, BLOCK))

    for k in range(0, probe_count, PIVOTS):
        g, s = divmod(k, 8)
        span = range(PIVOTS)
        col = [[wide(work[i][:, k + j : k + j + 1]) for i in range(g, groups)] for j in span]
        row = [wide(work[g][s + j : s + j + 1, :]) for j in span]
        local = [[wide(col[j][0][s + i : s + i + 1, :]) for j in range(i + 1)] for i in span]
        lower = [[None] * PIVOTS for _ in span]
        inv, roots = [], []
        for p in range(0, PIVOTS, 2):
            a, b, c = local[p][p], local[p + 1][p], local[p + 1][p + 1]
            det = a * c - b * b
            inv_a, inv_det = 1.0 / a, 1.0 / det
            inv_1 = a * inv_det
            slope = b * inv_a
            inv += [inv_a, inv_1]
            roots += [lax.rsqrt(a), lax.rsqrt(det * inv_a)]
            lower[p + 1][p] = slope
            for i in range(p + 2, PIVOTS):
                u, v = local[i][p], local[i][p + 1]
                lower[i][p] = u * inv_a
                lower[i][p + 1] = (v - slope * u) * inv_1
                for j in range(p + 2, i + 1):
                    t, w = local[j][p], local[j][p + 1]
                    local[i][j] = (
                        local[i][j] - (u * (c * t - b * w) + v * (a * w - b * t)) * inv_det
                    )

        def reduce(v):
            done = []
            for j in span:
                value = v[j]
                for i in range(j):
                    value = value - lower[j][i] * done[i]
                done.append(value)
            return done

        reduced = reduce(row)
        scaled = [v * w for v, w in zip(reduced, inv)]
        for j in span:
            inverse[g] = jnp.where(sub == s + j, reduced[j] * roots[j], inverse[g])
        for i in range(g, groups):
            column = reduce([col[j][i - g] for j in span])
            if not (i == g and s + PIVOTS == 8):
                update = work[i]
                for j in range(0, PIVOTS, 2):
                    update = update - (column[j] * scaled[j] + column[j + 1] * scaled[j + 1])
                work[i] = jnp.where(sub >= s + PIVOTS, update, work[i]) if i == g else update
            for j in span:
                keep = column[j] * roots[j]
                if i == g:
                    keep = jnp.where(sub >= s + j, keep, 0.0)
                factor[i] = jnp.where(lanes == k + j, keep, factor[i])
    return factor, inverse


def basis_kernel(
    gram_hbm, xcat_hbm, rank_hbm, basis_hbm, factor_ref, gram_ref, xcat, rank_ref, out, sem
):
    halves, cells, _ = out.shape
    probe_count = factor_ref.shape[0]
    rows = cells // probe_count
    cols = halves * BLOCK
    piece = gram_ref.shape[1]
    groups = probe_count // 8
    load_gram = pltpu.make_async_copy(gram_hbm, gram_ref, sem.at[0])
    load_gram.start()
    load_sketch = pltpu.make_async_copy(xcat_hbm, xcat, sem.at[1])
    load_sketch.start()
    load_rank = pltpu.make_async_copy(rank_hbm, rank_ref, sem.at[2])
    load_rank.start()
    load_gram.wait()
    sub = lax.broadcasted_iota(jnp.int32, (8, BLOCK), 0)
    lanes = lax.broadcasted_iota(jnp.int32, (8, BLOCK), 1)
    work = []
    for g in range(groups):
        at = 8 * g % piece
        own = gram_ref[8 * g // piece % 2, at : at + 8, :]
        if 8 * g >= 2 * piece:
            own = shifted(own, probe_count)
        unit = jnp.where(lanes == sub + (8 * g + probe_count), 1.0, 0.0)
        work.append(jnp.where(lanes < probe_count, own, unit))
    factor, inverse = eliminate(work, probe_count)
    load_rank.wait()
    rank = rank_ref[0]
    for g in range(groups):
        factor_ref[8 * g : 8 * g + 8, :] = factor[g][:, 0:probe_count]
    lower = jnp.concatenate(
        [
            jnp.where((sub + 8 * g < rank) & (lanes >= probe_count), inverse[g], 0.0)
            for g in range(groups)
        ],
        axis=0,
    )
    lower = lower + shifted(lower, probe_count)
    l_high, l_low = split(lower)
    both = jnp.concatenate([l_high, l_low], axis=0)
    load_sketch.wait()
    stores = []
    for h in range(halves):
        for r in range(rows):
            here = slice(r * cols + h * BLOCK, r * cols + (h + 1) * BLOCK)
            solved = dot(both, xcat[:, here], NN)
            out[h, pl.ds(r, probe_count, stride=rows), :] = (
                solved[0:probe_count] + solved[probe_count:]
            )
        store = pltpu.make_async_copy(
            out.at[h], basis_hbm.at[:, pl.ds(h * BLOCK, BLOCK)], sem.at[3 + h]
        )
        store.start()
        stores.append(store)
    for store in stores:
        store.wait()


def per_device(
    n_mesh, n_obs, nz, probes, velocity, viscosity, friction, obs_block, obs_weight, obs_prec, rank
):
    probe_count, rows, cols = probes.shape
    per_dev = obs_weight.shape[1]
    ny = n_mesh // nz
    piece = probe_count // 4
    dma = pltpu.SemaphoreType.DMA
    vmem = pl.BlockSpec(memory_space=pltpu.VMEM)
    hbm = pl.BlockSpec(memory_space=pltpu.HBM)
    xcat, gram = pl.pallas_call(
        functools.partial(sketch_kernel, n_mesh, n_obs, nz),
        out_shape=(
            jax.ShapeDtypeStruct((2 * probe_count, rows * cols), BF16),
            jax.ShapeDtypeStruct((2, piece, BLOCK), F32),
        ),
        in_specs=[hbm] * 7,
        out_specs=(hbm, hbm),
        scratch_shapes=[
            pltpu.VMEM((probe_count, rows, cols), BF16),
            pltpu.VMEM((rows, cols), F32),
            pltpu.VMEM((1, per_dev), jnp.int32),
            pltpu.VMEM((1, per_dev, BLOCK), F32),
            pltpu.VMEM((1, per_dev), F32),
            pltpu.VMEM((cols // BLOCK, probe_count * rows, BLOCK), F32),
            pltpu.VMEM((rows, probe_count, cols), F32),
            pltpu.VMEM((rows, probe_count, cols), F32),
            pltpu.VMEM((7, rows, cols), F32),
            pltpu.VMEM((2, rows, cols), F32),
            pltpu.VMEM((2, 8, cols), F32),
            pltpu.VMEM((2, 8, cols), F32),
            pltpu.VMEM((2, rows, BLOCK), F32),
            pltpu.VMEM((2, probe_count, cols), BF16),
            pltpu.VMEM((2, probe_count, cols), BF16),
            pltpu.VMEM((2, 8, BLOCK), F32),
            pltpu.VMEM((2, 8, BLOCK), F32),
            pltpu.VMEM((2, probe_count, cols), BF16),
            pltpu.VMEM((2, probe_count, cols), BF16),
            pltpu.VMEM((2, 8, BLOCK), F32),
            pltpu.VMEM((2, 8, BLOCK), F32),
            pltpu.VMEM((16, BLOCK), F32),
            pltpu.VMEM((n_obs, per_dev + 16, BLOCK), jnp.int16),
            pltpu.VMEM((n_obs * per_dev, 2 * BLOCK), BF16),
            pltpu.VMEM((cols // BLOCK, rows * probe_count, 2 * BLOCK), BF16),
            pltpu.VMEM((2 * probe_count, rows * cols), BF16),
            pltpu.VMEM((2, piece, BLOCK), F32),
            pltpu.VMEM((piece, BLOCK), F32),
            pltpu.VMEM((n_obs // 2 * ny, piece, BLOCK), F32),
            pltpu.VMEM((nz, piece, BLOCK), F32),
            pltpu.VMEM((2, piece, BLOCK), F32),
            dma((7,)),
            dma((17,)),
            dma((17,)),
            pltpu.SemaphoreType.REGULAR((3, 2)),
            pltpu.SemaphoreType.REGULAR((2, 2)),
        ],
        compiler_params=pltpu.CompilerParams(collective_id=0, has_side_effects=True),
    )(probes, velocity, viscosity, friction, obs_block, obs_weight, obs_prec)
    basis, factor = pl.pallas_call(
        basis_kernel,
        out_shape=(
            jax.ShapeDtypeStruct((probe_count * rows, cols), F32),
            jax.ShapeDtypeStruct((probe_count, probe_count), F32),
        ),
        in_specs=[hbm, hbm, hbm],
        out_specs=(hbm, vmem),
        scratch_shapes=[
            pltpu.VMEM((2, piece, BLOCK), F32),
            pltpu.VMEM((2 * probe_count, rows * cols), BF16),
            pltpu.SMEM((1,), jnp.int32),
            pltpu.VMEM((cols // BLOCK, probe_count * rows, BLOCK), F32),
            dma((3 + cols // BLOCK,)),
        ],
    )(gram, xcat, rank)
    return basis.reshape(probe_count, rows, cols), factor


def solution(mesh):
    in_specs = (
        P(None, "mesh", "obs"),
        P("mesh", "obs"),
        P("mesh", "obs"),
        P("mesh", "obs"),
        P("mesh", "obs"),
        P("mesh", "obs", None),
        P("mesh", "obs"),
        P(),
    )
    n_mesh, n_obs = mesh.shape["mesh"], mesh.shape["obs"]
    nz = Z_RING if n_mesh % Z_RING == 0 else n_mesh // 2
    return jax.shard_map(
        functools.partial(per_device, n_mesh, n_obs, nz),
        mesh=mesh,
        in_specs=in_specs,
        out_specs=(P(None, "mesh", "obs"), P()),
        check_vma=False,
    )
```

```python
import functools

import jax
import jax.numpy as jnp
from jax import lax
from jax.experimental import pallas as pl
from jax.experimental.pallas import tpu as pltpu
from jax.sharding import PartitionSpec as P

BLOCK = 128
PRIOR = 1.0
Z_RING = 16
NEAR = 1
PIVOTS = 8
WEIGHT_STEPS = 65534.0
PREC_STEPS = 32768.0
MESH = pl.DeviceIdType.MESH
F32 = jnp.float32
BF16 = jnp.bfloat16
NORTH, SOUTH, WEST, EAST = 0, 1, 2, 3
OPPOSITE = (SOUTH, NORTH, EAST, WEST)
NT = (((1,), (1,)), ((), ()))
NN = (((1,), (0,)), ((), ()))


def dot(a, b, dims):
    return lax.dot_general(a, b, dims, preferred_element_type=F32)


def split(x):
    high = x.astype(BF16)
    return high, (x - high.astype(F32)).astype(BF16)


def fixed(x):
    return jnp.floor(x + 0.5).astype(jnp.int32).astype(jnp.int16)


def shifted(x, amount):
    amount %= BLOCK
    return pltpu.roll(x, amount, 1) if amount else x


def sketch_kernel(
    n_mesh,
    n_obs,
    nz,
    probes_hbm,
    vel_hbm,
    visc_hbm,
    fric_hbm,
    block_hbm,
    weight_hbm,
    prec_hbm,
    xcat_hbm,
    gram_hbm,
    probes_ref,
    fric_ref,
    block_ref,
    weight_ref,
    prec_ref,
    probe_pr,
    field,
    forced,
    coef,
    tiles,
    edge_rows,
    rows_halo,
    cols_halo,
    prow,
    prow_halo,
    fcol,
    fcol_halo,
    srow,
    srow_halo,
    scol,
    scol_halo,
    meta,
    wall,
    wcat,
    tcat,
    xcat,
    part,
    chip_buf,
    plane_buf,
    z_buf,
    both_buf,
    load_sem,
    send_sem,
    recv_sem,
    z_token,
    y_token,
):
    ny = n_mesh // nz
    probe_count, rows, cols = probes_ref.shape
    halves = cols // BLOCK
    slab_columns = halves * n_obs
    per_dev = weight_ref.shape[1]
    obs_total = per_dev * n_obs
    piece = part.shape[1]
    nx = n_obs // 2
    groups = probe_count // 8
    WALL, CHIP, PLANE, ZS, BOTH, TILES, FORCED, SOURCE = 0, 1, 2, 3, 4, 5, 9, 13

    m = lax.axis_index("mesh")
    o = lax.axis_index("obs")
    y = m // nz
    z = lax.rem(m, nz)
    x = o // 2
    core = lax.rem(o, 2)
    sibling = {"obs": o + 1 - 2 * core}
    neighbours = (
        {"mesh": lax.rem(m + n_mesh - 1, n_mesh)},
        {"mesh": lax.rem(m + 1, n_mesh)},
        {"obs": lax.rem(o + n_obs - 1, n_obs)},
        {"obs": lax.rem(o + 1, n_obs)},
    )
    obs_peers = [
        {"obs": lax.rem(o + d, n_obs)}
        for d in sorted(range(1, n_obs), key=lambda d: -min(d, n_obs - d))
    ]
    plane_peers = [
        {"mesh": lax.rem(y + dy, ny) * nz + z, "obs": lax.rem(o + 2 * dx, n_obs)}
        for dx, dy in sorted(
            ((dx, dy) for dx in range(nx) for dy in range(ny) if dx or dy),
            key=lambda d: -min(d[0], nx - d[0]) - min(d[1], ny - d[1]),
        )
    ]

    def y_peer(d):
        return {"mesh": lax.rem(y + d, ny) * nz + z}

    def z_peer(d):
        return {"mesh": y * nz + lax.rem(z + d, nz)}

    z_peers = [z_peer(d) for d in sorted(range(1, nz), key=lambda d: -min(d, nz - d))]
    near_z = [z_peer(d) for d in range(1, nz) if min(d, nz - d) <= NEAR]

    names = (probes_hbm, weight_hbm, block_hbm, prec_hbm, visc_hbm, vel_hbm, fric_hbm)
    places = (probes_ref, weight_ref, block_ref, prec_ref, tiles.at[0], tiles.at[1], fric_ref)
    loads = [
        pltpu.make_async_copy(src, dst, load_sem.at[i])
        for i, (src, dst) in enumerate(zip(names, places))
    ]
    barrier = pltpu.get_barrier_semaphore()
    inner = (m > 0, m < n_mesh - 1, o > 0, o < n_obs - 1)
    over_wrap = (inner[NORTH] & (z == 0), inner[SOUTH] & (z == nz - 1))
    partners = obs_peers + [y_peer(d) for d in sorted({1, ny - 1})] + near_z
    for peer in partners:
        pl.semaphore_signal(barrier, inc=1, device_id=peer, device_id_type=MESH)
    for side in (NORTH, SOUTH):

        @pl.when(over_wrap[side])
        def _():
            pl.semaphore_signal(
                barrier, inc=1, device_id=neighbours[side], device_id_type=MESH
            )

    for load in loads:
        load.start()

    rows_in = (rows_halo, prow_halo, srow_halo)
    columns_in = (cols_halo, fcol_halo, scol_halo)
    for side in range(4):

        @pl.when(jnp.logical_not(inner[side]))
        def _():
            for buf in columns_in if side >= WEST else rows_in:
                buf[side % 2] = jnp.zeros(buf.shape[1:], buf.dtype)

    lane = lax.broadcasted_iota(jnp.int32, (1, BLOCK), 1)
    meta[...] = jnp.zeros((16, BLOCK), F32)
    for load in loads[1:4]:
        load.wait()
    wall[o, 0:per_dev, :] = fixed(weight_ref[0] * WEIGHT_STEPS)
    scaled_prec = prec_ref[...] * PREC_STEPS
    coarse = jnp.floor(scaled_prec)
    meta[0:1, 0:per_dev] = block_ref[...].astype(F32)
    meta[1:2, 0:per_dev] = coarse
    meta[2:3, 0:per_dev] = (scaled_prec - coarse) * (PREC_STEPS - 1)
    tail = meta[...]
    wall[o, per_dev : per_dev + 16, :] = fixed(tail + shifted(tail, per_dev))

    loads[0].wait()
    for h in range(halves):
        probe_pr[h] = (
            probes_ref[:, :, h * BLOCK : (h + 1) * BLOCK]
            .astype(F32)
            .reshape(probe_count * rows, BLOCK)
        )
    for load in loads[4:]:
        load.wait()

    def probe_rows(r):
        return [
            probe_pr[h, pl.ds(r, probe_count, stride=rows), :] for h in range(halves)
        ]

    def packed_edges(src, first):
        at = slice(0, BLOCK) if first else slice(cols - BLOCK, cols)
        out = jnp.zeros((8, BLOCK), F32)
        for g in range(groups):
            own = jnp.zeros((8, BLOCK), F32)
            for r in range(rows):
                value = src[r, 8 * g : 8 * g + 8, at]
                own = jnp.where(lane == r, shifted(value, r + (0 if first else 1)), own)
            out = out + shifted(own, rows * g)
        return out

    for r in range(rows):
        parts = probe_rows(r)
        for h in range(halves):
            at = slice(h * BLOCK, (h + 1) * BLOCK)
            forced[r, :, at] = parts[h] * tiles[1, r : r + 1, at]
            if r == 0:
                prow[0, :, at] = parts[h].astype(BF16)
            if r == rows - 1:
                prow[1, :, at] = parts[h].astype(BF16)
    eight = lax.broadcasted_iota(jnp.int32, (8, cols), 0)
    for i, r in enumerate((0, rows - 1)):
        edge_rows[i] = jnp.where(eight == 0, tiles[0, r : r + 1, :], tiles[1, r : r + 1, :])
    fcol[0] = packed_edges(forced, True)
    fcol[1] = packed_edges(forced, False)

    pl.semaphore_wait(
        barrier,
        len(partners) + over_wrap[0].astype(jnp.int32) + over_wrap[1].astype(jnp.int32),
    )

    def send(src, dst, stage, peer):
        pltpu.make_async_remote_copy(
            src_ref=src,
            dst_ref=dst,
            send_sem=send_sem.at[stage],
            recv_sem=recv_sem.at[stage],
            device_id=peer,
            device_id_type=MESH,
        ).start()

    def whole(buf, stage):
        return pltpu.make_async_remote_copy(
            src_ref=buf,
            dst_ref=buf,
            send_sem=send_sem.at[stage],
            recv_sem=recv_sem.at[stage],
            device_id=neighbours[NORTH],
            device_id_type=MESH,
        )

    unsent = []

    def arrived(buf, stage):
        copy = whole(buf, stage)
        unsent.append(copy)
        copy.wait_recv()

    edge_copies = []

    def to_neighbour(src, dst, stage, side):
        there = OPPOSITE[side]

        @pl.when(inner[side])
        def _():
            pltpu.make_async_remote_copy(
                src_ref=src,
                dst_ref=dst,
                send_sem=send_sem.at[stage + side],
                recv_sem=recv_sem.at[stage + there],
                device_id=neighbours[side],
                device_id_type=MESH,
            ).start()

        edge_copies.append((src, stage + side, side))

    def from_neighbour(buf, stage, side):
        @pl.when(inner[side])
        def _():
            whole(buf, stage + side).wait_recv()

    for i in range(2):
        edge = pl.ds(0, BLOCK) if i == 0 else pl.ds(cols - BLOCK, BLOCK)
        to_neighbour(tiles.at[0, :, edge], cols_halo.at[1 - i], TILES, WEST + i)
        to_neighbour(edge_rows.at[i], rows_halo.at[1 - i], TILES, NORTH + i)
    for i in range(2):
        to_neighbour(fcol.at[i], fcol_halo.at[1 - i], FORCED, WEST + i)
    for peer in obs_peers:
        send(wall.at[o], wall.at[o], WALL, peer)
    for i in range(2):
        to_neighbour(prow.at[i], prow_halo.at[1 - i], FORCED, NORTH + i)

    tokens = []
    reach = NEAR
    while 2 * reach <= nz // 2:
        tokens.append(reach)
        reach *= 2

    def tell(level):
        for side, d in enumerate((tokens[level], nz - tokens[level])):
            pl.semaphore_signal(
                z_token.at[level, side], inc=1, device_id=z_peer(d), device_id_type=MESH
            )

    def hear(level):
        for side in range(2):
            pl.semaphore_wait(z_token.at[level, side], 1)

    def advance(level):
        if level < len(tokens):
            hear(level)
            if level + 1 < len(tokens):
                tell(level + 1)

    def tell_y(level):
        for side, d in enumerate((1, ny - 1)):
            pl.semaphore_signal(
                y_token.at[level, side], inc=1, device_id=y_peer(d), device_id_type=MESH
            )

    def hear_y(level):
        for side in range(2):
            pl.semaphore_wait(y_token.at[level, side], 1)

    if tokens:
        tell(0)
    tell_y(0)

    for i in range(2):
        from_neighbour(rows_halo.at[i], TILES, NORTH + i)
        from_neighbour(cols_halo.at[i], TILES, WEST + i)
    row_id = lax.broadcasted_iota(jnp.int32, (rows, cols), 0)
    col_id = lax.broadcasted_iota(jnp.int32, (rows, cols), 1)
    visc = tiles[0]

    def face(side, ghost, shift, axis, edge):
        ghost = jnp.where(inner[side], ghost, 0.0)
        return 0.5 * (visc + jnp.where(edge, ghost, pltpu.roll(visc, shift, axis)))

    from_west, from_east = shifted(cols_halo[0], 1), shifted(cols_halo[1], -1)
    face_n = face(NORTH, rows_halo[0, 0:1, :], 1, 0, row_id == 0)
    face_s = face(SOUTH, rows_halo[1, 0:1, :], rows - 1, 0, row_id == rows - 1)
    face_w = face(WEST, jnp.concatenate([from_west] * halves, axis=1), 1, 1, col_id == 0)
    face_e = face(
        EAST, jnp.concatenate([from_east] * halves, axis=1), cols - 1, 1, col_id == cols - 1
    )
    coef[0] = fric_ref[...] + face_n + face_s + face_w + face_e
    coef[1] = jnp.where(inner[NORTH] | (row_id > 0), face_n, 0.0)
    coef[2] = jnp.where(inner[SOUTH] | (row_id < rows - 1), face_s, 0.0)
    coef[3] = jnp.where(col_id > 0, face_w, 0.0)
    coef[4] = jnp.where(col_id < cols - 1, face_e, 0.0)
    coef[5] = jnp.where(inner[WEST] & (col_id == 0), face_w, 0.0)
    coef[6] = jnp.where(inner[EAST] & (col_id == cols - 1), face_e, 0.0)

    def interior(src, r):
        left, right = src[r, :, 0:BLOCK], src[r, :, BLOCK:cols]
        left_up, right_up = shifted(left, 1), shifted(right, 1)
        left_dn, right_dn = shifted(left, -1), shifted(right, -1)
        west = (left_up, jnp.where(lane == 0, left_up, right_up))
        east = (jnp.where(lane == BLOCK - 1, right_dn, left_dn), right_dn)
        out = []
        for h, centre in enumerate((left, right)):
            at = slice(h * BLOCK, (h + 1) * BLOCK)
            value = coef[0, r : r + 1, at] * centre
            if r < rows - 1:
                value = value - coef[2, r : r + 1, at] * src[r + 1, :, at]
            if r > 0:
                value = value - coef[1, r : r + 1, at] * src[r - 1, :, at]
            value = value - coef[4, r : r + 1, at] * east[h]
            value = value - coef[3, r : r + 1, at] * west[h]
            out.append(value)
        return out

    def spread(halo):
        return [
            jnp.concatenate([shifted(halo[i], -rows * g) for g in range(groups)], axis=0)
            for i in range(2)
        ]

    def with_columns(out, r, halo):
        from_west = shifted(halo[0], -r)
        from_east = shifted(halo[1], -1 - r)
        return [
            out[0] - coef[5, r : r + 1, 0:BLOCK] * from_west,
            out[1] - coef[6, r : r + 1, BLOCK:cols] * from_east,
        ]

    for r in range(rows):
        left, right = interior(forced, r)
        field[r, :, 0:BLOCK] = left
        field[r, :, BLOCK:cols] = right
    for i in range(2):
        from_neighbour(fcol_halo.at[i], FORCED, WEST + i)
    columns = spread(fcol_halo)
    order = [0, rows - 1] + list(range(1, rows - 1))

    def tangent(r):
        out = with_columns([field[r, :, 0:BLOCK], field[r, :, BLOCK:cols]], r, columns)
        place = order.index(r)
        here = slice(place * probe_count, (place + 1) * probe_count)
        for h in range(halves):
            at = slice(h * BLOCK, (h + 1) * BLOCK)
            if r == 0:
                scale = coef[1, 0:1, at] * rows_halo[0, 1:2, at]
                out[h] = out[h] - scale * prow_halo[0, :, at].astype(F32)
            if r == rows - 1:
                scale = coef[2, r : r + 1, at] * rows_halo[1, 1:2, at]
                out[h] = out[h] - scale * prow_halo[1, :, at].astype(F32)
            tcat[h, here, 0:BLOCK] = out[h].astype(BF16)
            tcat[h, here, BLOCK : 2 * BLOCK] = out[h].astype(BF16)

    for r in order[2:]:
        tangent(r)
    advance(0)

    arrived(wall.at[pl.ds(0, n_obs - 1)], WALL)
    for i in range(n_obs):
        w_high, w_low = split(wall[i, 0:per_dev, :].astype(jnp.int32).astype(F32))
        wcat[i * per_dev : (i + 1) * per_dev, 0:BLOCK] = w_high
        wcat[i * per_dev : (i + 1) * per_dev, BLOCK : 2 * BLOCK] = w_low
    per_row = BLOCK // per_dev
    tails = [wall[i, per_dev : per_dev + 16, :].astype(jnp.int32).astype(F32) for i in range(n_obs)]
    chunks = []
    for c in range(obs_total // BLOCK):
        value = tails[c * per_row]
        for k in range(1, per_row):
            value = jnp.where(lane < k * per_dev, value, tails[c * per_row + k])
        chunks.append(value)
    tail = jnp.concatenate(chunks, axis=1)
    obs_at = tail[0:1]
    prec = (tail[1:2] + tail[2:3] * (1.0 / (PREC_STEPS - 1))) * (1.0 / PREC_STEPS)
    obs_scale = prec * (1.0 / WEIGHT_STEPS**2)
    weights = wcat[...]
    for i in range(2):
        from_neighbour(prow_halo.at[i], FORCED, NORTH + i)
    for r in order[:2]:
        tangent(r)
    for group in (order[:2], order[2:]):
        start = order.index(group[0]) * probe_count
        size = len(group) * probe_count
        for h in range(halves):
            picked = dot(tcat[h, start : start + size, :], weights, NT)
            masked = []
            for k, r in enumerate(group):
                own = (r * slab_columns + o * halves + h).astype(F32)
                scale = jnp.where(obs_at == own, obs_scale, 0.0)
                masked.append(picked[k * probe_count : (k + 1) * probe_count] * scale)
            mis_high, mis_low = split(jnp.concatenate(masked, axis=0))
            both = dot(mis_high, weights, NN)
            low = dot(mis_low, weights[:, 0:BLOCK], NN)
            source = both[:, 0:BLOCK] + (both[:, BLOCK:] + low)
            for k, r in enumerate(group):
                field[r, :, h * BLOCK : (h + 1) * BLOCK] = source[
                    k * probe_count : (k + 1) * probe_count
                ]
        if group[0] == 0:
            for i in range(2):
                srow[i] = field[(rows - 1) * i].astype(BF16)
                to_neighbour(srow.at[i], srow_halo.at[1 - i], SOURCE, NORTH + i)
    scol[0] = packed_edges(field, True)
    scol[1] = packed_edges(field, False)
    for i in range(2):
        to_neighbour(scol.at[i], scol_halo.at[1 - i], SOURCE, WEST + i)

    advance(1)
    hear_y(0)
    tell_y(1)

    for r in range(rows):
        left, right = interior(field, r)
        forced[r, :, 0:BLOCK] = left
        forced[r, :, BLOCK:cols] = right
    for i in range(2):
        from_neighbour(scol_halo.at[i], SOURCE, WEST + i)
    columns = spread(scol_halo)
    quad = 0.0
    for group in (order[2:], order[:2]):
        if group[0] == 0:
            for i in range(2):
                from_neighbour(srow_halo.at[i], SOURCE, NORTH + i)
        for r in group:
            out = with_columns([forced[r, :, 0:BLOCK], forced[r, :, BLOCK:cols]], r, columns)
            parts = probe_rows(r)
            for h in range(halves):
                at = slice(h * BLOCK, (h + 1) * BLOCK)
                if r == 0:
                    out[h] = out[h] - coef[1, 0:1, at] * srow_halo[0, :, at].astype(F32)
                if r == rows - 1:
                    out[h] = out[h] - coef[2, r : r + 1, at] * srow_halo[1, :, at].astype(F32)
                s_high, s_low = split(tiles[1, r : r + 1, at] * out[h] + PRIOR * parts[h])
                here = slice(r * cols + h * BLOCK, r * cols + (h + 1) * BLOCK)
                xcat[0:probe_count, here] = s_high
                xcat[probe_count : 2 * probe_count, here] = s_low
        if group[0] == 0:
            both = [xcat[:, r * cols : (r + 1) * cols] for r in group]
            for sketch in both:
                quad = quad + dot(sketch, sketch, NT)
        else:
            sketch = xcat[:, group[0] * cols : (group[-1] + 1) * cols]
            quad = dot(sketch, sketch, NT)

    keep_sketch = pltpu.make_async_copy(xcat, xcat_hbm, load_sem.at[0])
    keep_sketch.start()
    pair = quad[0:probe_count] + quad[probe_count:]
    gram = pair + shifted(pair, probe_count)
    half = probe_count // 2
    packed = jnp.where(lane < probe_count, gram[0:half], gram[half:])
    for i in range(2):
        part[i] = packed[i * piece : (i + 1) * piece]

    def total(buf, count):
        values = [buf[i] for i in range(count)]
        while len(values) > 1:
            values = [
                sum(values[i : i + 2][1:], values[i]) for i in range(0, len(values), 2)
            ]
        return values[0]

    send(part.at[1 - core], chip_buf, CHIP, sibling)
    hear_y(1)
    arrived(chip_buf, CHIP)
    here = y * nx + x
    plane_buf[here] = part[core] + chip_buf[...]
    for peer in plane_peers:
        send(plane_buf.at[here], plane_buf.at[here], PLANE, peer)
    advance(2)
    arrived(plane_buf.at[pl.ds(0, nx * ny - 1)], PLANE)
    z_buf[z] = total(plane_buf, nx * ny)
    for peer in z_peers:
        send(z_buf.at[z], z_buf.at[z], ZS, peer)
    arrived(z_buf.at[pl.ds(0, nz - 1)], ZS)
    cells = rows * cols * n_mesh * n_obs
    both_buf[core] = total(z_buf, nz) / cells
    send(both_buf.at[core], both_buf.at[core], BOTH, sibling)
    arrived(both_buf.at[0], BOTH)
    keep_gram = pltpu.make_async_copy(both_buf, gram_hbm, load_sem.at[1])
    keep_gram.start()
    for copy in unsent:
        copy.wait_send()
    for src, at, side in edge_copies:

        @pl.when(inner[side])
        def _():
            whole(src, at).wait_send()

    keep_sketch.wait()
    keep_gram.wait()


def eliminate(work, probe_count):
    sub = lax.broadcasted_iota(jnp.int32, (8, BLOCK), 0)
    lanes = lax.broadcasted_iota(jnp.int32, (8, BLOCK), 1)
    groups = len(work)
    factor = [jnp.zeros((8, BLOCK), F32)] * groups
    inverse = [jnp.zeros((8, BLOCK), F32)] * groups

    def wide(x):
        return jnp.broadcast_to(x, (8, BLOCK))

    for k in range(0, probe_count, PIVOTS):
        g, s = divmod(k, 8)
        span = range(PIVOTS)
        col = [[wide(work[i][:, k + j : k + j + 1]) for i in range(g, groups)] for j in span]
        row = [wide(work[g][s + j : s + j + 1, :]) for j in span]
        local = [[wide(col[j][0][s + i : s + i + 1, :]) for j in range(i + 1)] for i in span]
        lower = [[None] * PIVOTS for _ in span]
        inv, roots = [], []
        for p in range(0, PIVOTS, 2):
            a, b, c = local[p][p], local[p + 1][p], local[p + 1][p + 1]
            det = a * c - b * b
            inv_a, inv_det = 1.0 / a, 1.0 / det
            inv_1 = a * inv_det
            slope = b * inv_a
            inv += [inv_a, inv_1]
            roots += [lax.rsqrt(a), lax.rsqrt(det * inv_a)]
            lower[p + 1][p] = slope
            for i in range(p + 2, PIVOTS):
                u, v = local[i][p], local[i][p + 1]
                lower[i][p] = u * inv_a
                lower[i][p + 1] = (v - slope * u) * inv_1
                for j in range(p + 2, i + 1):
                    t, w = local[j][p], local[j][p + 1]
                    local[i][j] = (
                        local[i][j] - (u * (c * t - b * w) + v * (a * w - b * t)) * inv_det
                    )

        def reduce(v):
            done = []
            for j in span:
                value = v[j]
                for i in range(j):
                    value = value - lower[j][i] * done[i]
                done.append(value)
            return done

        reduced = reduce(row)
        scaled = [v * w for v, w in zip(reduced, inv)]
        for j in span:
            inverse[g] = jnp.where(sub == s + j, reduced[j] * roots[j], inverse[g])
        for i in range(g, groups):
            column = reduce([col[j][i - g] for j in span])
            if not (i == g and s + PIVOTS == 8):
                update = work[i]
                for j in range(0, PIVOTS, 2):
                    update = update - (column[j] * scaled[j] + column[j + 1] * scaled[j + 1])
                work[i] = jnp.where(sub >= s + PIVOTS, update, work[i]) if i == g else update
            for j in span:
                keep = column[j] * roots[j]
                if i == g:
                    keep = jnp.where(sub >= s + j, keep, 0.0)
                factor[i] = jnp.where(lanes == k + j, keep, factor[i])
    return factor, inverse


def basis_kernel(
    gram_hbm, xcat_hbm, rank_hbm, basis_hbm, factor_ref, gram_ref, xcat, rank_ref, out, sem
):
    halves, cells, _ = out.shape
    probe_count = factor_ref.shape[0]
    rows = cells // probe_count
    cols = halves * BLOCK
    piece = gram_ref.shape[1]
    groups = probe_count // 8
    load_gram = pltpu.make_async_copy(gram_hbm, gram_ref, sem.at[0])
    load_gram.start()
    load_sketch = pltpu.make_async_copy(xcat_hbm, xcat, sem.at[1])
    load_sketch.start()
    load_rank = pltpu.make_async_copy(rank_hbm, rank_ref, sem.at[2])
    load_rank.start()
    load_gram.wait()
    sub = lax.broadcasted_iota(jnp.int32, (8, BLOCK), 0)
    lanes = lax.broadcasted_iota(jnp.int32, (8, BLOCK), 1)
    work = []
    for g in range(groups):
        at = 8 * g % piece
        own = gram_ref[8 * g // piece % 2, at : at + 8, :]
        if 8 * g >= 2 * piece:
            own = shifted(own, probe_count)
        unit = jnp.where(lanes == sub + (8 * g + probe_count), 1.0, 0.0)
        work.append(jnp.where(lanes < probe_count, own, unit))
    factor, inverse = eliminate(work, probe_count)
    load_rank.wait()
    rank = rank_ref[0]
    for g in range(groups):
        factor_ref[8 * g : 8 * g + 8, :] = factor[g][:, 0:probe_count]
    lower = jnp.concatenate(
        [
            jnp.where((sub + 8 * g < rank) & (lanes >= probe_count), inverse[g], 0.0)
            for g in range(groups)
        ],
        axis=0,
    )
    lower = lower + shifted(lower, probe_count)
    l_high, l_low = split(lower)
    both = jnp.concatenate([l_high, l_low], axis=0)
    load_sketch.wait()
    stores = []
    for h in range(halves):
        for r in range(rows):
            here = slice(r * cols + h * BLOCK, r * cols + (h + 1) * BLOCK)
            solved = dot(both, xcat[:, here], NN)
            out[h, pl.ds(r, probe_count, stride=rows), :] = (
                solved[0:probe_count] + solved[probe_count:]
            )
        store = pltpu.make_async_copy(
            out.at[h], basis_hbm.at[:, pl.ds(h * BLOCK, BLOCK)], sem.at[3 + h]
        )
        store.start()
        stores.append(store)
    for store in stores:
        store.wait()


def per_device(
    n_mesh, n_obs, nz, probes, velocity, viscosity, friction, obs_block, obs_weight, obs_prec, rank
):
    probe_count, rows, cols = probes.shape
    per_dev = obs_weight.shape[1]
    ny = n_mesh // nz
    piece = probe_count // 4
    dma = pltpu.SemaphoreType.DMA
    vmem = pl.BlockSpec(memory_space=pltpu.VMEM)
    hbm = pl.BlockSpec(memory_space=pltpu.HBM)
    xcat, gram = pl.pallas_call(
        functools.partial(sketch_kernel, n_mesh, n_obs, nz),
        out_shape=(
            jax.ShapeDtypeStruct((2 * probe_count, rows * cols), BF16),
            jax.ShapeDtypeStruct((2, piece, BLOCK), F32),
        ),
        in_specs=[hbm] * 7,
        out_specs=(hbm, hbm),
        scratch_shapes=[
            pltpu.VMEM((probe_count, rows, cols), BF16),
            pltpu.VMEM((rows, cols), F32),
            pltpu.VMEM((1, per_dev), jnp.int32),
            pltpu.VMEM((1, per_dev, BLOCK), F32),
            pltpu.VMEM((1, per_dev), F32),
            pltpu.VMEM((cols // BLOCK, probe_count * rows, BLOCK), F32),
            pltpu.VMEM((rows, probe_count, cols), F32),
            pltpu.VMEM((rows, probe_count, cols), F32),
            pltpu.VMEM((7, rows, cols), F32),
            pltpu.VMEM((2, rows, cols), F32),
            pltpu.VMEM((2, 8, cols), F32),
            pltpu.VMEM((2, 8, cols), F32),
            pltpu.VMEM((2, rows, BLOCK), F32),
            pltpu.VMEM((2, probe_count, cols), BF16),
            pltpu.VMEM((2, probe_count, cols), BF16),
            pltpu.VMEM((2, 8, BLOCK), F32),
            pltpu.VMEM((2, 8, BLOCK), F32),
            pltpu.VMEM((2, probe_count, cols), BF16),
            pltpu.VMEM((2, probe_count, cols), BF16),
            pltpu.VMEM((2, 8, BLOCK), F32),
            pltpu.VMEM((2, 8, BLOCK), F32),
            pltpu.VMEM((16, BLOCK), F32),
            pltpu.VMEM((n_obs, per_dev + 16, BLOCK), jnp.int16),
            pltpu.VMEM((n_obs * per_dev, 2 * BLOCK), BF16),
            pltpu.VMEM((cols // BLOCK, rows * probe_count, 2 * BLOCK), BF16),
            pltpu.VMEM((2 * probe_count, rows * cols), BF16),
            pltpu.VMEM((2, piece, BLOCK), F32),
            pltpu.VMEM((piece, BLOCK), F32),
            pltpu.VMEM((n_obs // 2 * ny, piece, BLOCK), F32),
            pltpu.VMEM((nz, piece, BLOCK), F32),
            pltpu.VMEM((2, piece, BLOCK), F32),
            dma((7,)),
            dma((17,)),
            dma((17,)),
            pltpu.SemaphoreType.REGULAR((3, 2)),
            pltpu.SemaphoreType.REGULAR((2, 2)),
        ],
        compiler_params=pltpu.CompilerParams(collective_id=0, has_side_effects=True),
    )(probes, velocity, viscosity, friction, obs_block, obs_weight, obs_prec)
    basis, factor = pl.pallas_call(
        basis_kernel,
        out_shape=(
            jax.ShapeDtypeStruct((probe_count * rows, cols), F32),
            jax.ShapeDtypeStruct((probe_count, probe_count), F32),
        ),
        in_specs=[hbm, hbm, hbm],
        out_specs=(hbm, vmem),
        scratch_shapes=[
            pltpu.VMEM((2, piece, BLOCK), F32),
            pltpu.VMEM((2 * probe_count, rows * cols), BF16),
            pltpu.SMEM((1,), jnp.int32),
            pltpu.VMEM((cols // BLOCK, probe_count * rows, BLOCK), F32),
            dma((3 + cols // BLOCK,)),
        ],
    )(gram, xcat, rank)
    return basis.reshape(probe_count, rows, cols), factor


def solution(mesh):
    in_specs = (
        P(None, "mesh", "obs"),
        P("mesh", "obs"),
        P("mesh", "obs"),
        P("mesh", "obs"),
        P("mesh", "obs"),
        P("mesh", "obs", None),
        P("mesh", "obs"),
        P(),
    )
    n_mesh, n_obs = mesh.shape["mesh"], mesh.shape["obs"]
    nz = Z_RING if n_mesh % Z_RING == 0 else n_mesh // 2
    return jax.shard_map(
        functools.partial(per_device, n_mesh, n_obs, nz),
        mesh=mesh,
        in_specs=in_specs,
        out_specs=(P(None, "mesh", "obs"), P()),
        check_vma=False,
    )
```

```python
import functools

import jax
import jax.numpy as jnp
from jax import lax
from jax.experimental import pallas as pl
from jax.experimental.pallas import tpu as pltpu
from jax.sharding import PartitionSpec as P

BLOCK = 128
PRIOR = 1.0
Z_RING = 16
NEAR = 1
PIVOTS = 8
WEIGHT_STEPS = 65534.0
PREC_STEPS = 32768.0
MESH = pl.DeviceIdType.MESH
F32 = jnp.float32
BF16 = jnp.bfloat16
NORTH, SOUTH, WEST, EAST = 0, 1, 2, 3
OPPOSITE = (SOUTH, NORTH, EAST, WEST)
NT = (((1,), (1,)), ((), ()))
NN = (((1,), (0,)), ((), ()))


def dot(a, b, dims):
    return lax.dot_general(a, b, dims, preferred_element_type=F32)


def split(x):
    high = x.astype(BF16)
    return high, (x - high.astype(F32)).astype(BF16)


def fixed(x):
    return jnp.floor(x + 0.5).astype(jnp.int32).astype(jnp.int16)


def shifted(x, amount):
    amount %= BLOCK
    return pltpu.roll(x, amount, 1) if amount else x


def sketch_kernel(
    n_mesh,
    n_obs,
    nz,
    probes_hbm,
    vel_hbm,
    visc_hbm,
    fric_hbm,
    block_hbm,
    weight_hbm,
    prec_hbm,
    xcat_hbm,
    gram_hbm,
    probes_ref,
    fric_ref,
    block_ref,
    weight_ref,
    prec_ref,
    probe_pr,
    field,
    forced,
    coef,
    tiles,
    edge_rows,
    rows_halo,
    cols_halo,
    prow,
    prow_halo,
    fcol,
    fcol_halo,
    srow,
    srow_halo,
    scol,
    scol_halo,
    meta,
    wall,
    wcat,
    tcat,
    xcat,
    part,
    chip_buf,
    plane_buf,
    z_buf,
    both_buf,
    load_sem,
    send_sem,
    recv_sem,
    z_token,
    y_token,
):
    ny = n_mesh // nz
    probe_count, rows, cols = probes_ref.shape
    halves = cols // BLOCK
    slab_columns = halves * n_obs
    per_dev = weight_ref.shape[1]
    obs_total = per_dev * n_obs
    piece = part.shape[1]
    nx = n_obs // 2
    groups = probe_count // 8
    WALL, CHIP, PLANE, ZS, BOTH, TILES, FORCED, SOURCE = 0, 1, 2, 3, 4, 5, 9, 13

    m = lax.axis_index("mesh")
    o = lax.axis_index("obs")
    y = m // nz
    z = lax.rem(m, nz)
    x = o // 2
    core = lax.rem(o, 2)
    sibling = {"obs": o + 1 - 2 * core}
    neighbours = (
        {"mesh": lax.rem(m + n_mesh - 1, n_mesh)},
        {"mesh": lax.rem(m + 1, n_mesh)},
        {"obs": lax.rem(o + n_obs - 1, n_obs)},
        {"obs": lax.rem(o + 1, n_obs)},
    )
    obs_peers = [
        {"obs": lax.rem(o + d, n_obs)}
        for d in sorted(range(1, n_obs), key=lambda d: -min(d, n_obs - d))
    ]
    plane_peers = [
        {"mesh": lax.rem(y + dy, ny) * nz + z, "obs": lax.rem(o + 2 * dx, n_obs)}
        for dx, dy in sorted(
            ((dx, dy) for dx in range(nx) for dy in range(ny) if dx or dy),
            key=lambda d: -min(d[0], nx - d[0]) - min(d[1], ny - d[1]),
        )
    ]

    def y_peer(d):
        return {"mesh": lax.rem(y + d, ny) * nz + z}

    def z_peer(d):
        return {"mesh": y * nz + lax.rem(z + d, nz)}

    z_peers = [z_peer(d) for d in sorted(range(1, nz), key=lambda d: -min(d, nz - d))]
    near_z = [z_peer(d) for d in range(1, nz) if min(d, nz - d) <= NEAR]

    names = (probes_hbm, weight_hbm, block_hbm, prec_hbm, visc_hbm, vel_hbm, fric_hbm)
    places = (probes_ref, weight_ref, block_ref, prec_ref, tiles.at[0], tiles.at[1], fric_ref)
    loads = [
        pltpu.make_async_copy(src, dst, load_sem.at[i])
        for i, (src, dst) in enumerate(zip(names, places))
    ]
    barrier = pltpu.get_barrier_semaphore()
    inner = (m > 0, m < n_mesh - 1, o > 0, o < n_obs - 1)
    over_wrap = (inner[NORTH] & (z == 0), inner[SOUTH] & (z == nz - 1))
    partners = obs_peers + [y_peer(d) for d in sorted({1, ny - 1})] + near_z
    for peer in partners:
        pl.semaphore_signal(barrier, inc=1, device_id=peer, device_id_type=MESH)
    for side in (NORTH, SOUTH):

        @pl.when(over_wrap[side])
        def _():
            pl.semaphore_signal(
                barrier, inc=1, device_id=neighbours[side], device_id_type=MESH
            )

    for load in loads:
        load.start()

    rows_in = (rows_halo, prow_halo, srow_halo)
    columns_in = (cols_halo, fcol_halo, scol_halo)
    for side in range(4):

        @pl.when(jnp.logical_not(inner[side]))
        def _():
            for buf in columns_in if side >= WEST else rows_in:
                buf[side % 2] = jnp.zeros(buf.shape[1:], buf.dtype)

    lane = lax.broadcasted_iota(jnp.int32, (1, BLOCK), 1)
    meta[...] = jnp.zeros((16, BLOCK), F32)
    for load in loads[1:4]:
        load.wait()
    wall[o, 0:per_dev, :] = fixed(weight_ref[0] * WEIGHT_STEPS)
    scaled_prec = prec_ref[...] * PREC_STEPS
    coarse = jnp.floor(scaled_prec)
    meta[0:1, 0:per_dev] = block_ref[...].astype(F32)
    meta[1:2, 0:per_dev] = coarse
    meta[2:3, 0:per_dev] = (scaled_prec - coarse) * (PREC_STEPS - 1)
    tail = meta[...]
    wall[o, per_dev : per_dev + 16, :] = fixed(tail + shifted(tail, per_dev))

    loads[0].wait()
    for h in range(halves):
        probe_pr[h] = (
            probes_ref[:, :, h * BLOCK : (h + 1) * BLOCK]
            .astype(F32)
            .reshape(probe_count * rows, BLOCK)
        )
    for load in loads[4:]:
        load.wait()

    def probe_rows(r):
        return [
            probe_pr[h, pl.ds(r, probe_count, stride=rows), :] for h in range(halves)
        ]

    def packed_edges(src, first):
        at = slice(0, BLOCK) if first else slice(cols - BLOCK, cols)
        out = jnp.zeros((8, BLOCK), F32)
        for g in range(groups):
            own = jnp.zeros((8, BLOCK), F32)
            for r in range(rows):
                value = src[r, 8 * g : 8 * g + 8, at]
                own = jnp.where(lane == r, shifted(value, r + (0 if first else 1)), own)
            out = out + shifted(own, rows * g)
        return out

    for r in range(rows):
        parts = probe_rows(r)
        for h in range(halves):
            at = slice(h * BLOCK, (h + 1) * BLOCK)
            forced[r, :, at] = parts[h] * tiles[1, r : r + 1, at]
            if r == 0:
                prow[0, :, at] = parts[h].astype(BF16)
            if r == rows - 1:
                prow[1, :, at] = parts[h].astype(BF16)
    eight = lax.broadcasted_iota(jnp.int32, (8, cols), 0)
    for i, r in enumerate((0, rows - 1)):
        edge_rows[i] = jnp.where(eight == 0, tiles[0, r : r + 1, :], tiles[1, r : r + 1, :])
    fcol[0] = packed_edges(forced, True)
    fcol[1] = packed_edges(forced, False)

    pl.semaphore_wait(
        barrier,
        len(partners) + over_wrap[0].astype(jnp.int32) + over_wrap[1].astype(jnp.int32),
    )

    def send(src, dst, stage, peer):
        pltpu.make_async_remote_copy(
            src_ref=src,
            dst_ref=dst,
            send_sem=send_sem.at[stage],
            recv_sem=recv_sem.at[stage],
            device_id=peer,
            device_id_type=MESH,
        ).start()

    def whole(buf, stage):
        return pltpu.make_async_remote_copy(
            src_ref=buf,
            dst_ref=buf,
            send_sem=send_sem.at[stage],
            recv_sem=recv_sem.at[stage],
            device_id=neighbours[NORTH],
            device_id_type=MESH,
        )

    unsent = []

    def arrived(buf, stage):
        copy = whole(buf, stage)
        unsent.append(copy)
        copy.wait_recv()

    edge_copies = []

    def to_neighbour(src, dst, stage, side):
        there = OPPOSITE[side]

        @pl.when(inner[side])
        def _():
            pltpu.make_async_remote_copy(
                src_ref=src,
                dst_ref=dst,
                send_sem=send_sem.at[stage + side],
                recv_sem=recv_sem.at[stage + there],
                device_id=neighbours[side],
                device_id_type=MESH,
            ).start()

        edge_copies.append((src, stage + side, side))

    def from_neighbour(buf, stage, side):
        @pl.when(inner[side])
        def _():
            whole(buf, stage + side).wait_recv()

    for i in range(2):
        edge = pl.ds(0, BLOCK) if i == 0 else pl.ds(cols - BLOCK, BLOCK)
        to_neighbour(tiles.at[0, :, edge], cols_halo.at[1 - i], TILES, WEST + i)
        to_neighbour(edge_rows.at[i], rows_halo.at[1 - i], TILES, NORTH + i)
    for i in range(2):
        to_neighbour(fcol.at[i], fcol_halo.at[1 - i], FORCED, WEST + i)
    for peer in obs_peers:
        send(wall.at[o], wall.at[o], WALL, peer)
    for i in range(2):
        to_neighbour(prow.at[i], prow_halo.at[1 - i], FORCED, NORTH + i)

    tokens = []
    reach = NEAR
    while 2 * reach <= nz // 2:
        tokens.append(reach)
        reach *= 2

    def tell(level):
        for side, d in enumerate((tokens[level], nz - tokens[level])):
            pl.semaphore_signal(
                z_token.at[level, side], inc=1, device_id=z_peer(d), device_id_type=MESH
            )

    def hear(level):
        for side in range(2):
            pl.semaphore_wait(z_token.at[level, side], 1)

    def advance(level):
        if level < len(tokens):
            hear(level)
            if level + 1 < len(tokens):
                tell(level + 1)

    def tell_y(level):
        for side, d in enumerate((1, ny - 1)):
            pl.semaphore_signal(
                y_token.at[level, side], inc=1, device_id=y_peer(d), device_id_type=MESH
            )

    def hear_y(level):
        for side in range(2):
            pl.semaphore_wait(y_token.at[level, side], 1)

    if tokens:
        tell(0)
    tell_y(0)

    for i in range(2):
        from_neighbour(rows_halo.at[i], TILES, NORTH + i)
        from_neighbour(cols_halo.at[i], TILES, WEST + i)
    row_id = lax.broadcasted_iota(jnp.int32, (rows, cols), 0)
    col_id = lax.broadcasted_iota(jnp.int32, (rows, cols), 1)
    visc = tiles[0]

    def face(side, ghost, shift, axis, edge):
        ghost = jnp.where(inner[side], ghost, 0.0)
        return 0.5 * (visc + jnp.where(edge, ghost, pltpu.roll(visc, shift, axis)))

    from_west, from_east = shifted(cols_halo[0], 1), shifted(cols_halo[1], -1)
    face_n = face(NORTH, rows_halo[0, 0:1, :], 1, 0, row_id == 0)
    face_s = face(SOUTH, rows_halo[1, 0:1, :], rows - 1, 0, row_id == rows - 1)
    face_w = face(WEST, jnp.concatenate([from_west] * halves, axis=1), 1, 1, col_id == 0)
    face_e = face(
        EAST, jnp.concatenate([from_east] * halves, axis=1), cols - 1, 1, col_id == cols - 1
    )
    coef[0] = fric_ref[...] + face_n + face_s + face_w + face_e
    coef[1] = jnp.where(inner[NORTH] | (row_id > 0), face_n, 0.0)
    coef[2] = jnp.where(inner[SOUTH] | (row_id < rows - 1), face_s, 0.0)
    coef[3] = jnp.where(col_id > 0, face_w, 0.0)
    coef[4] = jnp.where(col_id < cols - 1, face_e, 0.0)
    coef[5] = jnp.where(inner[WEST] & (col_id == 0), face_w, 0.0)
    coef[6] = jnp.where(inner[EAST] & (col_id == cols - 1), face_e, 0.0)

    def interior(src, r):
        left, right = src[r, :, 0:BLOCK], src[r, :, BLOCK:cols]
        left_up, right_up = shifted(left, 1), shifted(right, 1)
        left_dn, right_dn = shifted(left, -1), shifted(right, -1)
        west = (left_up, jnp.where(lane == 0, left_up, right_up))
        east = (jnp.where(lane == BLOCK - 1, right_dn, left_dn), right_dn)
        out = []
        for h, centre in enumerate((left, right)):
            at = slice(h * BLOCK, (h + 1) * BLOCK)
            value = coef[0, r : r + 1, at] * centre
            if r < rows - 1:
                value = value - coef[2, r : r + 1, at] * src[r + 1, :, at]
            if r > 0:
                value = value - coef[1, r : r + 1, at] * src[r - 1, :, at]
            value = value - coef[4, r : r + 1, at] * east[h]
            value = value - coef[3, r : r + 1, at] * west[h]
            out.append(value)
        return out

    def spread(halo):
        return [
            jnp.concatenate([shifted(halo[i], -rows * g) for g in range(groups)], axis=0)
            for i in range(2)
        ]

    def with_columns(out, r, halo):
        from_west = shifted(halo[0], -r)
        from_east = shifted(halo[1], -1 - r)
        return [
            out[0] - coef[5, r : r + 1, 0:BLOCK] * from_west,
            out[1] - coef[6, r : r + 1, BLOCK:cols] * from_east,
        ]

    for r in range(rows):
        left, right = interior(forced, r)
        field[r, :, 0:BLOCK] = left
        field[r, :, BLOCK:cols] = right
    for i in range(2):
        from_neighbour(fcol_halo.at[i], FORCED, WEST + i)
    columns = spread(fcol_halo)
    order = [0, rows - 1] + list(range(1, rows - 1))

    def tangent(r):
        out = with_columns([field[r, :, 0:BLOCK], field[r, :, BLOCK:cols]], r, columns)
        place = order.index(r)
        here = slice(place * probe_count, (place + 1) * probe_count)
        for h in range(halves):
            at = slice(h * BLOCK, (h + 1) * BLOCK)
            if r == 0:
                scale = coef[1, 0:1, at] * rows_halo[0, 1:2, at]
                out[h] = out[h] - scale * prow_halo[0, :, at].astype(F32)
            if r == rows - 1:
                scale = coef[2, r : r + 1, at] * rows_halo[1, 1:2, at]
                out[h] = out[h] - scale * prow_halo[1, :, at].astype(F32)
            tcat[h, here, 0:BLOCK] = out[h].astype(BF16)
            tcat[h, here, BLOCK : 2 * BLOCK] = out[h].astype(BF16)

    for r in order[2:]:
        tangent(r)
    advance(0)

    arrived(wall.at[pl.ds(0, n_obs - 1)], WALL)
    for i in range(n_obs):
        w_high, w_low = split(wall[i, 0:per_dev, :].astype(jnp.int32).astype(F32))
        wcat[i * per_dev : (i + 1) * per_dev, 0:BLOCK] = w_high
        wcat[i * per_dev : (i + 1) * per_dev, BLOCK : 2 * BLOCK] = w_low
    per_row = BLOCK // per_dev
    tails = [wall[i, per_dev : per_dev + 16, :].astype(jnp.int32).astype(F32) for i in range(n_obs)]
    chunks = []
    for c in range(obs_total // BLOCK):
        value = tails[c * per_row]
        for k in range(1, per_row):
            value = jnp.where(lane < k * per_dev, value, tails[c * per_row + k])
        chunks.append(value)
    tail = jnp.concatenate(chunks, axis=1)
    obs_at = tail[0:1]
    prec = (tail[1:2] + tail[2:3] * (1.0 / (PREC_STEPS - 1))) * (1.0 / PREC_STEPS)
    obs_scale = prec * (1.0 / WEIGHT_STEPS**2)
    weights = wcat[...]
    for i in range(2):
        from_neighbour(prow_halo.at[i], FORCED, NORTH + i)
    for r in order[:2]:
        tangent(r)
    for group in (order[:2], order[2:]):
        start = order.index(group[0]) * probe_count
        size = len(group) * probe_count
        for h in range(halves):
            picked = dot(tcat[h, start : start + size, :], weights, NT)
            masked = []
            for k, r in enumerate(group):
                own = (r * slab_columns + o * halves + h).astype(F32)
                scale = jnp.where(obs_at == own, obs_scale, 0.0)
                masked.append(picked[k * probe_count : (k + 1) * probe_count] * scale)
            mis_high, mis_low = split(jnp.concatenate(masked, axis=0))
            both = dot(mis_high, weights, NN)
            low = dot(mis_low, weights[:, 0:BLOCK], NN)
            source = both[:, 0:BLOCK] + (both[:, BLOCK:] + low)
            for k, r in enumerate(group):
                field[r, :, h * BLOCK : (h + 1) * BLOCK] = source[
                    k * probe_count : (k + 1) * probe_count
                ]
        if group[0] == 0:
            for i in range(2):
                srow[i] = field[(rows - 1) * i].astype(BF16)
                to_neighbour(srow.at[i], srow_halo.at[1 - i], SOURCE, NORTH + i)
    scol[0] = packed_edges(field, True)
    scol[1] = packed_edges(field, False)
    for i in range(2):
        to_neighbour(scol.at[i], scol_halo.at[1 - i], SOURCE, WEST + i)

    for r in range(rows):
        left, right = interior(field, r)
        forced[r, :, 0:BLOCK] = left
        forced[r, :, BLOCK:cols] = right
    advance(1)
    hear_y(0)
    tell_y(1)
    for i in range(2):
        from_neighbour(scol_halo.at[i], SOURCE, WEST + i)
    columns = spread(scol_halo)
    quad = 0.0
    for group in (order[2:], order[:2]):
        if group[0] == 0:
            for i in range(2):
                from_neighbour(srow_halo.at[i], SOURCE, NORTH + i)
        for r in group:
            out = with_columns([forced[r, :, 0:BLOCK], forced[r, :, BLOCK:cols]], r, columns)
            parts = probe_rows(r)
            for h in range(halves):
                at = slice(h * BLOCK, (h + 1) * BLOCK)
                if r == 0:
                    out[h] = out[h] - coef[1, 0:1, at] * srow_halo[0, :, at].astype(F32)
                if r == rows - 1:
                    out[h] = out[h] - coef[2, r : r + 1, at] * srow_halo[1, :, at].astype(F32)
                s_high, s_low = split(tiles[1, r : r + 1, at] * out[h] + PRIOR * parts[h])
                here = slice(r * cols + h * BLOCK, r * cols + (h + 1) * BLOCK)
                xcat[0:probe_count, here] = s_high
                xcat[probe_count : 2 * probe_count, here] = s_low
        if group[0] == 0:
            both = [xcat[:, r * cols : (r + 1) * cols] for r in group]
            for sketch in both:
                quad = quad + dot(sketch, sketch, NT)
        else:
            sketch = xcat[:, group[0] * cols : (group[-1] + 1) * cols]
            quad = dot(sketch, sketch, NT)

    keep_sketch = pltpu.make_async_copy(xcat, xcat_hbm, load_sem.at[0])
    keep_sketch.start()
    pair = quad[0:probe_count] + quad[probe_count:]
    gram = pair + shifted(pair, probe_count)
    half = probe_count // 2
    packed = jnp.where(lane < probe_count, gram[0:half], gram[half:])
    for i in range(2):
        part[i] = packed[i * piece : (i + 1) * piece]

    def total(buf, count):
        values = [buf[i] for i in range(count)]
        while len(values) > 1:
            values = [
                sum(values[i : i + 2][1:], values[i]) for i in range(0, len(values), 2)
            ]
        return values[0]

    send(part.at[1 - core], chip_buf, CHIP, sibling)
    hear_y(1)
    arrived(chip_buf, CHIP)
    here = y * nx + x
    plane_buf[here] = part[core] + chip_buf[...]
    for peer in plane_peers:
        send(plane_buf.at[here], plane_buf.at[here], PLANE, peer)
    advance(2)
    arrived(plane_buf.at[pl.ds(0, nx * ny - 1)], PLANE)
    z_buf[z] = total(plane_buf, nx * ny)
    for peer in z_peers:
        send(z_buf.at[z], z_buf.at[z], ZS, peer)
    for copy in unsent:
        copy.wait_send()
    for src, at, side in edge_copies:

        @pl.when(inner[side])
        def _():
            whole(src, at).wait_send()

    keep_sketch.wait()
    done = len(unsent)
    arrived(z_buf.at[pl.ds(0, nz - 1)], ZS)
    cells = rows * cols * n_mesh * n_obs
    both_buf[core] = total(z_buf, nz) / cells
    send(both_buf.at[core], both_buf.at[core], BOTH, sibling)
    arrived(both_buf.at[0], BOTH)
    keep_gram = pltpu.make_async_copy(both_buf, gram_hbm, load_sem.at[1])
    keep_gram.start()
    for copy in unsent[done:]:
        copy.wait_send()
    keep_gram.wait()


def eliminate(work, probe_count):
    sub = lax.broadcasted_iota(jnp.int32, (8, BLOCK), 0)
    lanes = lax.broadcasted_iota(jnp.int32, (8, BLOCK), 1)
    groups = len(work)
    factor = [jnp.zeros((8, BLOCK), F32)] * groups
    inverse = [jnp.zeros((8, BLOCK), F32)] * groups

    def wide(x):
        return jnp.broadcast_to(x, (8, BLOCK))

    for k in range(0, probe_count, PIVOTS):
        g, s = divmod(k, 8)
        span = range(PIVOTS)
        col = [[wide(work[i][:, k + j : k + j + 1]) for i in range(g, groups)] for j in span]
        row = [wide(work[g][s + j : s + j + 1, :]) for j in span]
        local = [[wide(col[j][0][s + i : s + i + 1, :]) for j in range(i + 1)] for i in span]
        lower = [[None] * PIVOTS for _ in span]
        inv, roots = [], []
        for p in range(0, PIVOTS, 2):
            a, b, c = local[p][p], local[p + 1][p], local[p + 1][p + 1]
            det = a * c - b * b
            inv_a, inv_det = 1.0 / a, 1.0 / det
            inv_1 = a * inv_det
            slope = b * inv_a
            inv += [inv_a, inv_1]
            roots += [lax.rsqrt(a), lax.rsqrt(det * inv_a)]
            lower[p + 1][p] = slope
            for i in range(p + 2, PIVOTS):
                u, v = local[i][p], local[i][p + 1]
                lower[i][p] = u * inv_a
                lower[i][p + 1] = (v - slope * u) * inv_1
                for j in range(p + 2, i + 1):
                    t, w = local[j][p], local[j][p + 1]
                    local[i][j] = (
                        local[i][j] - (u * (c * t - b * w) + v * (a * w - b * t)) * inv_det
                    )

        def reduce(v):
            done = []
            for j in span:
                value = v[j]
                for i in range(j):
                    value = value - lower[j][i] * done[i]
                done.append(value)
            return done

        reduced = reduce(row)
        scaled = [v * w for v, w in zip(reduced, inv)]
        for j in span:
            inverse[g] = jnp.where(sub == s + j, reduced[j] * roots[j], inverse[g])
        for i in range(g, groups):
            column = reduce([col[j][i - g] for j in span])
            if not (i == g and s + PIVOTS == 8):
                update = work[i]
                for j in range(0, PIVOTS, 2):
                    update = update - (column[j] * scaled[j] + column[j + 1] * scaled[j + 1])
                work[i] = jnp.where(sub >= s + PIVOTS, update, work[i]) if i == g else update
            for j in span:
                keep = column[j] * roots[j]
                if i == g:
                    keep = jnp.where(sub >= s + j, keep, 0.0)
                factor[i] = jnp.where(lanes == k + j, keep, factor[i])
    return factor, inverse


def basis_kernel(
    gram_hbm, xcat_hbm, rank_hbm, basis_hbm, factor_ref, gram_ref, xcat, rank_ref, out, sem
):
    halves, cells, _ = out.shape
    probe_count = factor_ref.shape[0]
    rows = cells // probe_count
    cols = halves * BLOCK
    piece = gram_ref.shape[1]
    groups = probe_count // 8
    load_gram = pltpu.make_async_copy(gram_hbm, gram_ref, sem.at[0])
    load_gram.start()
    load_sketch = pltpu.make_async_copy(xcat_hbm, xcat, sem.at[1])
    load_sketch.start()
    load_rank = pltpu.make_async_copy(rank_hbm, rank_ref, sem.at[2])
    load_rank.start()
    load_gram.wait()
    sub = lax.broadcasted_iota(jnp.int32, (8, BLOCK), 0)
    lanes = lax.broadcasted_iota(jnp.int32, (8, BLOCK), 1)
    work = []
    for g in range(groups):
        at = 8 * g % piece
        own = gram_ref[8 * g // piece % 2, at : at + 8, :]
        if 8 * g >= 2 * piece:
            own = shifted(own, probe_count)
        unit = jnp.where(lanes == sub + (8 * g + probe_count), 1.0, 0.0)
        work.append(jnp.where(lanes < probe_count, own, unit))
    factor, inverse = eliminate(work, probe_count)
    load_rank.wait()
    rank = rank_ref[0]
    for g in range(groups):
        factor_ref[8 * g : 8 * g + 8, :] = factor[g][:, 0:probe_count]
    lower = jnp.concatenate(
        [
            jnp.where((sub + 8 * g < rank) & (lanes >= probe_count), inverse[g], 0.0)
            for g in range(groups)
        ],
        axis=0,
    )
    lower = lower + shifted(lower, probe_count)
    l_high, l_low = split(lower)
    both = jnp.concatenate([l_high, l_low], axis=0)
    load_sketch.wait()
    stores = []
    for h in range(halves):
        for r in range(rows):
            here = slice(r * cols + h * BLOCK, r * cols + (h + 1) * BLOCK)
            solved = dot(both, xcat[:, here], NN)
            out[h, pl.ds(r, probe_count, stride=rows), :] = (
                solved[0:probe_count] + solved[probe_count:]
            )
        store = pltpu.make_async_copy(
            out.at[h], basis_hbm.at[:, pl.ds(h * BLOCK, BLOCK)], sem.at[3 + h]
        )
        store.start()
        stores.append(store)
    for store in stores:
        store.wait()


def per_device(
    n_mesh, n_obs, nz, probes, velocity, viscosity, friction, obs_block, obs_weight, obs_prec, rank
):
    probe_count, rows, cols = probes.shape
    per_dev = obs_weight.shape[1]
    ny = n_mesh // nz
    piece = probe_count // 4
    dma = pltpu.SemaphoreType.DMA
    vmem = pl.BlockSpec(memory_space=pltpu.VMEM)
    hbm = pl.BlockSpec(memory_space=pltpu.HBM)
    xcat, gram = pl.pallas_call(
        functools.partial(sketch_kernel, n_mesh, n_obs, nz),
        out_shape=(
            jax.ShapeDtypeStruct((2 * probe_count, rows * cols), BF16),
            jax.ShapeDtypeStruct((2, piece, BLOCK), F32),
        ),
        in_specs=[hbm] * 7,
        out_specs=(hbm, hbm),
        scratch_shapes=[
            pltpu.VMEM((probe_count, rows, cols), BF16),
            pltpu.VMEM((rows, cols), F32),
            pltpu.VMEM((1, per_dev), jnp.int32),
            pltpu.VMEM((1, per_dev, BLOCK), F32),
            pltpu.VMEM((1, per_dev), F32),
            pltpu.VMEM((cols // BLOCK, probe_count * rows, BLOCK), F32),
            pltpu.VMEM((rows, probe_count, cols), F32),
            pltpu.VMEM((rows, probe_count, cols), F32),
            pltpu.VMEM((7, rows, cols), F32),
            pltpu.VMEM((2, rows, cols), F32),
            pltpu.VMEM((2, 8, cols), F32),
            pltpu.VMEM((2, 8, cols), F32),
            pltpu.VMEM((2, rows, BLOCK), F32),
            pltpu.VMEM((2, probe_count, cols), BF16),
            pltpu.VMEM((2, probe_count, cols), BF16),
            pltpu.VMEM((2, 8, BLOCK), F32),
            pltpu.VMEM((2, 8, BLOCK), F32),
            pltpu.VMEM((2, probe_count, cols), BF16),
            pltpu.VMEM((2, probe_count, cols), BF16),
            pltpu.VMEM((2, 8, BLOCK), F32),
            pltpu.VMEM((2, 8, BLOCK), F32),
            pltpu.VMEM((16, BLOCK), F32),
            pltpu.VMEM((n_obs, per_dev + 16, BLOCK), jnp.int16),
            pltpu.VMEM((n_obs * per_dev, 2 * BLOCK), BF16),
            pltpu.VMEM((cols // BLOCK, rows * probe_count, 2 * BLOCK), BF16),
            pltpu.VMEM((2 * probe_count, rows * cols), BF16),
            pltpu.VMEM((2, piece, BLOCK), F32),
            pltpu.VMEM((piece, BLOCK), F32),
            pltpu.VMEM((n_obs // 2 * ny, piece, BLOCK), F32),
            pltpu.VMEM((nz, piece, BLOCK), F32),
            pltpu.VMEM((2, piece, BLOCK), F32),
            dma((7,)),
            dma((17,)),
            dma((17,)),
            pltpu.SemaphoreType.REGULAR((3, 2)),
            pltpu.SemaphoreType.REGULAR((2, 2)),
        ],
        compiler_params=pltpu.CompilerParams(collective_id=0, has_side_effects=True),
    )(probes, velocity, viscosity, friction, obs_block, obs_weight, obs_prec)
    basis, factor = pl.pallas_call(
        basis_kernel,
        out_shape=(
            jax.ShapeDtypeStruct((probe_count * rows, cols), F32),
            jax.ShapeDtypeStruct((probe_count, probe_count), F32),
        ),
        in_specs=[hbm, hbm, hbm],
        out_specs=(hbm, vmem),
        scratch_shapes=[
            pltpu.VMEM((2, piece, BLOCK), F32),
            pltpu.VMEM((2 * probe_count, rows * cols), BF16),
            pltpu.SMEM((1,), jnp.int32),
            pltpu.VMEM((cols // BLOCK, probe_count * rows, BLOCK), F32),
            dma((3 + cols // BLOCK,)),
        ],
    )(gram, xcat, rank)
    return basis.reshape(probe_count, rows, cols), factor


def solution(mesh):
    in_specs = (
        P(None, "mesh", "obs"),
        P("mesh", "obs"),
        P("mesh", "obs"),
        P("mesh", "obs"),
        P("mesh", "obs"),
        P("mesh", "obs", None),
        P("mesh", "obs"),
        P(),
    )
    n_mesh, n_obs = mesh.shape["mesh"], mesh.shape["obs"]
    nz = Z_RING if n_mesh % Z_RING == 0 else n_mesh // 2
    return jax.shard_map(
        functools.partial(per_device, n_mesh, n_obs, nz),
        mesh=mesh,
        in_specs=in_specs,
        out_specs=(P(None, "mesh", "obs"), P()),
        check_vma=False,
    )
```

```python
import functools

import jax
import jax.numpy as jnp
from jax import lax
from jax.experimental import pallas as pl
from jax.experimental.pallas import tpu as pltpu
from jax.sharding import PartitionSpec as P

BLOCK = 128
PRIOR = 1.0
Z_RING = 16
NEAR = 1
PIVOTS = 8
WEIGHT_STEPS = 65534.0
PREC_STEPS = 32768.0
MESH = pl.DeviceIdType.MESH
F32 = jnp.float32
BF16 = jnp.bfloat16
NORTH, SOUTH, WEST, EAST = 0, 1, 2, 3
OPPOSITE = (SOUTH, NORTH, EAST, WEST)
NT = (((1,), (1,)), ((), ()))
NN = (((1,), (0,)), ((), ()))


def dot(a, b, dims):
    return lax.dot_general(a, b, dims, preferred_element_type=F32)


def split(x):
    high = x.astype(BF16)
    return high, (x - high.astype(F32)).astype(BF16)


def fixed(x):
    return jnp.floor(x + 0.5).astype(jnp.int32).astype(jnp.int16)


def shifted(x, amount):
    amount %= BLOCK
    return pltpu.roll(x, amount, 1) if amount else x


def sketch_kernel(
    n_mesh,
    n_obs,
    nz,
    probes_hbm,
    vel_hbm,
    visc_hbm,
    fric_hbm,
    block_hbm,
    weight_hbm,
    prec_hbm,
    xcat_hbm,
    gram_hbm,
    probes_ref,
    fric_ref,
    block_ref,
    weight_ref,
    prec_ref,
    probe_pr,
    field,
    forced,
    coef,
    tiles,
    edge_rows,
    rows_halo,
    cols_halo,
    prow,
    prow_halo,
    fcol,
    fcol_halo,
    srow,
    srow_halo,
    scol,
    scol_halo,
    meta,
    wall,
    wcat,
    tcat,
    xcat,
    part,
    chip_buf,
    plane_buf,
    z_buf,
    both_buf,
    load_sem,
    send_sem,
    recv_sem,
    z_token,
    y_token,
):
    ny = n_mesh // nz
    probe_count, rows, cols = probes_ref.shape
    halves = cols // BLOCK
    slab_columns = halves * n_obs
    per_dev = weight_ref.shape[1]
    obs_total = per_dev * n_obs
    piece = part.shape[1]
    nx = n_obs // 2
    groups = probe_count // 8
    WALL, CHIP, PLANE, ZS, BOTH, TILES, FORCED, SOURCE = 0, 1, 2, 3, 4, 5, 9, 13

    m = lax.axis_index("mesh")
    o = lax.axis_index("obs")
    y = m // nz
    z = lax.rem(m, nz)
    x = o // 2
    core = lax.rem(o, 2)
    sibling = {"obs": o + 1 - 2 * core}
    neighbours = (
        {"mesh": lax.rem(m + n_mesh - 1, n_mesh)},
        {"mesh": lax.rem(m + 1, n_mesh)},
        {"obs": lax.rem(o + n_obs - 1, n_obs)},
        {"obs": lax.rem(o + 1, n_obs)},
    )
    obs_peers = [
        {"obs": lax.rem(o + d, n_obs)}
        for d in sorted(range(1, n_obs), key=lambda d: -min(d, n_obs - d))
    ]
    plane_peers = [
        {"mesh": lax.rem(y + dy, ny) * nz + z, "obs": lax.rem(o + 2 * dx, n_obs)}
        for dx, dy in sorted(
            ((dx, dy) for dx in range(nx) for dy in range(ny) if dx or dy),
            key=lambda d: -min(d[0], nx - d[0]) - min(d[1], ny - d[1]),
        )
    ]

    def y_peer(d):
        return {"mesh": lax.rem(y + d, ny) * nz + z}

    def z_peer(d):
        return {"mesh": y * nz + lax.rem(z + d, nz)}

    z_peers = [z_peer(d) for d in sorted(range(1, nz), key=lambda d: -min(d, nz - d))]
    near_z = [z_peer(d) for d in range(1, nz) if min(d, nz - d) <= NEAR]

    names = (probes_hbm, weight_hbm, block_hbm, prec_hbm, visc_hbm, vel_hbm, fric_hbm)
    places = (probes_ref, weight_ref, block_ref, prec_ref, tiles.at[0], tiles.at[1], fric_ref)
    loads = [
        pltpu.make_async_copy(src, dst, load_sem.at[i])
        for i, (src, dst) in enumerate(zip(names, places))
    ]
    for load in loads:
        load.start()

    barrier = pltpu.get_barrier_semaphore()
    inner = (m > 0, m < n_mesh - 1, o > 0, o < n_obs - 1)
    over_wrap = (inner[NORTH] & (z == 0), inner[SOUTH] & (z == nz - 1))
    partners = obs_peers + [y_peer(d) for d in sorted({1, ny - 1})] + near_z
    for peer in partners:
        pl.semaphore_signal(barrier, inc=1, device_id=peer, device_id_type=MESH)
    for side in (NORTH, SOUTH):

        @pl.when(over_wrap[side])
        def _():
            pl.semaphore_signal(
                barrier, inc=1, device_id=neighbours[side], device_id_type=MESH
            )

    rows_in = (rows_halo, prow_halo, srow_halo)
    columns_in = (cols_halo, fcol_halo, scol_halo)
    for side in range(4):

        @pl.when(jnp.logical_not(inner[side]))
        def _():
            for buf in columns_in if side >= WEST else rows_in:
                buf[side % 2] = jnp.zeros(buf.shape[1:], buf.dtype)

    lane = lax.broadcasted_iota(jnp.int32, (1, BLOCK), 1)
    meta[...] = jnp.zeros((16, BLOCK), F32)
    for load in loads[1:4]:
        load.wait()
    wall[o, 0:per_dev, :] = fixed(weight_ref[0] * WEIGHT_STEPS)
    scaled_prec = prec_ref[...] * PREC_STEPS
    coarse = jnp.floor(scaled_prec)
    meta[0:1, 0:per_dev] = block_ref[...].astype(F32)
    meta[1:2, 0:per_dev] = coarse
    meta[2:3, 0:per_dev] = (scaled_prec - coarse) * (PREC_STEPS - 1)
    tail = meta[...]
    wall[o, per_dev : per_dev + 16, :] = fixed(tail + shifted(tail, per_dev))

    loads[0].wait()
    for h in range(halves):
        probe_pr[h] = (
            probes_ref[:, :, h * BLOCK : (h + 1) * BLOCK]
            .astype(F32)
            .reshape(probe_count * rows, BLOCK)
        )
    for load in loads[4:]:
        load.wait()

    def probe_rows(r):
        return [
            probe_pr[h, pl.ds(r, probe_count, stride=rows), :] for h in range(halves)
        ]

    def packed_edges(src, first):
        at = slice(0, BLOCK) if first else slice(cols - BLOCK, cols)
        out = jnp.zeros((8, BLOCK), F32)
        for g in range(groups):
            own = jnp.zeros((8, BLOCK), F32)
            for r in range(rows):
                value = src[r, 8 * g : 8 * g + 8, at]
                own = jnp.where(lane == r, shifted(value, r + (0 if first else 1)), own)
            out = out + shifted(own, rows * g)
        return out

    for r in range(rows):
        parts = probe_rows(r)
        for h in range(halves):
            at = slice(h * BLOCK, (h + 1) * BLOCK)
            forced[r, :, at] = parts[h] * tiles[1, r : r + 1, at]
            if r == 0:
                prow[0, :, at] = parts[h].astype(BF16)
            if r == rows - 1:
                prow[1, :, at] = parts[h].astype(BF16)
    eight = lax.broadcasted_iota(jnp.int32, (8, cols), 0)
    for i, r in enumerate((0, rows - 1)):
        edge_rows[i] = jnp.where(eight == 0, tiles[0, r : r + 1, :], tiles[1, r : r + 1, :])
    fcol[0] = packed_edges(forced, True)
    fcol[1] = packed_edges(forced, False)

    pl.semaphore_wait(
        barrier,
        len(partners) + over_wrap[0].astype(jnp.int32) + over_wrap[1].astype(jnp.int32),
    )

    def send(src, dst, stage, peer):
        pltpu.make_async_remote_copy(
            src_ref=src,
            dst_ref=dst,
            send_sem=send_sem.at[stage],
            recv_sem=recv_sem.at[stage],
            device_id=peer,
            device_id_type=MESH,
        ).start()

    def whole(buf, stage):
        return pltpu.make_async_remote_copy(
            src_ref=buf,
            dst_ref=buf,
            send_sem=send_sem.at[stage],
            recv_sem=recv_sem.at[stage],
            device_id=neighbours[NORTH],
            device_id_type=MESH,
        )

    unsent = []

    def arrived(buf, stage):
        copy = whole(buf, stage)
        unsent.append(copy)
        copy.wait_recv()

    edge_copies = []

    def to_neighbour(src, dst, stage, side):
        there = OPPOSITE[side]

        @pl.when(inner[side])
        def _():
            pltpu.make_async_remote_copy(
                src_ref=src,
                dst_ref=dst,
                send_sem=send_sem.at[stage + side],
                recv_sem=recv_sem.at[stage + there],
                device_id=neighbours[side],
                device_id_type=MESH,
            ).start()

        edge_copies.append((src, stage + side, side))

    def from_neighbour(buf, stage, side):
        @pl.when(inner[side])
        def _():
            whole(buf, stage + side).wait_recv()

    for i in range(2):
        edge = pl.ds(0, BLOCK) if i == 0 else pl.ds(cols - BLOCK, BLOCK)
        to_neighbour(tiles.at[0, :, edge], cols_halo.at[1 - i], TILES, WEST + i)
        to_neighbour(edge_rows.at[i], rows_halo.at[1 - i], TILES, NORTH + i)
    for i in range(2):
        to_neighbour(fcol.at[i], fcol_halo.at[1 - i], FORCED, WEST + i)
    for peer in obs_peers:
        send(wall.at[o], wall.at[o], WALL, peer)
    for i in range(2):
        to_neighbour(prow.at[i], prow_halo.at[1 - i], FORCED, NORTH + i)

    tokens = []
    reach = NEAR
    while 2 * reach <= nz // 2:
        tokens.append(reach)
        reach *= 2

    def tell(level):
        for side, d in enumerate((tokens[level], nz - tokens[level])):
            pl.semaphore_signal(
                z_token.at[level, side], inc=1, device_id=z_peer(d), device_id_type=MESH
            )

    def hear(level):
        for side in range(2):
            pl.semaphore_wait(z_token.at[level, side], 1)

    def advance(level):
        if level < len(tokens):
            hear(level)
            if level + 1 < len(tokens):
                tell(level + 1)

    def tell_y(level):
        for side, d in enumerate((1, ny - 1)):
            pl.semaphore_signal(
                y_token.at[level, side], inc=1, device_id=y_peer(d), device_id_type=MESH
            )

    def hear_y(level):
        for side in range(2):
            pl.semaphore_wait(y_token.at[level, side], 1)

    if tokens:
        tell(0)
    tell_y(0)

    for i in range(2):
        from_neighbour(rows_halo.at[i], TILES, NORTH + i)
        from_neighbour(cols_halo.at[i], TILES, WEST + i)
    row_id = lax.broadcasted_iota(jnp.int32, (rows, cols), 0)
    col_id = lax.broadcasted_iota(jnp.int32, (rows, cols), 1)
    visc = tiles[0]

    def face(side, ghost, shift, axis, edge):
        ghost = jnp.where(inner[side], ghost, 0.0)
        return 0.5 * (visc + jnp.where(edge, ghost, pltpu.roll(visc, shift, axis)))

    from_west, from_east = shifted(cols_halo[0], 1), shifted(cols_halo[1], -1)
    face_n = face(NORTH, rows_halo[0, 0:1, :], 1, 0, row_id == 0)
    face_s = face(SOUTH, rows_halo[1, 0:1, :], rows - 1, 0, row_id == rows - 1)
    face_w = face(WEST, jnp.concatenate([from_west] * halves, axis=1), 1, 1, col_id == 0)
    face_e = face(
        EAST, jnp.concatenate([from_east] * halves, axis=1), cols - 1, 1, col_id == cols - 1
    )
    coef[0] = fric_ref[...] + face_n + face_s + face_w + face_e
    coef[1] = jnp.where(inner[NORTH] | (row_id > 0), face_n, 0.0)
    coef[2] = jnp.where(inner[SOUTH] | (row_id < rows - 1), face_s, 0.0)
    coef[3] = jnp.where(col_id > 0, face_w, 0.0)
    coef[4] = jnp.where(col_id < cols - 1, face_e, 0.0)
    coef[5] = jnp.where(inner[WEST] & (col_id == 0), face_w, 0.0)
    coef[6] = jnp.where(inner[EAST] & (col_id == cols - 1), face_e, 0.0)

    def interior(src, r):
        left, right = src[r, :, 0:BLOCK], src[r, :, BLOCK:cols]
        left_up, right_up = shifted(left, 1), shifted(right, 1)
        left_dn, right_dn = shifted(left, -1), shifted(right, -1)
        west = (left_up, jnp.where(lane == 0, left_up, right_up))
        east = (jnp.where(lane == BLOCK - 1, right_dn, left_dn), right_dn)
        out = []
        for h, centre in enumerate((left, right)):
            at = slice(h * BLOCK, (h + 1) * BLOCK)
            value = coef[0, r : r + 1, at] * centre
            if r < rows - 1:
                value = value - coef[2, r : r + 1, at] * src[r + 1, :, at]
            if r > 0:
                value = value - coef[1, r : r + 1, at] * src[r - 1, :, at]
            value = value - coef[4, r : r + 1, at] * east[h]
            value = value - coef[3, r : r + 1, at] * west[h]
            out.append(value)
        return out

    def spread(halo):
        return [
            jnp.concatenate([shifted(halo[i], -rows * g) for g in range(groups)], axis=0)
            for i in range(2)
        ]

    def with_columns(out, r, halo):
        from_west = shifted(halo[0], -r)
        from_east = shifted(halo[1], -1 - r)
        return [
            out[0] - coef[5, r : r + 1, 0:BLOCK] * from_west,
            out[1] - coef[6, r : r + 1, BLOCK:cols] * from_east,
        ]

    for r in range(rows):
        left, right = interior(forced, r)
        field[r, :, 0:BLOCK] = left
        field[r, :, BLOCK:cols] = right
    for i in range(2):
        from_neighbour(fcol_halo.at[i], FORCED, WEST + i)
    columns = spread(fcol_halo)
    order = [0, rows - 1] + list(range(1, rows - 1))

    def tangent(r):
        out = with_columns([field[r, :, 0:BLOCK], field[r, :, BLOCK:cols]], r, columns)
        place = order.index(r)
        here = slice(place * probe_count, (place + 1) * probe_count)
        for h in range(halves):
            at = slice(h * BLOCK, (h + 1) * BLOCK)
            if r == 0:
                scale = coef[1, 0:1, at] * rows_halo[0, 1:2, at]
                out[h] = out[h] - scale * prow_halo[0, :, at].astype(F32)
            if r == rows - 1:
                scale = coef[2, r : r + 1, at] * rows_halo[1, 1:2, at]
                out[h] = out[h] - scale * prow_halo[1, :, at].astype(F32)
            tcat[h, here, 0:BLOCK] = out[h].astype(BF16)
            tcat[h, here, BLOCK : 2 * BLOCK] = out[h].astype(BF16)

    for r in order[2:]:
        tangent(r)
    advance(0)

    arrived(wall.at[pl.ds(0, n_obs - 1)], WALL)
    for i in range(n_obs):
        w_high, w_low = split(wall[i, 0:per_dev, :].astype(jnp.int32).astype(F32))
        wcat[i * per_dev : (i + 1) * per_dev, 0:BLOCK] = w_high
        wcat[i * per_dev : (i + 1) * per_dev, BLOCK : 2 * BLOCK] = w_low
    per_row = BLOCK // per_dev
    tails = [wall[i, per_dev : per_dev + 16, :].astype(jnp.int32).astype(F32) for i in range(n_obs)]
    chunks = []
    for c in range(obs_total // BLOCK):
        value = tails[c * per_row]
        for k in range(1, per_row):
            value = jnp.where(lane < k * per_dev, value, tails[c * per_row + k])
        chunks.append(value)
    tail = jnp.concatenate(chunks, axis=1)
    obs_at = tail[0:1]
    prec = (tail[1:2] + tail[2:3] * (1.0 / (PREC_STEPS - 1))) * (1.0 / PREC_STEPS)
    obs_scale = prec * (1.0 / WEIGHT_STEPS**2)
    weights = wcat[...]
    for i in range(2):
        from_neighbour(prow_halo.at[i], FORCED, NORTH + i)
    for r in order[:2]:
        tangent(r)
    for group in (order[:2], order[2:]):
        start = order.index(group[0]) * probe_count
        size = len(group) * probe_count
        for h in range(halves):
            picked = dot(tcat[h, start : start + size, :], weights, NT)
            masked = []
            for k, r in enumerate(group):
                own = (r * slab_columns + o * halves + h).astype(F32)
                scale = jnp.where(obs_at == own, obs_scale, 0.0)
                masked.append(picked[k * probe_count : (k + 1) * probe_count] * scale)
            mis_high, mis_low = split(jnp.concatenate(masked, axis=0))
            both = dot(mis_high, weights, NN)
            low = dot(mis_low, weights[:, 0:BLOCK], NN)
            source = both[:, 0:BLOCK] + (both[:, BLOCK:] + low)
            for k, r in enumerate(group):
                field[r, :, h * BLOCK : (h + 1) * BLOCK] = source[
                    k * probe_count : (k + 1) * probe_count
                ]
        if group[0] == 0:
            for i in range(2):
                srow[i] = field[(rows - 1) * i].astype(BF16)
                to_neighbour(srow.at[i], srow_halo.at[1 - i], SOURCE, NORTH + i)
    scol[0] = packed_edges(field, True)
    scol[1] = packed_edges(field, False)
    for i in range(2):
        to_neighbour(scol.at[i], scol_halo.at[1 - i], SOURCE, WEST + i)

    for r in range(rows):
        left, right = interior(field, r)
        forced[r, :, 0:BLOCK] = left
        forced[r, :, BLOCK:cols] = right
    advance(1)
    hear_y(0)
    tell_y(1)
    for i in range(2):
        from_neighbour(scol_halo.at[i], SOURCE, WEST + i)
    columns = spread(scol_halo)
    quad = 0.0
    for group in (order[2:], order[:2]):
        if group[0] == 0:
            for i in range(2):
                from_neighbour(srow_halo.at[i], SOURCE, NORTH + i)
        for r in group:
            out = with_columns([forced[r, :, 0:BLOCK], forced[r, :, BLOCK:cols]], r, columns)
            parts = probe_rows(r)
            for h in range(halves):
                at = slice(h * BLOCK, (h + 1) * BLOCK)
                if r == 0:
                    out[h] = out[h] - coef[1, 0:1, at] * srow_halo[0, :, at].astype(F32)
                if r == rows - 1:
                    out[h] = out[h] - coef[2, r : r + 1, at] * srow_halo[1, :, at].astype(F32)
                s_high, s_low = split(tiles[1, r : r + 1, at] * out[h] + PRIOR * parts[h])
                here = slice(r * cols + h * BLOCK, r * cols + (h + 1) * BLOCK)
                xcat[0:probe_count, here] = s_high
                xcat[probe_count : 2 * probe_count, here] = s_low
        if group[0] == 0:
            both = [xcat[:, r * cols : (r + 1) * cols] for r in group]
            for sketch in both:
                quad = quad + dot(sketch, sketch, NT)
        else:
            sketch = xcat[:, group[0] * cols : (group[-1] + 1) * cols]
            quad = dot(sketch, sketch, NT)

    keep_sketch = pltpu.make_async_copy(xcat, xcat_hbm, load_sem.at[0])
    keep_sketch.start()
    pair = quad[0:probe_count] + quad[probe_count:]
    gram = pair + shifted(pair, probe_count)
    half = probe_count // 2
    packed = jnp.where(lane < probe_count, gram[0:half], gram[half:])
    for i in range(2):
        part[i] = packed[i * piece : (i + 1) * piece]

    def total(buf, count):
        values = [buf[i] for i in range(count)]
        while len(values) > 1:
            values = [
                sum(values[i : i + 2][1:], values[i]) for i in range(0, len(values), 2)
            ]
        return values[0]

    send(part.at[1 - core], chip_buf, CHIP, sibling)
    hear_y(1)
    arrived(chip_buf, CHIP)
    here = y * nx + x
    plane_buf[here] = part[core] + chip_buf[...]
    for peer in plane_peers:
        send(plane_buf.at[here], plane_buf.at[here], PLANE, peer)
    advance(2)
    arrived(plane_buf.at[pl.ds(0, nx * ny - 1)], PLANE)
    z_buf[z] = total(plane_buf, nx * ny)
    for peer in z_peers:
        send(z_buf.at[z], z_buf.at[z], ZS, peer)
    for copy in unsent:
        copy.wait_send()
    for src, at, side in edge_copies:

        @pl.when(inner[side])
        def _():
            whole(src, at).wait_send()

    keep_sketch.wait()
    done = len(unsent)
    arrived(z_buf.at[pl.ds(0, nz - 1)], ZS)
    cells = rows * cols * n_mesh * n_obs
    both_buf[core] = total(z_buf, nz) / cells
    send(both_buf.at[core], both_buf.at[core], BOTH, sibling)
    arrived(both_buf.at[0], BOTH)
    keep_gram = pltpu.make_async_copy(both_buf, gram_hbm, load_sem.at[1])
    keep_gram.start()
    for copy in unsent[done:]:
        copy.wait_send()
    keep_gram.wait()


def eliminate(work, probe_count):
    sub = lax.broadcasted_iota(jnp.int32, (8, BLOCK), 0)
    lanes = lax.broadcasted_iota(jnp.int32, (8, BLOCK), 1)
    groups = len(work)
    factor = [jnp.zeros((8, BLOCK), F32)] * groups
    inverse = [jnp.zeros((8, BLOCK), F32)] * groups

    def wide(x):
        return jnp.broadcast_to(x, (8, BLOCK))

    for k in range(0, probe_count, PIVOTS):
        g, s = divmod(k, 8)
        span = range(PIVOTS)
        col = [[wide(work[i][:, k + j : k + j + 1]) for i in range(g, groups)] for j in span]
        row = [wide(work[g][s + j : s + j + 1, :]) for j in span]
        local = [[wide(col[j][0][s + i : s + i + 1, :]) for j in range(i + 1)] for i in span]
        lower = [[None] * PIVOTS for _ in span]
        inv, roots = [], []
        for p in range(0, PIVOTS, 2):
            a, b, c = local[p][p], local[p + 1][p], local[p + 1][p + 1]
            det = a * c - b * b
            inv_a, inv_det = 1.0 / a, 1.0 / det
            inv_1 = a * inv_det
            slope = b * inv_a
            inv += [inv_a, inv_1]
            roots += [lax.rsqrt(a), lax.rsqrt(det * inv_a)]
            lower[p + 1][p] = slope
            for i in range(p + 2, PIVOTS):
                u, v = local[i][p], local[i][p + 1]
                lower[i][p] = u * inv_a
                lower[i][p + 1] = (v - slope * u) * inv_1
                for j in range(p + 2, i + 1):
                    t, w = local[j][p], local[j][p + 1]
                    local[i][j] = (
                        local[i][j] - (u * (c * t - b * w) + v * (a * w - b * t)) * inv_det
                    )

        def reduce(v):
            done = []
            for j in span:
                value = v[j]
                for i in range(j):
                    value = value - lower[j][i] * done[i]
                done.append(value)
            return done

        reduced = reduce(row)
        scaled = [v * w for v, w in zip(reduced, inv)]
        for j in span:
            inverse[g] = jnp.where(sub == s + j, reduced[j] * roots[j], inverse[g])
        for i in range(g, groups):
            column = reduce([col[j][i - g] for j in span])
            if not (i == g and s + PIVOTS == 8):
                update = work[i]
                for j in range(0, PIVOTS, 2):
                    update = update - (column[j] * scaled[j] + column[j + 1] * scaled[j + 1])
                work[i] = jnp.where(sub >= s + PIVOTS, update, work[i]) if i == g else update
            for j in span:
                keep = column[j] * roots[j]
                if i == g:
                    keep = jnp.where(sub >= s + j, keep, 0.0)
                factor[i] = jnp.where(lanes == k + j, keep, factor[i])
    return factor, inverse


def basis_kernel(
    gram_hbm, xcat_hbm, rank_hbm, basis_hbm, factor_ref, gram_ref, xcat, rank_ref, out, sem
):
    halves, cells, _ = out.shape
    probe_count = factor_ref.shape[0]
    rows = cells // probe_count
    cols = halves * BLOCK
    piece = gram_ref.shape[1]
    groups = probe_count // 8
    load_gram = pltpu.make_async_copy(gram_hbm, gram_ref, sem.at[0])
    load_gram.start()
    load_sketch = pltpu.make_async_copy(xcat_hbm, xcat, sem.at[1])
    load_sketch.start()
    load_rank = pltpu.make_async_copy(rank_hbm, rank_ref, sem.at[2])
    load_rank.start()
    load_gram.wait()
    sub = lax.broadcasted_iota(jnp.int32, (8, BLOCK), 0)
    lanes = lax.broadcasted_iota(jnp.int32, (8, BLOCK), 1)
    work = []
    for g in range(groups):
        at = 8 * g % piece
        own = gram_ref[8 * g // piece % 2, at : at + 8, :]
        if 8 * g >= 2 * piece:
            own = shifted(own, probe_count)
        unit = jnp.where(lanes == sub + (8 * g + probe_count), 1.0, 0.0)
        work.append(jnp.where(lanes < probe_count, own, unit))
    factor, inverse = eliminate(work, probe_count)
    load_rank.wait()
    rank = rank_ref[0]
    for g in range(groups):
        factor_ref[8 * g : 8 * g + 8, :] = factor[g][:, 0:probe_count]
    lower = jnp.concatenate(
        [
            jnp.where((sub + 8 * g < rank) & (lanes >= probe_count), inverse[g], 0.0)
            for g in range(groups)
        ],
        axis=0,
    )
    lower = lower + shifted(lower, probe_count)
    l_high, l_low = split(lower)
    both = jnp.concatenate([l_high, l_low], axis=0)
    load_sketch.wait()
    stores = []
    for h in range(halves):
        for r in range(rows):
            here = slice(r * cols + h * BLOCK, r * cols + (h + 1) * BLOCK)
            solved = dot(both, xcat[:, here], NN)
            out[h, pl.ds(r, probe_count, stride=rows), :] = (
                solved[0:probe_count] + solved[probe_count:]
            )
        store = pltpu.make_async_copy(
            out.at[h], basis_hbm.at[:, pl.ds(h * BLOCK, BLOCK)], sem.at[3 + h]
        )
        store.start()
        stores.append(store)
    for store in stores:
        store.wait()


def per_device(
    n_mesh, n_obs, nz, probes, velocity, viscosity, friction, obs_block, obs_weight, obs_prec, rank
):
    probe_count, rows, cols = probes.shape
    per_dev = obs_weight.shape[1]
    ny = n_mesh // nz
    piece = probe_count // 4
    dma = pltpu.SemaphoreType.DMA
    vmem = pl.BlockSpec(memory_space=pltpu.VMEM)
    hbm = pl.BlockSpec(memory_space=pltpu.HBM)
    xcat, gram = pl.pallas_call(
        functools.partial(sketch_kernel, n_mesh, n_obs, nz),
        out_shape=(
            jax.ShapeDtypeStruct((2 * probe_count, rows * cols), BF16),
            jax.ShapeDtypeStruct((2, piece, BLOCK), F32),
        ),
        in_specs=[hbm] * 7,
        out_specs=(hbm, hbm),
        scratch_shapes=[
            pltpu.VMEM((probe_count, rows, cols), BF16),
            pltpu.VMEM((rows, cols), F32),
            pltpu.VMEM((1, per_dev), jnp.int32),
            pltpu.VMEM((1, per_dev, BLOCK), F32),
            pltpu.VMEM((1, per_dev), F32),
            pltpu.VMEM((cols // BLOCK, probe_count * rows, BLOCK), F32),
            pltpu.VMEM((rows, probe_count, cols), F32),
            pltpu.VMEM((rows, probe_count, cols), F32),
            pltpu.VMEM((7, rows, cols), F32),
            pltpu.VMEM((2, rows, cols), F32),
            pltpu.VMEM((2, 8, cols), F32),
            pltpu.VMEM((2, 8, cols), F32),
            pltpu.VMEM((2, rows, BLOCK), F32),
            pltpu.VMEM((2, probe_count, cols), BF16),
            pltpu.VMEM((2, probe_count, cols), BF16),
            pltpu.VMEM((2, 8, BLOCK), F32),
            pltpu.VMEM((2, 8, BLOCK), F32),
            pltpu.VMEM((2, probe_count, cols), BF16),
            pltpu.VMEM((2, probe_count, cols), BF16),
            pltpu.VMEM((2, 8, BLOCK), F32),
            pltpu.VMEM((2, 8, BLOCK), F32),
            pltpu.VMEM((16, BLOCK), F32),
            pltpu.VMEM((n_obs, per_dev + 16, BLOCK), jnp.int16),
            pltpu.VMEM((n_obs * per_dev, 2 * BLOCK), BF16),
            pltpu.VMEM((cols // BLOCK, rows * probe_count, 2 * BLOCK), BF16),
            pltpu.VMEM((2 * probe_count, rows * cols), BF16),
            pltpu.VMEM((2, piece, BLOCK), F32),
            pltpu.VMEM((piece, BLOCK), F32),
            pltpu.VMEM((n_obs // 2 * ny, piece, BLOCK), F32),
            pltpu.VMEM((nz, piece, BLOCK), F32),
            pltpu.VMEM((2, piece, BLOCK), F32),
            dma((7,)),
            dma((17,)),
            dma((17,)),
            pltpu.SemaphoreType.REGULAR((3, 2)),
            pltpu.SemaphoreType.REGULAR((2, 2)),
        ],
        compiler_params=pltpu.CompilerParams(collective_id=0, has_side_effects=True),
    )(probes, velocity, viscosity, friction, obs_block, obs_weight, obs_prec)
    basis, factor = pl.pallas_call(
        basis_kernel,
        out_shape=(
            jax.ShapeDtypeStruct((probe_count * rows, cols), F32),
            jax.ShapeDtypeStruct((probe_count, probe_count), F32),
        ),
        in_specs=[hbm, hbm, hbm],
        out_specs=(hbm, vmem),
        scratch_shapes=[
            pltpu.VMEM((2, piece, BLOCK), F32),
            pltpu.VMEM((2 * probe_count, rows * cols), BF16),
            pltpu.SMEM((1,), jnp.int32),
            pltpu.VMEM((cols // BLOCK, probe_count * rows, BLOCK), F32),
            dma((3 + cols // BLOCK,)),
        ],
    )(gram, xcat, rank)
    return basis.reshape(probe_count, rows, cols), factor


def solution(mesh):
    in_specs = (
        P(None, "mesh", "obs"),
        P("mesh", "obs"),
        P("mesh", "obs"),
        P("mesh", "obs"),
        P("mesh", "obs"),
        P("mesh", "obs", None),
        P("mesh", "obs"),
        P(),
    )
    n_mesh, n_obs = mesh.shape["mesh"], mesh.shape["obs"]
    nz = Z_RING if n_mesh % Z_RING == 0 else n_mesh // 2
    return jax.shard_map(
        functools.partial(per_device, n_mesh, n_obs, nz),
        mesh=mesh,
        in_specs=in_specs,
        out_specs=(P(None, "mesh", "obs"), P()),
        check_vma=False,
    )
```
